256 devices in a mesh: gx: 32 (over z, x), gy: 4 (over y), blk: 2 (over core).
Axes of the slice: x: 4, y: 4, z: 8, core: 2. Of those that a mesh axis runs over, the one named last changes fastest.
Arguments:
- pressure: float32 [512, 256, 256], P('gx', 'gy', 'blk'), may hold values from -6 to 6
- pressure_prev: float32 [512, 256, 256], P('gx', 'gy', 'blk'), may hold values from -6 to 6
- buoyancy: float32 [512, 256, 256], P('gx', 'gy', 'blk'), may hold values from 0.5 to 2
- kappa: float32 [512, 256, 256], P('gx', 'gy', 'blk'), may hold values from 0.5 to 2
- hull_accel: float32 [131072, 128], P(('gx', 'gy', 'blk')), may hold values from -6 to 6
- row_block: int32 [131072, 1], P(('gx', 'gy', 'blk')), may hold values from 0 to 127; in each aligned block of 512 rows (0 to 511, 512 to 1023, ...) at most 8 rows name the same one
- row_column: int32 [131072, 1], P(('gx', 'gy', 'blk')), may hold values from 0 to 1023
Outputs:
- pressure_next: float32 [512, 256, 256], P('gx', 'gy', 'blk')
- hull_pressure: float32 [131072, 128], P(('gx', 'gy', 'blk'))
The draws below stay inside these ranges and needn't reach their ends.
Inputs may be any that keep to these rules, and one draw needn't show every extreme that they name: `row_block`: among the 512 rows of one device at most 8 name the same block, and exactly 8 do for some block.
All inputs are finite; a program needn't handle non-finite values.
Results may differ from the reference program's by a relative error of at most 0.00002.
Values sent between devices are 32-bit elements; how exact they have to be, the bound alone decides.
A program may use at most 64 MiB of HBM per device.

```python
import math
import jax
import jax.numpy as jnp
import numpy as np
from jax import lax

CX = 16
CY = 64
CZ = 128
HROWS = 512
NX = 512
NY = 256
NZ = 256
CAP = 8
HULL = 131072
N_GX = 32
N_GY = 4
N_BLK = 2


def set_ends(entries, key, least, largest):
    spot = [jax.random.randint(jax.random.fold_in(key, axis), (), 0, length) for axis, length in enumerate(entries.shape)]
    longest = entries.shape.index(max(entries.shape))
    neighbour = spot[:longest] + [(spot[longest] + 1) % entries.shape[longest]] + spot[longest + 1:]
    return entries.at[tuple(spot)].set(least).at[tuple(neighbour)].set(largest)


def levels(key, dims, shards, least, largest):
    level, own = 1.0, jax.random.fold_in(key, 6)
    for axis_at, blocks in shards:
        heights = jnp.exp(jax.random.uniform(jax.random.fold_in(own, axis_at), (blocks,), jnp.float32, least / len(shards), largest / len(shards)))
        level = level * jnp.repeat(heights, dims[axis_at] // blocks).reshape([-1 if axis == axis_at else 1 for axis in range(len(dims))])
    return level


def assign_block(stream_key, own, number, rows, count, top, reach, slope):
    sequence = jax.random.permutation(stream_key, count)
    packed, common = portions_of(count, rows * top, reach, slope, True), portions_of(count, rows * top, reach, slope, False)
    places = jnp.arange(count)

    def named(lengths, rotation):
        used = int((lengths > 0).sum())
        fixed = max(1, used // 4)
        moved = fixed + (places - fixed + rotation * (used - fixed)) % max(1, count - fixed)
        return jnp.zeros((count,), jnp.int32).at[sequence[jnp.where(places < fixed, places, moved)]].set(jnp.asarray(lengths, jnp.int32))

    lengths = jnp.where(number % 4 == 0, named(packed, number // 4), named(common, number - number // 4 - 1))
    mixed = jax.random.permutation(jax.random.fold_in(own, 3), count)
    giver, receiver = mixed[0:count // 2 * 2:2], mixed[1:count // 2 * 2:2]
    room = jnp.minimum(lengths[giver] - 1, reach - lengths[receiver]) // 2
    room = jnp.where((giver == sequence[0]) | (receiver == sequence[0]) | (lengths[receiver] == 0), 0, jnp.maximum(room, 0))
    moved = jax.random.randint(jax.random.fold_in(own, 4), (count // 2,), 0, 1 << 20) % (room + 1)
    lengths = lengths.at[giver].add(-moved).at[receiver].add(moved)
    items = jnp.searchsorted(jnp.cumsum(lengths), jnp.arange(rows * top), side="right").astype(jnp.int32)
    listing = items.reshape(top, rows).T
    listing = listing[jax.random.permutation(jax.random.fold_in(own, 1), rows)]
    rotation = jax.random.randint(jax.random.fold_in(own, 2), (rows, 1), 0, top)
    return jnp.take_along_axis(listing, (jnp.arange(top)[None, :] + rotation) % top, axis=1)


def portions_of(count, total, most, skew, full):
    portions = [(1 << 20) // math.isqrt(grade ** skew) + 1 for grade in range(1, count + 1)]
    largest = most if full else min(most, max(-(-total // count), total * portions[0] // sum(portions)))
    least = 1 if total - largest >= count - 1 else 0
    holding, spare = [largest] + [least] * (count - 1), total - largest - least * (count - 1)
    while spare > 0:
        movable = [i for i in range(1, count) if holding[i] < largest] or [i for i in range(1, count) if holding[i] < most]
        mass, remaining = sum([portions[i] for i in movable]), spare
        for i in movable:
            more = min(most - holding[i], max(1, remaining * portions[i] // mass), spare)
            holding[i] = holding[i] + more
            spare = spare - more
    return np.array(holding)


def scatter_about(own_key, extent, scale, reach, shards=(), held_as=jnp.bfloat16):
    loudness = levels(own_key, extent, shards, -0.22, 0.18) if shards else 1.0
    entries = jax.random.normal(own_key, extent, jnp.float32) * scale * loudness
    return jnp.minimum(jnp.maximum(entries, -reach), reach).astype(held_as)


def setup_inputs(seed: int = 0) -> dict:
    key_of = jax.random.split(jax.random.key(seed), 8)
    pressure = scatter_about(key_of[0], (NX, NY, NZ), 1.0, 6.0, ((0, 32), (1, 4), (2, 2)), jnp.float32)
    pressure_prev = scatter_about(key_of[1], (NX, NY, NZ), 1.0, 6.0, ((0, 32), (1, 4), (2, 2)), jnp.float32)
    buoyancy = jnp.clip(jnp.exp(math.log(2.0) - 1.3862944 * jax.random.uniform(key_of[2], (NX, NY, NZ), jnp.float32) ** levels(key_of[2], (NX, NY, NZ), ((0, 32), (1, 4), (2, 2)), -0.2, 0.2)), 0.5, 2.0)
    kappa = jnp.clip(jnp.exp(math.log(2.0) - 1.3862944 * jax.random.uniform(key_of[3], (NX, NY, NZ), jnp.float32) ** levels(key_of[3], (NX, NY, NZ), ((0, 32), (1, 4), (2, 2)), -0.2, 0.2)), 0.5, 2.0)
    hull_accel = scatter_about(key_of[4], (HULL, CZ), 1.0, 6.0, ((0, 256),), jnp.float32)
    row_block_keys = jax.random.split(jax.random.fold_in(key_of[5], 1), HULL // HROWS)
    row_block_turns = jax.random.permutation(jax.random.fold_in(key_of[5], 3), HULL // HROWS)
    row_block = jax.vmap(lambda own, number: assign_block(jax.random.fold_in(key_of[5], 2), own, number, HROWS, N_GX * N_GY, 1, CAP, 2))(row_block_keys, row_block_turns).reshape((HULL, 1))
    row_column = set_ends(jax.random.randint(key_of[6], (HULL, 1), 0, CX * CY), jax.random.fold_in(key_of[6], 1), 0, (CX * CY) - 1).astype(jnp.int32)
    return dict(pressure=pressure, pressure_prev=pressure_prev, buoyancy=buoyancy, kappa=kappa, hull_accel=hull_accel, row_block=row_block, row_column=row_column)


courant_sq = 0.05
source_gain = 0.5


def trim_edge(field, width, skip_dim):
    for other_dim in range(3):
        if other_dim != skip_dim:
            field = lax.slice_in_dim(field, width, field.shape[other_dim] - width, axis=other_dim)
    return field


def fourth_diff(field, along_dim, length_out):
    def shifted(offset):
        return lax.slice_in_dim(field, offset, offset + length_out, axis=along_dim)
    return (27.0 * (shifted(2) - shifted(1)) - (shifted(3) - shifted(0))) / 24.0


def operator(padded, buoy_pad):
    summed = None
    for along_dim in range(3):
        press_line = trim_edge(padded, 3, along_dim)
        buoy_line = trim_edge(buoy_pad, 2, along_dim)
        length_out = padded.shape[along_dim] - 6
        gradient = fourth_diff(press_line, along_dim, length_out + 3)
        face_buoy = (lax.slice_in_dim(buoy_line, 0, length_out + 3, axis=along_dim)
                     + lax.slice_in_dim(buoy_line, 1, length_out + 4, axis=along_dim)) * 0.5
        axis_term = fourth_diff(gradient * face_buoy, along_dim, length_out)
        summed = axis_term if summed is None else summed + axis_term
    return summed


def reference(pressure, pressure_prev, buoyancy, kappa, hull_accel, row_block, row_column):
    hull_rows = hull_accel.shape[0]
    device_ids = jnp.arange(hull_rows, dtype=jnp.int32) // HROWS
    depth = (device_ids % N_BLK).astype(jnp.int32)
    block_ids = row_block[:, 0].astype(jnp.int32)
    column = row_column[:, 0].astype(jnp.int32)
    x_cells = (block_ids // N_GY) * CX + column // CY
    y_cells = (block_ids % N_GY) * CY + column % CY
    source = jnp.zeros((NX, NY, N_BLK, CZ), jnp.float32).at[x_cells, y_cells, depth].add(hull_accel)
    source = source.reshape(NX, NY, NZ)
    buoy_pad = jnp.pad(buoyancy, 2)
    lap_one = operator(jnp.pad(pressure, 3), buoy_pad)
    pressure_mid = 2.0 * pressure - pressure_prev + kappa * (courant_sq * lap_one + source_gain * source)
    lap_two = operator(jnp.pad(pressure_mid, 3), buoy_pad)
    pressure_next = 2.0 * pressure_mid - pressure + kappa * (courant_sq * lap_two + source_gain * source)
    picked = pressure_next.reshape(NX, NY, N_BLK, CZ)[x_cells, y_cells, depth]
    return pressure_next, picked
```

```python
import functools

import jax
import jax.numpy as jnp
from jax import lax
from jax.experimental import pallas as pl
from jax.experimental.pallas import tpu as pltpu
from jax.sharding import PartitionSpec as P

MESH = pl.DeviceIdType.MESH
F32 = jnp.float32
BF16 = jnp.bfloat16
LANES = 128
CAP = 8
MSG = 9
COURANT = 0.05
GAIN = 0.5
FACE = COURANT * 0.5 / 576.0


def torus(n_gx, n_gy):
    nx = 4 if n_gx % 4 == 0 and n_gx > 4 else 2
    return n_gx // nx, nx, n_gy


def split2(v):
    hi = v.astype(BF16)
    lo = (v - hi.astype(F32)).astype(BF16)
    return hi, lo


def parts(v):
    hi, lo = split2(v)
    return jnp.concatenate([hi, lo], axis=1)


def joined(v):
    return v[:, :LANES] + v[:, LANES:]


def wide(a, b, c, d):
    return 27.0 * (c - b) - (d - a)


def dot(a, b):
    return jnp.dot(a, b, preferred_element_type=F32)


def dot_nt(a, b):
    return lax.dot_general(a, b, (((1,), (1,)), ((), ())), preferred_element_type=F32)


def dot_tn(a, b):
    return lax.dot_general(a, b, (((0,), (0,)), ((), ())), preferred_element_type=F32)


def onehot(mask):
    return jnp.where(mask, 1.0, 0.0).astype(BF16)


def kernel(
    dims,
    p_hbm, prev_hbm, b_hbm, kap_hbm, hull_hbm, rb_ref, rc_ref,
    out_hbm, hp_hbm,
    E, EB, E2, OP, OB, OM, PREV, KAP, HULL, FX, FY, BX, BY, BZ, BZO, SRC, NEXT,
    SB, RV, PK, RET, Q, PM, HOUT,
    in_sem, out_sem, hs_sem, hr_sem, ms_sem, mr_sem, as_sem, ar_sem, bs_sem, br_sem, self_sem,
):
    nz, nx, ny = dims
    NB = nz * nx * ny
    G = nx * ny
    GS = G * CAP
    X, Y = PREV.shape[0], PREV.shape[1]
    HR = HULL.shape[0]
    n_gx = nz * nx
    gx = lax.axis_index("gx")
    gy = lax.axis_index("gy")
    blk = lax.axis_index("blk")
    zi = gx // nx
    xi = gx % nx
    me = gx * ny + gy

    zs = [(zi + dz) % nz for dz in range(nz)]
    xs = [(xi + dx) % nx for dx in range(nx)]
    ys = [(gy + dy) % ny for dy in range(ny)]
    zb = [(zi + nz - dz) % nz for dz in range(nz)]
    xb = [(xi + nx - dx) % nx for dx in range(nx)]
    yb = [(gy + ny - dy) % ny for dy in range(ny)]
    half = nz // 2
    order = [half]
    for step in range(half - 1, 0, -1):
        order += [step, nz - step]
    order += [0]
    offsets = {dz: [(dx, dy) for dx in range(nx) for dy in range(ny)] for dz in range(nz)}

    barrier = pltpu.get_barrier_semaphore()
    for dz in order:
        for dx, dy in offsets[dz]:
            if (dz, dx, dy) != (0, 0, 0):
                pl.semaphore_signal(
                    barrier, inc=1, device_id=(zs[dz] * nx + xs[dx], ys[dy], blk), device_id_type=MESH
                )
    pl.semaphore_signal(barrier, inc=1, device_id=(gx, gy, 1 - blk), device_id_type=MESH)

    loads = [
        pltpu.make_async_copy(hull_hbm, HULL, in_sem.at[0]),
        pltpu.make_async_copy(p_hbm, E.at[pl.ds(3, X), pl.ds(8, Y)], in_sem.at[1]),
        pltpu.make_async_copy(b_hbm, EB.at[pl.ds(2, X), pl.ds(8, Y)], in_sem.at[2]),
        pltpu.make_async_copy(prev_hbm, PREV, in_sem.at[3]),
        pltpu.make_async_copy(kap_hbm, KAP, in_sem.at[4]),
    ]
    for load in loads:
        load.start()

    for ref, w in ((E, 3), (EB, 2), (E2, 3)):
        @pl.when(gx == 0)
        def _(ref=ref, w=w):
            ref[0:w] = jnp.zeros((w,) + ref.shape[1:], F32)

        @pl.when(gx == n_gx - 1)
        def _(ref=ref, w=w):
            ref[w + X :] = jnp.zeros((w,) + ref.shape[1:], F32)

        @pl.when(gy == 0)
        def _(ref=ref, w=w):
            ref[w : w + X, 0:8] = jnp.zeros((X, 8, LANES), F32)

        @pl.when(gy == ny - 1)
        def _(ref=ref, w=w):
            ref[w : w + X, 8 + Y :] = jnp.zeros((X, 8, LANES), F32)

    rb = rb_ref[...]
    owner = onehot(jnp.broadcast_to(rb, (NB, HR)) == lax.broadcasted_iota(jnp.int32, (NB, HR), 0))
    before = onehot(
        lax.broadcasted_iota(jnp.int32, (HR, HR), 0) < lax.broadcasted_iota(jnp.int32, (HR, HR), 1)
    )
    earlier = dot(owner, before)
    slot = jnp.sum(owner.astype(F32) * earlier, axis=0, keepdims=True).astype(jnp.int32)
    placing = rb * CAP + slot
    code = rc_ref[...] + 1
    lane_row = lax.broadcasted_iota(jnp.int32, (LANES, HR), 0)
    slot_b = jnp.broadcast_to(slot, (LANES, HR))
    picked_hi = jnp.where(lane_row == slot_b, jnp.broadcast_to(code // 32, (LANES, HR)), 0)
    picked_lo = jnp.where(lane_row == slot_b + CAP, jnp.broadcast_to(code % 32, (LANES, HR)), 0)
    codes = (picked_hi + picked_lo).astype(F32).astype(BF16)
    cols = dot_nt(owner, codes)
    SB[:, 8:16, :] = jnp.broadcast_to(cols.reshape(NB, 1, LANES), (NB, 8, LANES))

    loads[0].wait()
    hull_parts = parts(HULL[...])

    def pack(m, _):
        rows = lax.broadcasted_iota(jnp.int32, (GS, HR), 0) + m * GS
        pt = onehot(rows == jnp.broadcast_to(placing, (GS, HR)))
        SB[pl.ds(m * G, G), 0:8, :] = joined(dot(pt, hull_parts)).reshape(G, 8, LANES)
        return 0

    lax.fori_loop(0, nz, pack, 0)

    pl.semaphore_wait(barrier, NB)

    def shares(src, dst, width, lo, hi, send, recv):
        return [
            (gx < n_gx - 1, gx > 0, pltpu.make_async_remote_copy(
                src.at[pl.ds(X + lo - width, width), pl.ds(8, Y)], dst.at[pl.ds(lo - width, width), pl.ds(8, Y)],
                send.at[0], recv.at[0], device_id=(jnp.minimum(gx + 1, n_gx - 1), gy, blk), device_id_type=MESH)),
            (gx > 0, gx < n_gx - 1, pltpu.make_async_remote_copy(
                src.at[pl.ds(lo, width), pl.ds(8, Y)], dst.at[pl.ds(X + lo, width), pl.ds(8, Y)],
                send.at[1], recv.at[1], device_id=(jnp.maximum(gx - 1, 0), gy, blk), device_id_type=MESH)),
            (gy < ny - 1, gy > 0, pltpu.make_async_remote_copy(
                src.at[pl.ds(lo, X), pl.ds(Y, 8)], dst.at[pl.ds(lo, X), pl.ds(0, 8)],
                send.at[2], recv.at[2], device_id=(gx, jnp.minimum(gy + 1, ny - 1), blk), device_id_type=MESH)),
            (gy > 0, gy < ny - 1, pltpu.make_async_remote_copy(
                src.at[pl.ds(lo, X), pl.ds(8, 8)], dst.at[pl.ds(lo, X), pl.ds(8 + Y, 8)],
                send.at[3], recv.at[3], device_id=(gx, jnp.maximum(gy - 1, 0), blk), device_id_type=MESH)),
            (None, None, pltpu.make_async_remote_copy(
                src.at[pl.ds(lo, X), pl.ds(8, Y)], hi,
                send.at[4], recv.at[4], device_id=(gx, gy, 1 - blk), device_id_type=MESH)),
        ]

    def start(copies):
        for sends, _, copy in copies:
            if sends is None:
                copy.start()
            else:
                pl.when(sends)(lambda copy=copy: copy.start())

    def finish(copies):
        for sends, gets, copy in copies:
            if sends is None:
                copy.wait_send()
                copy.wait_recv()
            else:
                pl.when(sends)(lambda copy=copy: copy.wait_send())
                pl.when(gets)(lambda copy=copy: copy.wait_recv())

    loads[1].wait()
    loads[2].wait()
    halo_p = shares(E, E, 3, 3, OP, hs_sem.at[0], hr_sem.at[0])
    halo_b = shares(EB, EB, 2, 2, OB, hs_sem.at[1], hr_sem.at[1])
    start(halo_p)
    start(halo_b)

    for dz in order:
        for dx, dy in offsets[dz]:
            k = (dz * nx + dx) * ny + dy
            if k == 0:
                continue
            dest_gx = zs[dz] * nx + xs[dx]
            pltpu.make_async_remote_copy(
                SB.at[dest_gx * ny + ys[dy], pl.ds(0, MSG)], RV.at[k, pl.ds(0, MSG)],
                as_sem, ar_sem.at[dz], device_id=(dest_gx, ys[dy], blk), device_id_type=MESH,
            ).start()
    own = pltpu.make_async_copy(SB.at[me, pl.ds(0, MSG)], RV.at[0, pl.ds(0, MSG)], self_sem.at[0])
    own.start()

    weights_row = lax.broadcasted_iota(jnp.int32, (16, LANES), 0)
    place_row = lax.broadcasted_iota(jnp.int32, (16, HR), 0)
    place_code = jnp.where(
        place_row == 0, jnp.broadcast_to(placing // 32, (16, HR)),
        jnp.where(place_row == 1, jnp.broadcast_to(placing % 32, (16, HR)), 0),
    ).astype(F32).astype(BF16)
    place_w = jnp.where(weights_row == 0, 32.0, jnp.where(weights_row == 1, 1.0, 0.0)).astype(BF16)
    placing_col = dot_tn(place_code, place_w)
    span = min(LANES, NB * CAP)
    for m in range(NB * CAP // span):
        cell = (lax.broadcasted_iota(jnp.int32, (HR, span), 1) + m * span).astype(F32)
        PM[:, m * span : (m + 1) * span] = onehot(placing_col[:, :span] == cell)

    lane = lax.broadcasted_iota(jnp.int32, (Y, LANES), 1)
    mine_left = jnp.broadcast_to(blk, (Y, LANES)) == 0
    halo_lanes = (lane < LANES // 2) == mine_left

    def outer(other):
        return jnp.where(halo_lanes, other, 0.0)

    def up(k, near, far):
        return pltpu.roll(jnp.where(lane < k, far, near), LANES - k, 1)

    def down(k, near, far):
        return pltpu.roll(jnp.where(lane >= LANES - k, far, near), k, 1)

    finish(halo_b)

    def faces_x(i, _):
        BX[i] = (EB[i, 8 : 8 + Y] + EB[i + 1, 8 : 8 + Y]) * FACE
        return 0

    lax.fori_loop(0, X + 3, faces_x, 0)

    def faces_yz(i, _):
        BY[i] = (EB[i + 2, 6 : 14 + Y] + EB[i + 2, 7 : 15 + Y]) * FACE
        own_b = EB[i + 2, 8 : 8 + Y]
        far_b = outer(OB[i])
        BZ[i] = (own_b + up(1, own_b, far_b)) * FACE
        BZO[i] = (far_b + up(1, far_b, own_b)) * FACE
        return 0

    lax.fori_loop(0, X, faces_yz, 0)

    def flux_x(src):
        def body(i, _):
            FX[i] = wide(src[i, 8 : 8 + Y], src[i + 1, 8 : 8 + Y], src[i + 2, 8 : 8 + Y], src[i + 3, 8 : 8 + Y]) * BX[i]
            return 0

        lax.fori_loop(0, X + 3, body, 0)

    def laplace(src, other, i):
        total = wide(FX[i], FX[i + 1], FX[i + 2], FX[i + 3])
        FY[...] = wide(src[i + 3, 5 : 13 + Y], src[i + 3, 6 : 14 + Y], src[i + 3, 7 : 15 + Y], src[i + 3, 8 : 16 + Y]) * BY[i]
        total = total + wide(FY[0:Y], FY[1 : 1 + Y], FY[2 : 2 + Y], FY[3 : 3 + Y])
        near = src[i + 3, 8 : 8 + Y]
        far = outer(other[i])
        flux = wide(down(1, near, far), near, up(1, near, far), up(2, near, far)) * BZ[i]
        beyond = wide(down(1, far, near), far, up(1, far, near), up(2, far, near)) * BZO[i]
        return total + wide(down(2, flux, beyond), down(1, flux, beyond), flux, up(1, flux, beyond))

    loads[3].wait()
    loads[4].wait()
    finish(halo_p)
    flux_x(E)

    def first(i, _):
        E2[i + 3, 8 : 8 + Y] = 2.0 * E[i + 3, 8 : 8 + Y] - PREV[i] + KAP[i] * laplace(E, OP, i)
        return 0

    lax.fori_loop(0, X, first, 0)

    def wait_group(buf, rows, count, sem):
        ref = buf.at[pl.ds(0, count), pl.ds(0, rows)]
        pltpu.make_async_copy(ref, ref, sem).wait()

    tag = lax.broadcasted_iota(jnp.int32, (8, LANES), 1)
    row8 = lax.broadcasted_iota(jnp.int32, (8, LANES), 0)
    keep = (tag == row8) | (tag == row8 + CAP)
    w_lane = lax.broadcasted_iota(jnp.int32, (8, LANES), 1)
    w_code = jnp.where(w_lane < CAP, 32.0, jnp.where(w_lane < 2 * CAP, 1.0, 0.0)).astype(BF16)
    cells = X * Y

    def masked(dz):
        rows = [
            jnp.where(keep, jnp.broadcast_to(RV[dz * G + j, 8:9, :], (8, LANES)), 0.0) for j in range(G)
        ]
        return jnp.concatenate(rows, axis=0).astype(BF16)

    chunk = min(256, cells)
    for n, dz in enumerate(order):
        if dz == 0:
            if G > 1:
                wait_group(RV, MSG, G - 1, ar_sem.at[0])
            own.wait()
        else:
            wait_group(RV, MSG, G, ar_sem.at[dz])
        col_lane = dot_nt(w_code, masked(dz)).astype(jnp.int32) - 1
        rows = parts(RV[dz * G : (dz + 1) * G, 0:8, :].reshape(GS, LANES))
        col_b = jnp.broadcast_to(col_lane[0:1], (chunk, GS))

        def add(m, _, first_group=(n == 0), rows=rows, col_b=col_b):
            ids = lax.broadcasted_iota(jnp.int32, (chunk, GS), 0) + m * chunk
            val = joined(dot(onehot(ids == col_b), rows))
            at = pl.ds(m * chunk, chunk)
            SRC[at] = val if first_group else SRC[at] + val
            return 0

        lax.fori_loop(0, cells // chunk, add, 0)

    def middle(i, _):
        pushed = (GAIN * KAP[i]) * SRC[pl.ds(i * Y, Y)]
        E2[i + 3, 8 : 8 + Y] = E2[i + 3, 8 : 8 + Y] + pushed
        PREV[i] = pushed - E[i + 3, 8 : 8 + Y]
        return 0

    lax.fori_loop(0, X, middle, 0)
    halo_m = shares(E2, E2, 3, 3, OM, ms_sem, mr_sem)
    start(halo_m)

    w_full = jnp.where(
        lax.broadcasted_iota(jnp.int32, (LANES, LANES), 0) < CAP, 32.0,
        jnp.where(lax.broadcasted_iota(jnp.int32, (LANES, LANES), 0) < 2 * CAP, 1.0, 0.0),
    ).astype(BF16)
    for dz in order:
        col_sub = dot(masked(dz), w_full) - 1.0

        for m in range(cells // LANES):
            ids = (lax.broadcasted_iota(jnp.int32, (GS, LANES), 1) + m * LANES).astype(F32)
            Q[dz * GS : (dz + 1) * GS, m * LANES : (m + 1) * LANES] = onehot(col_sub == ids)

    finish(halo_m)
    flux_x(E2)

    def second(i, _):
        val = 2.0 * E2[i + 3, 8 : 8 + Y] + PREV[i] + KAP[i] * laplace(E2, OM, i)
        OP[i] = val
        hi, lo = split2(val)
        NEXT[pl.ds(i * Y, Y), 0:LANES] = hi
        NEXT[pl.ds(i * Y, Y), LANES : 2 * LANES] = lo
        return 0

    lax.fori_loop(0, X, second, 0)
    out_copy = pltpu.make_async_copy(OP, out_hbm, out_sem.at[0])
    out_copy.start()

    for dz in order:
        PK[dz * G : (dz + 1) * G] = joined(dot(Q[dz * GS : (dz + 1) * GS], NEXT[...])).reshape(G, 8, LANES)
        for dx, dy in offsets[dz]:
            k = (dz * nx + dx) * ny + dy
            if k == 0:
                continue
            pltpu.make_async_remote_copy(
                PK.at[k], RET.at[me], bs_sem, br_sem,
                device_id=(zb[dz] * nx + xb[dx], yb[dy], blk), device_id_type=MESH,
            ).start()
    back = pltpu.make_async_copy(PK.at[0], RET.at[me], self_sem.at[1])
    back.start()

    sent = SB.at[pl.ds(0, NB - 1), pl.ds(0, MSG)]
    pltpu.make_async_copy(sent, sent, as_sem).wait()
    for sem in (bs_sem, br_sem):
        moved = PK.at[pl.ds(0, NB - 1)]
        pltpu.make_async_copy(moved, moved, sem).wait()
    back.wait()
    HOUT[...] = joined(dot(PM[...], parts(RET[...].reshape(NB * CAP, LANES))))
    hull_copy = pltpu.make_async_copy(HOUT, hp_hbm, out_sem.at[1])
    hull_copy.start()
    hull_copy.wait()
    out_copy.wait()


def solution(mesh):
    n_gx, n_gy = mesh.shape["gx"], mesh.shape["gy"]
    dims = torus(n_gx, n_gy)
    NB = n_gx * n_gy

    def local(pressure, pressure_prev, buoyancy, kappa, hull_accel, row_block, row_column):
        X, Y, Z = pressure.shape
        HR = hull_accel.shape[0]
        any_spec = pl.BlockSpec(memory_space=pl.ANY)
        vmem_spec = pl.BlockSpec(memory_space=pltpu.VMEM)
        dma = pltpu.SemaphoreType.DMA
        V = pltpu.VMEM
        return pl.pallas_call(
            functools.partial(kernel, dims),
            out_shape=(
                jax.ShapeDtypeStruct((X, Y, Z), F32),
                jax.ShapeDtypeStruct((HR, Z), F32),
            ),
            in_specs=[any_spec] * 5 + [vmem_spec] * 2,
            out_specs=[any_spec] * 2,
            scratch_shapes=[
                V((X + 6, Y + 16, Z), F32),
                V((X + 4, Y + 16, Z), F32),
                V((X + 6, Y + 16, Z), F32),
                V((X, Y, Z), F32),
                V((X, Y, Z), F32),
                V((X, Y, Z), F32),
                V((X, Y, Z), F32),
                V((X, Y, Z), F32),
                V((HR, Z), F32),
                V((X + 3, Y, Z), F32),
                V((Y + 8, Z), F32),
                V((X + 3, Y, Z), F32),
                V((X, Y + 8, Z), F32),
                V((X, Y, Z), F32),
                V((X, Y, Z), F32),
                V((X * Y, Z), F32),
                V((X * Y, 2 * Z), BF16),
                V((NB, 16, Z), F32),
                V((NB, 16, Z), F32),
                V((NB, CAP, Z), F32),
                V((NB, CAP, Z), F32),
                V((NB * CAP, X * Y), BF16),
                V((HR, NB * CAP), BF16),
                V((HR, Z), F32),
                dma((5,)), dma((2,)), dma((2, 5)), dma((2, 5)), dma((5,)), dma((5,)),
                dma, dma((dims[0],)), dma, dma, dma((2,)),
            ],
            compiler_params=pltpu.CompilerParams(collective_id=0, has_side_effects=True, vmem_limit_bytes=60 * 1024 * 1024),
            name="hull_leapfrog",
        )(
            pressure, pressure_prev, buoyancy, kappa, hull_accel,
            row_block.reshape(1, HR), row_column.reshape(1, HR),
        )

    return jax.shard_map(
        local,
        mesh=mesh,
        in_specs=(
            P("gx", "gy", "blk"),
            P("gx", "gy", "blk"),
            P("gx", "gy", "blk"),
            P("gx", "gy", "blk"),
            P(("gx", "gy", "blk"), None),
            P(("gx", "gy", "blk"), None),
            P(("gx", "gy", "blk"), None),
        ),
        out_specs=(P("gx", "gy", "blk"), P(("gx", "gy", "blk"), None)),
        check_vma=False,
    )
```

```python
import functools

import jax
import jax.numpy as jnp
from jax import lax
from jax.experimental import pallas as pl
from jax.experimental.pallas import tpu as pltpu
from jax.sharding import PartitionSpec as P

MESH = pl.DeviceIdType.MESH
F32 = jnp.float32
BF16 = jnp.bfloat16
LANES = 128
CAP = 8
COURANT = 0.05
GAIN = 0.5
FACE = COURANT * 0.5 / 576.0


def torus(n_gx, n_gy):
    nx = 4 if n_gx % 4 == 0 and n_gx > 4 else 2
    return n_gx // nx, nx, n_gy


def split2(v):
    hi = v.astype(BF16)
    lo = (v - hi.astype(F32)).astype(BF16)
    return hi, lo


def parts(v):
    hi, lo = split2(v)
    return jnp.concatenate([hi, lo], axis=1)


def joined(v):
    return v[:, :LANES] + v[:, LANES:]


def wide(a, b, c, d):
    return 27.0 * (c - b) - (d - a)


def dot(a, b):
    return jnp.dot(a, b, preferred_element_type=F32)


def dot_nt(a, b):
    return lax.dot_general(a, b, (((1,), (1,)), ((), ())), preferred_element_type=F32)


def dot_tn(a, b):
    return lax.dot_general(a, b, (((0,), (0,)), ((), ())), preferred_element_type=F32)


def onehot(mask):
    return jnp.where(mask, 1.0, 0.0).astype(BF16)


def kernel(
    dims,
    p_hbm, prev_hbm, b_hbm, kap_hbm, hull_hbm, rb_ref, rc_ref,
    out_hbm, hp_hbm,
    E, EB, E2, ZS, ZR, PREV, KAP, HULL, FX, FY, TOT, BX, BY, BZ, BZO, NEXT,
    CS, CR, CA, MC, SB, RV, PK, RET, Q, QT, PM, HOUT,
    in_sem, out_sem, hs_sem, hr_sem, cs_sem, cr_sem, fs_sem, fr_sem, as_sem, ar_sem, bs_sem, br_sem, self_sem,
):
    nz, nx, ny = dims
    NB = nz * nx * ny
    G = nx * ny
    GS = G * CAP
    X, Y = PREV.shape[0], PREV.shape[1]
    T = Y // 8
    PER = LANES // (4 * T)
    HR = HULL.shape[0]
    cells = X * Y
    n_gx = nz * nx
    gx = lax.axis_index("gx")
    gy = lax.axis_index("gy")
    blk = lax.axis_index("blk")
    zi = gx // nx
    xi = gx % nx
    me = gx * ny + gy
    spot = xi * ny + gy

    zs = [(zi + dz) % nz for dz in range(nz)]
    xs = [(xi + dx) % nx for dx in range(nx)]
    ys = [(gy + dy) % ny for dy in range(ny)]
    zb = [(zi + nz - dz) % nz for dz in range(nz)]
    xb = [(xi + nx - dx) % nx for dx in range(nx)]
    yb = [(gy + ny - dy) % ny for dy in range(ny)]
    half = nz // 2
    order = [half]
    for step in range(half - 1, 0, -1):
        order += [step, nz - step]
    order += [0]
    plane = [(dx, dy) for dx in range(nx) for dy in range(ny)]

    barrier = pltpu.get_barrier_semaphore()
    for dz in order:
        for dx, dy in plane:
            if (dz, dx, dy) != (0, 0, 0):
                pl.semaphore_signal(
                    barrier, inc=1, device_id=(zs[dz] * nx + xs[dx], ys[dy], blk), device_id_type=MESH
                )
    pl.semaphore_signal(barrier, inc=1, device_id=(gx, gy, 1 - blk), device_id_type=MESH)

    loads = [
        pltpu.make_async_copy(hull_hbm, HULL, in_sem.at[0]),
        pltpu.make_async_copy(p_hbm, E.at[pl.ds(3, X), pl.ds(8, Y)], in_sem.at[1]),
        pltpu.make_async_copy(b_hbm, EB.at[pl.ds(2, X), pl.ds(8, Y)], in_sem.at[2]),
        pltpu.make_async_copy(prev_hbm, PREV, in_sem.at[3]),
        pltpu.make_async_copy(kap_hbm, KAP, in_sem.at[4]),
    ]
    for load in loads:
        load.start()

    for ref, w in ((E, 3), (EB, 2), (E2, 3)):
        @pl.when(gx == 0)
        def _(ref=ref, w=w):
            ref[0:w] = jnp.zeros((w,) + ref.shape[1:], F32)

        @pl.when(gx == n_gx - 1)
        def _(ref=ref, w=w):
            ref[w + X :] = jnp.zeros((w,) + ref.shape[1:], F32)

        @pl.when(gy == 0)
        def _(ref=ref, w=w):
            ref[w : w + X, 0:8] = jnp.zeros((X, 8, LANES), F32)

        @pl.when(gy == ny - 1)
        def _(ref=ref, w=w):
            ref[w : w + X, 8 + Y :] = jnp.zeros((X, 8, LANES), F32)

    rb = rb_ref[...]
    owner = onehot(jnp.broadcast_to(rb, (NB, HR)) == lax.broadcasted_iota(jnp.int32, (NB, HR), 0))
    before = onehot(
        lax.broadcasted_iota(jnp.int32, (HR, HR), 0) < lax.broadcasted_iota(jnp.int32, (HR, HR), 1)
    )
    earlier = dot(owner, before)
    slot = jnp.sum(owner.astype(F32) * earlier, axis=0, keepdims=True).astype(jnp.int32)
    placing = rb * CAP + slot
    code = rc_ref[...] + 1
    row_z = lax.broadcasted_iota(jnp.int32, (16, HR), 0)
    which_z = jnp.broadcast_to(placing // GS, (16, HR))
    coded = jnp.where(row_z == which_z, jnp.broadcast_to(code // 32, (16, HR)), 0) + jnp.where(
        row_z == which_z + 8, jnp.broadcast_to(code % 32, (16, HR)), 0
    )
    lane_of = onehot(lax.broadcasted_iota(jnp.int32, (LANES, HR), 0) == jnp.broadcast_to(placing % GS, (LANES, HR)))
    sums = dot_nt(coded.astype(F32).astype(BF16), lane_of)
    CS[...] = sums[0:8] * 32.0 + sums[8:16]

    loads[0].wait()
    hull_parts = parts(HULL[...])

    def pack(m, _):
        rows = lax.broadcasted_iota(jnp.int32, (GS, HR), 0) + m * GS
        pt = onehot(rows == jnp.broadcast_to(placing, (GS, HR)))
        SB[pl.ds(m * G, G)] = joined(dot(pt, hull_parts)).reshape(G, 8, LANES)
        return 0

    lax.fori_loop(0, nz, pack, 0)

    lane8 = lax.broadcasted_iota(jnp.int32, (8, LANES), 1)
    edge = jnp.where(jnp.broadcast_to(blk, (8, LANES)) == 0, (lane8 + 3) % LANES, lane8) // 4

    def gather_edge(field, ref, lo):
        for q in range(X // PER):
            acc = jnp.zeros((8, LANES), F32)
            for i in range(PER):
                for t in range(T):
                    m = i * T + t
                    tile = ref[lo + q * PER + i, 8 + 8 * t : 16 + 8 * t]
                    acc = jnp.where(edge == m, pltpu.roll(tile, 4 * m, 1) if m else tile, acc)
            ZS[field, q] = acc

    loads[1].wait()
    loads[2].wait()
    gather_edge(0, E, 3)
    gather_edge(1, EB, 2)

    pl.semaphore_wait(barrier, NB)

    def shares(ref, field, width):
        lo = width
        send, recv = hs_sem.at[field], hr_sem.at[field]
        return [
            (gx < n_gx - 1, gx > 0, pltpu.make_async_remote_copy(
                ref.at[pl.ds(X + lo - width, width), pl.ds(8, Y)], ref.at[pl.ds(lo - width, width), pl.ds(8, Y)],
                send.at[0], recv.at[0], device_id=(jnp.minimum(gx + 1, n_gx - 1), gy, blk), device_id_type=MESH)),
            (gx > 0, gx < n_gx - 1, pltpu.make_async_remote_copy(
                ref.at[pl.ds(lo, width), pl.ds(8, Y)], ref.at[pl.ds(X + lo, width), pl.ds(8, Y)],
                send.at[1], recv.at[1], device_id=(jnp.maximum(gx - 1, 0), gy, blk), device_id_type=MESH)),
            (gy < ny - 1, gy > 0, pltpu.make_async_remote_copy(
                ref.at[pl.ds(lo, X), pl.ds(Y, 8)], ref.at[pl.ds(lo, X), pl.ds(0, 8)],
                send.at[2], recv.at[2], device_id=(gx, jnp.minimum(gy + 1, ny - 1), blk), device_id_type=MESH)),
            (gy > 0, gy < ny - 1, pltpu.make_async_remote_copy(
                ref.at[pl.ds(lo, X), pl.ds(8, 8)], ref.at[pl.ds(lo, X), pl.ds(8 + Y, 8)],
                send.at[3], recv.at[3], device_id=(gx, jnp.maximum(gy - 1, 0), blk), device_id_type=MESH)),
            (None, None, pltpu.make_async_remote_copy(
                ZS.at[field], ZR.at[field],
                send.at[4], recv.at[4], device_id=(gx, gy, 1 - blk), device_id_type=MESH)),
        ]

    def start(copies):
        for sends, _, copy in copies:
            if sends is None:
                copy.start()
            else:
                pl.when(sends)(lambda copy=copy: copy.start())

    def finish(copies):
        for sends, gets, copy in copies:
            if sends is None:
                copy.wait_send()
                copy.wait_recv()
            else:
                pl.when(sends)(lambda copy=copy: copy.wait_send())
                pl.when(gets)(lambda copy=copy: copy.wait_recv())

    def drained(ref, sem):
        pltpu.make_async_copy(ref, ref, sem).wait()

    for dz in range(1, nz):
        pltpu.make_async_remote_copy(
            CS.at[pl.ds(zs[dz], 1)], CR.at[pl.ds(dz, 1)], cs_sem, cr_sem,
            device_id=(zs[dz] * nx + xi, gy, blk), device_id_type=MESH,
        ).start()
    own_col = pltpu.make_async_copy(CS.at[pl.ds(zi, 1)], CR.at[pl.ds(0, 1)], self_sem.at[0])
    own_col.start()

    halo_p = shares(E, 0, 3)
    halo_b = shares(EB, 1, 2)
    start(halo_p)
    start(halo_b)

    for dz in order:
        for dx, dy in plane:
            k = (dz * nx + dx) * ny + dy
            if k == 0:
                continue
            dest_gx = zs[dz] * nx + xs[dx]
            pltpu.make_async_remote_copy(
                SB.at[dest_gx * ny + ys[dy]], RV.at[k], as_sem, ar_sem,
                device_id=(dest_gx, ys[dy], blk), device_id_type=MESH,
            ).start()
    own = pltpu.make_async_copy(SB.at[me], RV.at[0], self_sem.at[1])
    own.start()

    drained(CR.at[pl.ds(0, nz - 1)], cr_sem)
    own_col.wait()
    for dx, dy in plane[1:]:
        pltpu.make_async_remote_copy(
            CR, CA.at[dx * ny + dy], fs_sem, fr_sem,
            device_id=(zi * nx + xs[dx], ys[dy], blk), device_id_type=MESH,
        ).start()
    own_tile = pltpu.make_async_copy(CR, CA.at[0], self_sem.at[2])
    own_tile.start()

    weights_row = lax.broadcasted_iota(jnp.int32, (16, LANES), 0)
    place_row = lax.broadcasted_iota(jnp.int32, (16, HR), 0)
    place_code = jnp.where(
        place_row == 0, jnp.broadcast_to(placing // 32, (16, HR)),
        jnp.where(place_row == 1, jnp.broadcast_to(placing % 32, (16, HR)), 0),
    ).astype(F32).astype(BF16)
    place_w = jnp.where(weights_row == 0, 32.0, jnp.where(weights_row == 1, 1.0, 0.0)).astype(BF16)
    placing_col = dot_tn(place_code, place_w)
    span = min(LANES, NB * CAP)
    for m in range(NB * CAP // span):
        cell = (lax.broadcasted_iota(jnp.int32, (HR, span), 1) + m * span).astype(F32)
        PM[:, m * span : (m + 1) * span] = onehot(placing_col[:, :span] == cell)

    lane = lax.broadcasted_iota(jnp.int32, (Y, LANES), 1)
    halo_lanes = (lane < LANES // 2) == (jnp.broadcast_to(blk, (Y, LANES)) == 0)

    def beside(field, q, i):
        packed = ZR[field, q]
        tiles = []
        for t in range(T):
            m = i * T + t
            tiles.append(pltpu.roll(packed, LANES - 4 * m, 1) if m else packed)
        return jnp.where(halo_lanes, jnp.concatenate(tiles, axis=0), 0.0)

    def up(k, near, far):
        return pltpu.roll(jnp.where(lane < k, far, near), LANES - k, 1)

    def down(k, near, far):
        return pltpu.roll(jnp.where(lane >= LANES - k, far, near), k, 1)

    finish(halo_b)

    def faces(q, _):
        for i in range(PER):
            c = q * PER + i
            BX[c] = (EB[c, 8 : 8 + Y] + EB[c + 1, 8 : 8 + Y]) * FACE
            BY[c] = (EB[c + 2, 6 : 14 + Y] + EB[c + 2, 7 : 15 + Y]) * FACE
            own_b = EB[c + 2, 8 : 8 + Y]
            far_b = beside(1, q, i)
            BZ[c] = (own_b + up(1, own_b, far_b)) * FACE
            BZO[c] = (far_b + up(1, far_b, own_b)) * FACE
        return 0

    lax.fori_loop(0, X // PER, faces, 0)
    for c in range(X, X + 3):
        BX[c] = (EB[c, 8 : 8 + Y] + EB[c + 1, 8 : 8 + Y]) * FACE

    def flux_x(src, c):
        FX[c] = wide(src[c, 8 : 8 + Y], src[c + 1, 8 : 8 + Y], src[c + 2, 8 : 8 + Y], src[c + 3, 8 : 8 + Y]) * BX[c]

    def inner_x(src):
        for c in range(3, X):
            flux_x(src, c)

    def outer_x(src):
        for c in (0, 1, 2, X, X + 1, X + 2):
            flux_x(src, c)

    def across(src, field):
        def body(q, _):
            for i in range(PER):
                c = q * PER + i
                FY[i] = wide(src[c + 3, 5 : 13 + Y], src[c + 3, 6 : 14 + Y], src[c + 3, 7 : 15 + Y], src[c + 3, 8 : 16 + Y]) * BY[c]
                near = src[c + 3, 8 : 8 + Y]
                far = beside(field, q, i)
                flux = wide(down(1, near, far), near, up(1, near, far), up(2, near, far)) * BZ[c]
                beyond = wide(down(1, far, near), far, up(1, far, near), up(2, far, near)) * BZO[c]
                TOT[c] = wide(FY[i, 0:Y], FY[i, 1 : 1 + Y], FY[i, 2 : 2 + Y], FY[i, 3 : 3 + Y]) + wide(
                    down(2, flux, beyond), down(1, flux, beyond), flux, up(1, flux, beyond)
                )
            return 0

        lax.fori_loop(0, X // PER, body, 0)

    def laplace(c):
        return TOT[c] + wide(FX[c], FX[c + 1], FX[c + 2], FX[c + 3])

    loads[3].wait()
    loads[4].wait()
    finish(halo_p)
    inner_x(E)
    outer_x(E)
    across(E, 0)

    def first(q, _):
        for i in range(PER):
            c = q * PER + i
            E2[c + 3, 8 : 8 + Y] = 2.0 * E[c + 3, 8 : 8 + Y] - PREV[c] + KAP[c] * laplace(c)
        return 0

    lax.fori_loop(0, X // PER, first, 0)

    drained(CA.at[pl.ds(0, G - 1)], fr_sem)
    own_tile.wait()
    keep = lane8 == lax.broadcasted_iota(jnp.int32, (8, LANES), 0) + spot * CAP
    for dz in range(nz):
        for j in range(G):
            line = jnp.where(keep, jnp.broadcast_to(CA[j, dz : dz + 1, :], (8, LANES)), 0.0)
            high = jnp.floor(line * (1.0 / 32.0))
            at = (dz * G + j) * 8
            MC[at : at + 8, 0:LANES] = high
            MC[at : at + 8, LANES:] = line - 32.0 * high
    w_lane = jnp.where(lax.broadcasted_iota(jnp.int32, (8, 2 * LANES), 1) < LANES, 32.0, 1.0).astype(BF16)
    w_full = jnp.where(lax.broadcasted_iota(jnp.int32, (2 * LANES, LANES), 0) < LANES, 32.0, 1.0).astype(BF16)
    col_lane = dot_nt(w_lane, MC[...].astype(BF16))[0:1].astype(jnp.int32) - 1
    chunk = min(LANES, cells)

    def build_qt(m, _):
        ids = lax.broadcasted_iota(jnp.int32, (chunk, NB * CAP), 0) + m * chunk
        QT[pl.ds(m * chunk, chunk)] = onehot(ids == jnp.broadcast_to(col_lane, (chunk, NB * CAP)))
        return 0

    lax.fori_loop(0, cells // chunk, build_qt, 0)

    def build_q(dz, _):
        col_sub = dot(MC[pl.ds(dz * GS, GS)].astype(BF16), w_full) - 1.0
        for m in range(cells // chunk):
            ids = (lax.broadcasted_iota(jnp.int32, (GS, chunk), 1) + m * chunk).astype(F32)
            Q[pl.ds(dz * GS, GS), m * chunk : (m + 1) * chunk] = onehot(col_sub[:, :chunk] == ids)
        return 0

    lax.fori_loop(0, nz, build_q, 0)

    drained(RV.at[pl.ds(0, NB - 1)], ar_sem)
    own.wait()
    rows = parts(RV[...].reshape(NB * CAP, LANES))
    halo_m = shares(E2, 2, 3)

    def middle(q, _):
        pushed = joined(dot(QT[pl.ds(q * PER * Y, PER * Y)], rows)).reshape(PER, Y, LANES)
        for i in range(PER):
            c = q * PER + i
            force = (GAIN * KAP[c]) * pushed[i]
            E2[c + 3, 8 : 8 + Y] = E2[c + 3, 8 : 8 + Y] + force
            PREV[c] = force - E[c + 3, 8 : 8 + Y]
        return 0

    lax.fori_loop(0, X // PER, middle, 0)
    start(halo_m[0:4])
    gather_edge(2, E2, 3)
    start(halo_m[4:5])
    inner_x(E2)
    finish(halo_m[4:5])
    finish(halo_m[2:4])
    across(E2, 2)
    finish(halo_m[0:2])
    outer_x(E2)

    def second(q, _):
        for i in range(PER):
            c = q * PER + i
            val = 2.0 * E2[c + 3, 8 : 8 + Y] + PREV[c] + KAP[c] * laplace(c)
            TOT[c] = val
            hi, lo = split2(val)
            NEXT[pl.ds(c * Y, Y), 0:LANES] = hi
            NEXT[pl.ds(c * Y, Y), LANES : 2 * LANES] = lo
        return 0

    lax.fori_loop(0, X // PER, second, 0)
    out_copy = pltpu.make_async_copy(TOT, out_hbm, out_sem.at[0])
    out_copy.start()

    for dz in order:
        PK[dz * G : (dz + 1) * G] = joined(dot(Q[dz * GS : (dz + 1) * GS], NEXT[...])).reshape(G, 8, LANES)
        for dx, dy in plane:
            k = (dz * nx + dx) * ny + dy
            if k == 0:
                continue
            pltpu.make_async_remote_copy(
                PK.at[k], RET.at[me], bs_sem, br_sem,
                device_id=(zb[dz] * nx + xb[dx], yb[dy], blk), device_id_type=MESH,
            ).start()
    back = pltpu.make_async_copy(PK.at[0], RET.at[me], self_sem.at[3])
    back.start()

    drained(CR.at[pl.ds(0, nz - 1)], cs_sem)
    drained(CA.at[pl.ds(0, G - 1)], fs_sem)
    drained(SB.at[pl.ds(0, NB - 1)], as_sem)
    drained(PK.at[pl.ds(0, NB - 1)], bs_sem)
    drained(RET.at[pl.ds(0, NB - 1)], br_sem)
    back.wait()
    HOUT[...] = joined(dot(PM[...], parts(RET[...].reshape(NB * CAP, LANES))))
    hull_copy = pltpu.make_async_copy(HOUT, hp_hbm, out_sem.at[1])
    hull_copy.start()
    hull_copy.wait()
    out_copy.wait()


def solution(mesh):
    n_gx, n_gy = mesh.shape["gx"], mesh.shape["gy"]
    dims = torus(n_gx, n_gy)
    NB = n_gx * n_gy

    def local(pressure, pressure_prev, buoyancy, kappa, hull_accel, row_block, row_column):
        X, Y, Z = pressure.shape
        HR = hull_accel.shape[0]
        any_spec = pl.BlockSpec(memory_space=pl.ANY)
        vmem_spec = pl.BlockSpec(memory_space=pltpu.VMEM)
        dma = pltpu.SemaphoreType.DMA
        V = pltpu.VMEM
        return pl.pallas_call(
            functools.partial(kernel, dims),
            out_shape=(
                jax.ShapeDtypeStruct((X, Y, Z), F32),
                jax.ShapeDtypeStruct((HR, Z), F32),
            ),
            in_specs=[any_spec] * 5 + [vmem_spec] * 2,
            out_specs=[any_spec] * 2,
            scratch_shapes=[
                V((X + 6, Y + 16, Z), F32),
                V((X + 4, Y + 16, Z), F32),
                V((X + 6, Y + 16, Z), F32),
                V((3, X * Y // 256, 8, Z), F32),
                V((3, X * Y // 256, 8, Z), F32),
                V((X, Y, Z), F32),
                V((X, Y, Z), F32),
                V((HR, Z), F32),
                V((X + 3, Y, Z), F32),
                V((256 // Y, Y + 8, Z), F32),
                V((X, Y, Z), F32),
                V((X + 3, Y, Z), F32),
                V((X, Y + 8, Z), F32),
                V((X, Y, Z), F32),
                V((X, Y, Z), F32),
                V((X * Y, 2 * Z), BF16),
                V((8, Z), F32),
                V((dims[0], Z), F32),
                V((dims[1] * dims[2], dims[0], Z), F32),
                V((NB * CAP, 2 * Z), F32),
                V((NB, CAP, Z), F32),
                V((NB, CAP, Z), F32),
                V((NB, CAP, Z), F32),
                V((NB, CAP, Z), F32),
                V((NB * CAP, X * Y), BF16),
                V((X * Y, NB * CAP), BF16),
                V((HR, NB * CAP), BF16),
                V((HR, Z), F32),
                dma((5,)), dma((2,)), dma((3, 5)), dma((3, 5)),
                dma, dma, dma, dma, dma, dma, dma, dma, dma((4,)),
            ],
            compiler_params=pltpu.CompilerParams(collective_id=0, has_side_effects=True, vmem_limit_bytes=60 * 1024 * 1024),
            name="hull_leapfrog",
        )(
            pressure, pressure_prev, buoyancy, kappa, hull_accel,
            row_block.reshape(1, HR), row_column.reshape(1, HR),
        )

    return jax.shard_map(
        local,
        mesh=mesh,
        in_specs=(
            P("gx", "gy", "blk"),
            P("gx", "gy", "blk"),
            P("gx", "gy", "blk"),
            P("gx", "gy", "blk"),
            P(("gx", "gy", "blk"), None),
            P(("gx", "gy", "blk"), None),
            P(("gx", "gy", "blk"), None),
        ),
        out_specs=(P("gx", "gy", "blk"), P(("gx", "gy", "blk"), None)),
        check_vma=False,
    )
```

```python
import functools

import jax
import jax.numpy as jnp
from jax import lax
from jax.experimental import pallas as pl
from jax.experimental.pallas import tpu as pltpu
from jax.sharding import PartitionSpec as P

MESH = pl.DeviceIdType.MESH
F32 = jnp.float32
BF16 = jnp.bfloat16
LANES = 128
CAP = 8
COURANT = 0.05
GAIN = 0.5
FACE = COURANT * 0.5 / 576.0


def torus(n_gx, n_gy):
    nx = 4 if n_gx % 4 == 0 and n_gx > 4 else 2
    return n_gx // nx, nx, n_gy


def split2(v):
    hi = v.astype(BF16)
    lo = (v - hi.astype(F32)).astype(BF16)
    return hi, lo


def parts(v):
    hi, lo = split2(v)
    return jnp.concatenate([hi, lo], axis=1)


def joined(v):
    return v[:, :LANES] + v[:, LANES:]


def wide(a, b, c, d):
    return 27.0 * (c - b) - (d - a)


def dot(a, b):
    return jnp.dot(a, b, preferred_element_type=F32)


def dot_nt(a, b):
    return lax.dot_general(a, b, (((1,), (1,)), ((), ())), preferred_element_type=F32)


def dot_tn(a, b):
    return lax.dot_general(a, b, (((0,), (0,)), ((), ())), preferred_element_type=F32)


def onehot(mask):
    return jnp.where(mask, 1.0, 0.0).astype(BF16)


def kernel(
    dims,
    p_hbm, prev_hbm, b_hbm, kap_hbm, hull_hbm, rb_hbm, rc_hbm,
    out_ref, hp_ref,
    E, EB, E2, ZS, ZR, PREV, KAP, HULL, FX, FY, TOT, BX, BY, BZ, BZO, NEXT,
    CS, CR, CA, MC, SB, RV, ROWS, PK, RET, Q, QT, PM, RB, RC,
    in_sem, hs_sem, hr_sem, cs_sem, cr_sem, fs_sem, fr_sem, as_sem, ar_sem, bs_sem, br_sem, self_sem,
):
    nz, nx, ny = dims
    NB = nz * nx * ny
    G = nx * ny
    GS = G * CAP
    X, Y = PREV.shape[0], PREV.shape[1]
    T = Y // 8
    PER = LANES // (4 * T)
    HR = HULL.shape[0]
    cells = X * Y
    n_gx = nz * nx
    gx = lax.axis_index("gx")
    gy = lax.axis_index("gy")
    blk = lax.axis_index("blk")
    zi = gx // nx
    xi = gx % nx
    me = gx * ny + gy
    spot = xi * ny + gy

    zs = [(zi + dz) % nz for dz in range(nz)]
    xs = [(xi + dx) % nx for dx in range(nx)]
    ys = [(gy + dy) % ny for dy in range(ny)]
    zb = [(zi + nz - dz) % nz for dz in range(nz)]
    xb = [(xi + nx - dx) % nx for dx in range(nx)]
    yb = [(gy + ny - dy) % ny for dy in range(ny)]
    plane = [(dx, dy) for dx in range(nx) for dy in range(ny)]

    def hops(offset):
        return sum(min(d, n - d) for d, n in zip(offset, dims))

    slots = sorted(
        [(dz, dx, dy) for dz in range(nz) for dx, dy in plane],
        key=lambda o: (-hops(o), o[0] % 2),
    )
    parts_n = 4
    share = NB // parts_n

    def group_of(k):
        return k // share

    barrier = pltpu.get_barrier_semaphore()
    for dz, dx, dy in slots[:-1]:
        pl.semaphore_signal(
            barrier, inc=1, device_id=(zs[dz] * nx + xs[dx], ys[dy], blk), device_id_type=MESH
        )
    pl.semaphore_signal(barrier, inc=1, device_id=(gx, gy, 1 - blk), device_id_type=MESH)

    loads = [
        pltpu.make_async_copy(rb_hbm, RB, in_sem.at[5]),
        pltpu.make_async_copy(rc_hbm, RC, in_sem.at[6]),
        pltpu.make_async_copy(hull_hbm, HULL, in_sem.at[0]),
        pltpu.make_async_copy(p_hbm, E.at[pl.ds(3, X), pl.ds(8, Y)], in_sem.at[1]),
        pltpu.make_async_copy(b_hbm, EB.at[pl.ds(2, X), pl.ds(8, Y)], in_sem.at[2]),
        pltpu.make_async_copy(prev_hbm, PREV, in_sem.at[3]),
        pltpu.make_async_copy(kap_hbm, KAP, in_sem.at[4]),
    ]
    for load in loads:
        load.start()

    for ref, w in ((E, 3), (EB, 2), (E2, 3)):
        @pl.when(gx == 0)
        def _(ref=ref, w=w):
            ref[0:w] = jnp.zeros((w,) + ref.shape[1:], F32)

        @pl.when(gx == n_gx - 1)
        def _(ref=ref, w=w):
            ref[w + X :] = jnp.zeros((w,) + ref.shape[1:], F32)

        @pl.when(gy == 0)
        def _(ref=ref, w=w):
            ref[w : w + X, 0:8] = jnp.zeros((X, 8, LANES), F32)

        @pl.when(gy == ny - 1)
        def _(ref=ref, w=w):
            ref[w : w + X, 8 + Y :] = jnp.zeros((X, 8, LANES), F32)

    loads[0].wait()
    loads[1].wait()
    rb = RB[...]
    owner = onehot(jnp.broadcast_to(rb, (NB, HR)) == lax.broadcasted_iota(jnp.int32, (NB, HR), 0))
    before = onehot(
        lax.broadcasted_iota(jnp.int32, (HR, HR), 0) < lax.broadcasted_iota(jnp.int32, (HR, HR), 1)
    )
    earlier = dot(owner, before)
    slot = jnp.sum(owner.astype(F32) * earlier, axis=0, keepdims=True).astype(jnp.int32)
    placing = rb * CAP + slot
    code = RC[...] + 1
    row_z = lax.broadcasted_iota(jnp.int32, (16, HR), 0)
    which_z = jnp.broadcast_to(placing // GS, (16, HR))
    coded = jnp.where(row_z == which_z, jnp.broadcast_to(code // 32, (16, HR)), 0) + jnp.where(
        row_z == which_z + 8, jnp.broadcast_to(code % 32, (16, HR)), 0
    )
    lane_of = onehot(lax.broadcasted_iota(jnp.int32, (LANES, HR), 0) == jnp.broadcast_to(placing % GS, (LANES, HR)))
    sums = dot_nt(coded.astype(F32).astype(BF16), lane_of)
    CS[...] = sums[0:8] * 32.0 + sums[8:16]

    loads[2].wait()
    hull_parts = parts(HULL[...])

    def pack(m, _):
        rows = lax.broadcasted_iota(jnp.int32, (GS, HR), 0) + m * GS
        pt = onehot(rows == jnp.broadcast_to(placing, (GS, HR)))
        SB[pl.ds(m * G, G)] = joined(dot(pt, hull_parts)).reshape(G, 8, LANES)
        return 0

    lax.fori_loop(0, nz, pack, 0)

    lane8 = lax.broadcasted_iota(jnp.int32, (8, LANES), 1)
    edge = jnp.where(jnp.broadcast_to(blk, (8, LANES)) == 0, (lane8 + 3) % LANES, lane8) // 4

    def gather_edge(field, ref, lo):
        for q in range(X // PER):
            acc = jnp.zeros((8, LANES), F32)
            for i in range(PER):
                for t in range(T):
                    m = i * T + t
                    tile = ref[lo + q * PER + i, 8 + 8 * t : 16 + 8 * t]
                    acc = jnp.where(edge == m, pltpu.roll(tile, 4 * m, 1) if m else tile, acc)
            ZS[field, q] = acc

    loads[3].wait()
    loads[4].wait()
    gather_edge(0, E, 3)
    gather_edge(1, EB, 2)

    pl.semaphore_wait(barrier, NB)

    def shares(ref, field, width):
        lo = width
        send, recv = hs_sem.at[field], hr_sem.at[field]
        return [
            (gx < n_gx - 1, gx > 0, pltpu.make_async_remote_copy(
                ref.at[pl.ds(X + lo - width, width), pl.ds(8, Y)], ref.at[pl.ds(lo - width, width), pl.ds(8, Y)],
                send.at[0], recv.at[0], device_id=(jnp.minimum(gx + 1, n_gx - 1), gy, blk), device_id_type=MESH)),
            (gx > 0, gx < n_gx - 1, pltpu.make_async_remote_copy(
                ref.at[pl.ds(lo, width), pl.ds(8, Y)], ref.at[pl.ds(X + lo, width), pl.ds(8, Y)],
                send.at[1], recv.at[1], device_id=(jnp.maximum(gx - 1, 0), gy, blk), device_id_type=MESH)),
            (gy < ny - 1, gy > 0, pltpu.make_async_remote_copy(
                ref.at[pl.ds(lo, X), pl.ds(Y + 8 - width, width)], ref.at[pl.ds(lo, X), pl.ds(8 - width, width)],
                send.at[2], recv.at[2], device_id=(gx, jnp.minimum(gy + 1, ny - 1), blk), device_id_type=MESH)),
            (gy > 0, gy < ny - 1, pltpu.make_async_remote_copy(
                ref.at[pl.ds(lo, X), pl.ds(8, width)], ref.at[pl.ds(lo, X), pl.ds(8 + Y, width)],
                send.at[3], recv.at[3], device_id=(gx, jnp.maximum(gy - 1, 0), blk), device_id_type=MESH)),
            (None, None, pltpu.make_async_remote_copy(
                ZS.at[field], ZR.at[field],
                send.at[4], recv.at[4], device_id=(gx, gy, 1 - blk), device_id_type=MESH)),
        ]

    def start(copies):
        for sends, _, copy in copies:
            if sends is None:
                copy.start()
            else:
                pl.when(sends)(lambda copy=copy: copy.start())

    def finish(copies):
        for sends, gets, copy in copies:
            if sends is None:
                copy.wait_send()
                copy.wait_recv()
            else:
                pl.when(sends)(lambda copy=copy: copy.wait_send())
                pl.when(gets)(lambda copy=copy: copy.wait_recv())

    def drained(ref, sem):
        pltpu.make_async_copy(ref, ref, sem).wait()

    for dz in range(1, nz):
        pltpu.make_async_remote_copy(
            CS.at[pl.ds(zs[dz], 1)], CR.at[pl.ds(dz, 1)], cs_sem, cr_sem,
            device_id=(zs[dz] * nx + xi, gy, blk), device_id_type=MESH,
        ).start()
    own_col = pltpu.make_async_copy(CS.at[pl.ds(zi, 1)], CR.at[pl.ds(0, 1)], self_sem.at[0])
    own_col.start()

    halo_p = shares(E, 0, 3)
    halo_b = shares(EB, 1, 2)
    start(halo_p)
    start(halo_b)

    for k, (dz, dx, dy) in enumerate(slots[:-1]):
        dest_gx = zs[dz] * nx + xs[dx]
        pltpu.make_async_remote_copy(
            SB.at[dest_gx * ny + ys[dy]], RV.at[k], as_sem, ar_sem.at[group_of(k)],
            device_id=(dest_gx, ys[dy], blk), device_id_type=MESH,
        ).start()
    own = pltpu.make_async_copy(SB.at[me], RV.at[NB - 1], self_sem.at[1])
    own.start()

    drained(CR.at[pl.ds(0, nz - 1)], cr_sem)
    own_col.wait()
    for dx, dy in plane[1:]:
        pltpu.make_async_remote_copy(
            CR, CA.at[dx * ny + dy], fs_sem, fr_sem,
            device_id=(zi * nx + xs[dx], ys[dy], blk), device_id_type=MESH,
        ).start()
    own_tile = pltpu.make_async_copy(CR, CA.at[0], self_sem.at[2])
    own_tile.start()

    rel_z = (placing // GS + (nz - zi)) % nz
    rel_x = (placing // (CAP * ny) % nx + (nx - xi)) % nx
    rel_y = (placing // CAP % ny + (ny - gy)) % ny
    relative = ((rel_z * nx + rel_x) * ny + rel_y) * CAP + placing % CAP
    weights_row = lax.broadcasted_iota(jnp.int32, (16, LANES), 0)
    place_row = lax.broadcasted_iota(jnp.int32, (16, HR), 0)
    place_code = jnp.where(
        place_row == 0, jnp.broadcast_to(relative // 32, (16, HR)),
        jnp.where(place_row == 1, jnp.broadcast_to(relative % 32, (16, HR)), 0),
    ).astype(F32).astype(BF16)
    place_w = jnp.where(weights_row == 0, 32.0, jnp.where(weights_row == 1, 1.0, 0.0)).astype(BF16)
    placing_col = dot_tn(place_code, place_w)
    span = min(LANES, NB * CAP)
    for m in range(NB * CAP // span):
        spot_lane = lax.broadcasted_iota(jnp.int32, (8, span), 1)
        label = spot_lane % CAP
        for j in range(span // CAP):
            dz, dx, dy = slots[m * (span // CAP) + j]
            base = ((dz * nx + dx) * ny + dy) * CAP
            label = jnp.where(spot_lane // CAP == j, label + base, label)
        label = jnp.broadcast_to(label[0:1], (HR, span)).astype(F32)
        PM[:, m * span : (m + 1) * span] = onehot(placing_col[:, :span] == label)

    lane = lax.broadcasted_iota(jnp.int32, (Y, LANES), 1)
    halo_lanes = (lane < LANES // 2) == (jnp.broadcast_to(blk, (Y, LANES)) == 0)

    def beside(field, q, i):
        packed = ZR[field, q]
        tiles = []
        for t in range(T):
            m = i * T + t
            tiles.append(pltpu.roll(packed, LANES - 4 * m, 1) if m else packed)
        return jnp.where(halo_lanes, jnp.concatenate(tiles, axis=0), 0.0)

    def up(k, near, far):
        return pltpu.roll(jnp.where(lane < k, far, near), LANES - k, 1)

    def down(k, near, far):
        return pltpu.roll(jnp.where(lane >= LANES - k, far, near), k, 1)

    finish(halo_b)

    def faces(q, _):
        for i in range(PER):
            c = q * PER + i
            BX[c] = (EB[c, 8 : 8 + Y] + EB[c + 1, 8 : 8 + Y]) * FACE
            BY[c] = (EB[c + 2, 6 : 14 + Y] + EB[c + 2, 7 : 15 + Y]) * FACE
            own_b = EB[c + 2, 8 : 8 + Y]
            far_b = beside(1, q, i)
            BZ[c] = (own_b + up(1, own_b, far_b)) * FACE
            BZO[c] = (far_b + up(1, far_b, own_b)) * FACE
        return 0

    lax.fori_loop(0, X // PER, faces, 0)
    for c in range(X, X + 3):
        BX[c] = (EB[c, 8 : 8 + Y] + EB[c + 1, 8 : 8 + Y]) * FACE

    def flux_x(src, c):
        FX[c] = wide(src[c, 8 : 8 + Y], src[c + 1, 8 : 8 + Y], src[c + 2, 8 : 8 + Y], src[c + 3, 8 : 8 + Y]) * BX[c]

    def inner_x(src):
        for c in range(3, X):
            flux_x(src, c)

    def outer_x(src):
        for c in (0, 1, 2, X, X + 1, X + 2):
            flux_x(src, c)

    def across_z(src, field):
        def body(q, _):
            for i in range(PER):
                c = q * PER + i
                near = src[c + 3, 8 : 8 + Y]
                far = beside(field, q, i)
                flux = wide(down(1, near, far), near, up(1, near, far), up(2, near, far)) * BZ[c]
                beyond = wide(down(1, far, near), far, up(1, far, near), up(2, far, near)) * BZO[c]
                TOT[c] = wide(down(2, flux, beyond), down(1, flux, beyond), flux, up(1, flux, beyond))
            return 0

        lax.fori_loop(0, X // PER, body, 0)

    def across_y(src, c, i):
        FY[i] = wide(src[c + 3, 5 : 13 + Y], src[c + 3, 6 : 14 + Y], src[c + 3, 7 : 15 + Y], src[c + 3, 8 : 16 + Y]) * BY[c]
        return wide(FY[i, 0:Y], FY[i, 1 : 1 + Y], FY[i, 2 : 2 + Y], FY[i, 3 : 3 + Y])

    def laplace(c):
        return TOT[c] + wide(FX[c], FX[c + 1], FX[c + 2], FX[c + 3])

    loads[5].wait()
    loads[6].wait()
    finish(halo_p)
    inner_x(E)
    outer_x(E)
    across_z(E, 0)

    def first(q, _):
        for i in range(PER):
            c = q * PER + i
            E2[c + 3, 8 : 8 + Y] = 2.0 * E[c + 3, 8 : 8 + Y] - PREV[c] + KAP[c] * (laplace(c) + across_y(E, c, i))
        return 0

    lax.fori_loop(0, X // PER, first, 0)

    drained(CA.at[pl.ds(0, G - 1)], fr_sem)
    own_tile.wait()
    keep = lane8 == lax.broadcasted_iota(jnp.int32, (8, LANES), 0) + spot * CAP
    for k, (dz, dx, dy) in enumerate(slots):
        line = jnp.where(keep, jnp.broadcast_to(CA[dx * ny + dy, dz : dz + 1, :], (8, LANES)), 0.0)
        high = jnp.floor(line * (1.0 / 32.0))
        MC[k * 8 : k * 8 + 8, 0:LANES] = high
        MC[k * 8 : k * 8 + 8, LANES:] = line - 32.0 * high
    w_lane = jnp.where(lax.broadcasted_iota(jnp.int32, (8, 2 * LANES), 1) < LANES, 32.0, 1.0).astype(BF16)
    w_full = jnp.where(lax.broadcasted_iota(jnp.int32, (2 * LANES, LANES), 0) < LANES, 32.0, 1.0).astype(BF16)
    col_lane = dot_nt(w_lane, MC[...].astype(BF16))[0:1].astype(jnp.int32) - 1
    chunk = min(LANES, cells)

    def build_qt(m, _):
        ids = lax.broadcasted_iota(jnp.int32, (chunk, NB * CAP), 0) + m * chunk
        QT[pl.ds(m * chunk, chunk)] = onehot(ids == jnp.broadcast_to(col_lane, (chunk, NB * CAP)))
        return 0

    lax.fori_loop(0, cells // chunk, build_qt, 0)

    def build_q(dz, _):
        col_sub = dot(MC[pl.ds(dz * GS, GS)].astype(BF16), w_full) - 1.0
        for m in range(cells // chunk):
            ids = (lax.broadcasted_iota(jnp.int32, (GS, chunk), 1) + m * chunk).astype(F32)
            Q[pl.ds(dz * GS, GS), m * chunk : (m + 1) * chunk] = onehot(col_sub[:, :chunk] == ids)
        return 0

    lax.fori_loop(0, nz, build_q, 0)

    for n in range(parts_n):
        last = n == parts_n - 1
        drained(RV.at[pl.ds(0, share - 1 if last else share)], ar_sem.at[n])
        if last:
            own.wait()
        ROWS[n * share * CAP : (n + 1) * share * CAP] = parts(
            RV[n * share : (n + 1) * share].reshape(share * CAP, LANES)
        )
    halo_m = shares(E2, 2, 3)

    def middle(q):
        pushed = joined(dot(QT[q * PER * Y : (q + 1) * PER * Y], ROWS[...])).reshape(PER, Y, LANES)
        for i in range(PER):
            c = q * PER + i
            force = (GAIN * KAP[c]) * pushed[i]
            E2[c + 3, 8 : 8 + Y] = E2[c + 3, 8 : 8 + Y] + force
            PREV[c] = force - E[c + 3, 8 : 8 + Y]

    quads = X // PER
    ends = sorted({0, quads - 1})
    inside = [q for q in range(quads) if q not in ends]
    for q in ends:
        middle(q)
    start(halo_m[0:2])
    for q in inside:
        middle(q)
    start(halo_m[2:4])
    gather_edge(2, E2, 3)
    start(halo_m[4:5])
    inner_x(E2)
    finish(halo_m[4:5])
    across_z(E2, 2)
    finish(halo_m[2:4])

    def second(q, with_y):
        for i in range(PER):
            c = q * PER + i
            total = laplace(c)
            if with_y:
                total = total + across_y(E2, c, i)
            val = 2.0 * E2[c + 3, 8 : 8 + Y] + PREV[c] + KAP[c] * total
            out_ref[c] = val
            hi, lo = split2(val)
            NEXT[c * Y : (c + 1) * Y, 0:LANES] = hi
            NEXT[c * Y : (c + 1) * Y, LANES : 2 * LANES] = lo

    for q in inside:
        second(q, True)
    for q in ends:
        for i in range(PER):
            c = q * PER + i
            TOT[c] = TOT[c] + across_y(E2, c, i)

    pieces = max(parts_n, NB * CAP // LANES)
    count = NB // pieces

    def pick(n, quad):
        at = slice(quad * PER * Y, (quad + 1) * PER * Y)
        return joined(dot(Q[n * count * CAP : (n + 1) * count * CAP, at], NEXT[at])).reshape(count, 8, LANES)

    for n in range(pieces):
        total = None
        for q in inside:
            total = pick(n, q) if total is None else total + pick(n, q)
        if total is not None:
            PK[n * count : (n + 1) * count] = total
    finish(halo_m[0:2])
    outer_x(E2)
    for q in ends:
        second(q, False)

    for n in range(pieces):
        total = None
        for q in ends:
            total = pick(n, q) if total is None else total + pick(n, q)
        if inside:
            total = total + PK[n * count : (n + 1) * count]
        PK[n * count : (n + 1) * count] = total
        for k in range(n * count, (n + 1) * count):
            dz, dx, dy = slots[k]
            if k < NB - 1:
                pltpu.make_async_remote_copy(
                    PK.at[k], RET.at[k], bs_sem, br_sem.at[group_of(k)],
                    device_id=(zb[dz] * nx + xb[dx], yb[dy], blk), device_id_type=MESH,
                ).start()
    back = pltpu.make_async_copy(PK.at[NB - 1], RET.at[NB - 1], self_sem.at[3])
    back.start()

    drained(CR.at[pl.ds(0, nz - 1)], cs_sem)
    drained(CA.at[pl.ds(0, G - 1)], fs_sem)
    drained(SB.at[pl.ds(0, NB - 1)], as_sem)
    for n in range(parts_n):
        last = n == parts_n - 1
        drained(RET.at[pl.ds(0, share - 1 if last else share)], br_sem.at[n])
        if last:
            back.wait()
        at = slice(n * share * CAP, (n + 1) * share * CAP)
        got = joined(dot(PM[:, at], parts(RET[n * share : (n + 1) * share].reshape(share * CAP, LANES))))
        hp_ref[...] = got if n == 0 else hp_ref[...] + got
    drained(PK.at[pl.ds(0, NB - 1)], bs_sem)


def keep_out(field, rows, field_out, rows_out, sem):
    copies = [
        pltpu.make_async_copy(field, field_out, sem.at[0]),
        pltpu.make_async_copy(rows, rows_out, sem.at[1]),
    ]
    for copy in copies:
        copy.start()
    for copy in copies:
        copy.wait()


def solution(mesh):
    n_gx, n_gy = mesh.shape["gx"], mesh.shape["gy"]
    dims = torus(n_gx, n_gy)
    NB = n_gx * n_gy

    def local(pressure, pressure_prev, buoyancy, kappa, hull_accel, row_block, row_column):
        X, Y, Z = pressure.shape
        HR = hull_accel.shape[0]
        any_spec = pl.BlockSpec(memory_space=pltpu.HBM)
        vmem_spec = pl.BlockSpec(memory_space=pltpu.VMEM)
        dma = pltpu.SemaphoreType.DMA
        V = pltpu.VMEM
        results = pl.pallas_call(
            functools.partial(kernel, dims),
            out_shape=(
                jax.ShapeDtypeStruct((X, Y, Z), F32),
                jax.ShapeDtypeStruct((HR, Z), F32),
            ),
            in_specs=[any_spec] * 7,
            out_specs=[vmem_spec] * 2,
            scratch_shapes=[
                V((X + 6, Y + 16, Z), F32),
                V((X + 4, Y + 16, Z), F32),
                V((X + 6, Y + 16, Z), F32),
                V((3, X * Y // 256, 8, Z), F32),
                V((3, X * Y // 256, 8, Z), F32),
                V((X, Y, Z), F32),
                V((X, Y, Z), F32),
                V((HR, Z), F32),
                V((X + 3, Y, Z), F32),
                V((256 // Y, Y + 8, Z), F32),
                V((X, Y, Z), F32),
                V((X + 3, Y, Z), F32),
                V((X, Y + 8, Z), F32),
                V((X, Y, Z), F32),
                V((X, Y, Z), F32),
                V((X * Y, 2 * Z), BF16),
                V((8, Z), F32),
                V((dims[0], Z), F32),
                V((dims[1] * dims[2], dims[0], Z), F32),
                V((NB * CAP, 2 * Z), F32),
                V((NB, CAP, Z), F32),
                V((NB, CAP, Z), F32),
                V((NB * CAP, 2 * Z), BF16),
                V((NB, CAP, Z), F32),
                V((NB, CAP, Z), F32),
                V((NB * CAP, X * Y), BF16),
                V((X * Y, NB * CAP), BF16),
                V((HR, NB * CAP), BF16),
                V((1, HR), jnp.int32),
                V((1, HR), jnp.int32),
                dma((7,)), dma((3, 5)), dma((3, 5)),
                dma, dma, dma, dma, dma, dma((4,)), dma, dma((4,)), dma((4,)),
            ],
            compiler_params=pltpu.CompilerParams(collective_id=0, has_side_effects=True, vmem_limit_bytes=36 * 1024 * 1024),
            name="hull_leapfrog",
        )(
            *(pltpu.with_memory_space_constraint(v, pltpu.HBM) for v in (
                pressure, pressure_prev, buoyancy, kappa, hull_accel,
                row_block.reshape(1, HR), row_column.reshape(1, HR),
            ))
        )
        return pl.pallas_call(
            keep_out,
            out_shape=(
                jax.ShapeDtypeStruct((X, Y, Z), F32),
                jax.ShapeDtypeStruct((HR, Z), F32),
            ),
            in_specs=[vmem_spec] * 2,
            out_specs=[any_spec] * 2,
            scratch_shapes=[dma((2,))],
            compiler_params=pltpu.CompilerParams(vmem_limit_bytes=2 * 1024 * 1024),
            name="write_out",
        )(*results)

    return jax.shard_map(
        local,
        mesh=mesh,
        in_specs=(
            P("gx", "gy", "blk"),
            P("gx", "gy", "blk"),
            P("gx", "gy", "blk"),
            P("gx", "gy", "blk"),
            P(("gx", "gy", "blk"), None),
            P(("gx", "gy", "blk"), None),
            P(("gx", "gy", "blk"), None),
        ),
        out_specs=(P("gx", "gy", "blk"), P(("gx", "gy", "blk"), None)),
        check_vma=False,
    )
```

```python
import functools

import jax
import jax.numpy as jnp
from jax import lax
from jax.experimental import pallas as pl
from jax.experimental.pallas import tpu as pltpu
from jax.sharding import PartitionSpec as P

MESH = pl.DeviceIdType.MESH
F32 = jnp.float32
BF16 = jnp.bfloat16
LANES = 128
CAP = 8
COURANT = 0.05
GAIN = 0.5
FACE = COURANT * 0.5 / 576.0


def torus(n_gx, n_gy):
    nx = 4 if n_gx % 4 == 0 and n_gx > 4 else 2
    return n_gx // nx, nx, n_gy


def split2(v):
    hi = v.astype(BF16)
    lo = (v - hi.astype(F32)).astype(BF16)
    return hi, lo


def parts(v):
    hi, lo = split2(v)
    return jnp.concatenate([hi, lo], axis=1)


def joined(v):
    return v[:, :LANES] + v[:, LANES:]


def wide(a, b, c, d):
    return 27.0 * (c - b) - (d - a)


def dot(a, b):
    return jnp.dot(a, b, preferred_element_type=F32)


def dot_nt(a, b):
    return lax.dot_general(a, b, (((1,), (1,)), ((), ())), preferred_element_type=F32)


def dot_tn(a, b):
    return lax.dot_general(a, b, (((0,), (0,)), ((), ())), preferred_element_type=F32)


def onehot(mask):
    return jnp.where(mask, 1.0, 0.0).astype(BF16)


def kernel(
    dims,
    p_hbm, prev_hbm, b_hbm, kap_hbm, hull_hbm, rb_hbm, rc_hbm,
    out_ref, hp_ref,
    E, EB, E2, ZS, ZR, SPLIT, ZW, ZB, PREV, KAP, HULL, FX, FY, TOT, BX, BY, BZ, NEXT,
    CS, CR, CA, MC, SB, RV, ROWS, PK, RET, Q, QT, PM, RB, RC,
    in_sem, hs_sem, hr_sem, cs_sem, cr_sem, fs_sem, fr_sem, as_sem, ar_sem, bs_sem, br_sem, self_sem,
):
    nz, nx, ny = dims
    NB = nz * nx * ny
    G = nx * ny
    GS = G * CAP
    X, Y = PREV.shape[0], PREV.shape[1]
    T = Y // 8
    PER = LANES // (4 * T)
    HR = HULL.shape[0]
    cells = X * Y
    n_gx = nz * nx
    gx = lax.axis_index("gx")
    gy = lax.axis_index("gy")
    blk = lax.axis_index("blk")
    zi = gx // nx
    xi = gx % nx
    me = gx * ny + gy
    spot = xi * ny + gy

    zs = [(zi + dz) % nz for dz in range(nz)]
    xs = [(xi + dx) % nx for dx in range(nx)]
    ys = [(gy + dy) % ny for dy in range(ny)]
    zb = [(zi + nz - dz) % nz for dz in range(nz)]
    xb = [(xi + nx - dx) % nx for dx in range(nx)]
    yb = [(gy + ny - dy) % ny for dy in range(ny)]
    plane = [(dx, dy) for dx in range(nx) for dy in range(ny)]

    def hops(offset):
        return sum(min(d, n - d) for d, n in zip(offset, dims))

    slots = sorted(
        [(dz, dx, dy) for dz in range(nz) for dx, dy in plane],
        key=lambda o: (-hops(o), o[0] % 2),
    )
    parts_n = 4
    share = NB // parts_n

    def group_of(k):
        return k // share

    loads = [
        pltpu.make_async_copy(rb_hbm, RB, in_sem.at[5]),
        pltpu.make_async_copy(rc_hbm, RC, in_sem.at[6]),
        pltpu.make_async_copy(hull_hbm, HULL, in_sem.at[0]),
        pltpu.make_async_copy(p_hbm, E.at[pl.ds(3, X), pl.ds(8, Y)], in_sem.at[1]),
        pltpu.make_async_copy(b_hbm, EB.at[pl.ds(2, X), pl.ds(8, Y)], in_sem.at[2]),
        pltpu.make_async_copy(prev_hbm, PREV, in_sem.at[3]),
        pltpu.make_async_copy(kap_hbm, KAP, in_sem.at[4]),
    ]
    for load in loads:
        load.start()

    barrier = pltpu.get_barrier_semaphore()
    for dz, dx, dy in slots[:-1]:
        pl.semaphore_signal(
            barrier, inc=1, device_id=(zs[dz] * nx + xs[dx], ys[dy], blk), device_id_type=MESH
        )
    pl.semaphore_signal(barrier, inc=1, device_id=(gx, gy, 1 - blk), device_id_type=MESH)

    for ref, w in ((E, 3), (EB, 2), (E2, 3)):
        @pl.when(gx == 0)
        def _(ref=ref, w=w):
            ref[0:w] = jnp.zeros((w,) + ref.shape[1:], F32)

        @pl.when(gx == n_gx - 1)
        def _(ref=ref, w=w):
            ref[w + X :] = jnp.zeros((w,) + ref.shape[1:], F32)

        @pl.when(gy == 0)
        def _(ref=ref, w=w):
            ref[w : w + X, 0:8] = jnp.zeros((X, 8, LANES), F32)

        @pl.when(gy == ny - 1)
        def _(ref=ref, w=w):
            ref[w : w + X, 8 + Y :] = jnp.zeros((X, 8, LANES), F32)

    loads[0].wait()
    loads[1].wait()
    rb = RB[...]
    owner = onehot(jnp.broadcast_to(rb, (NB, HR)) == lax.broadcasted_iota(jnp.int32, (NB, HR), 0))
    before = onehot(
        lax.broadcasted_iota(jnp.int32, (HR, HR), 0) < lax.broadcasted_iota(jnp.int32, (HR, HR), 1)
    )
    earlier = dot(owner, before)
    slot = jnp.sum(owner.astype(F32) * earlier, axis=0, keepdims=True).astype(jnp.int32)
    placing = rb * CAP + slot
    code = RC[...] + 1
    row_z = lax.broadcasted_iota(jnp.int32, (16, HR), 0)
    which_z = jnp.broadcast_to(placing // GS, (16, HR))
    coded = jnp.where(row_z == which_z, jnp.broadcast_to(code // 32, (16, HR)), 0) + jnp.where(
        row_z == which_z + 8, jnp.broadcast_to(code % 32, (16, HR)), 0
    )
    lane_of = onehot(lax.broadcasted_iota(jnp.int32, (LANES, HR), 0) == jnp.broadcast_to(placing % GS, (LANES, HR)))
    sums = dot_nt(coded.astype(F32).astype(BF16), lane_of)
    CS[...] = sums[0:8] * 32.0 + sums[8:16]

    loads[2].wait()
    hull_parts = parts(HULL[...])

    def pack(m, _):
        rows = lax.broadcasted_iota(jnp.int32, (GS, HR), 0) + m * GS
        pt = onehot(rows == jnp.broadcast_to(placing, (GS, HR)))
        SB[pl.ds(m * G, G)] = joined(dot(pt, hull_parts)).reshape(G, 8, LANES)
        return 0

    lax.fori_loop(0, nz, pack, 0)

    e_row = lax.broadcasted_iota(jnp.int32, (8, 2 * LANES), 0)
    e_lane = lax.broadcasted_iota(jnp.int32, (8, 2 * LANES), 1) % LANES
    first_sent = jnp.broadcast_to((1 - blk) * (LANES - 3), (8, 2 * LANES))
    wanted = jnp.where(e_row < 3, first_sent + e_row, jnp.where(e_row < 5, e_row - 3, e_row + (LANES - 7)))
    edge_w = onehot((e_lane == wanted) & (e_row < 7))

    def split_planes(ref, lo, q):
        at = pl.ds(q * PER * Y, PER * Y)
        planes = [ref[q * PER + i + lo, 8 : 8 + Y] for i in range(PER)]
        SPLIT[at] = parts(jnp.concatenate(planes, axis=0))

    def gather_edge(field):
        ZS[field] = dot_nt(edge_w, SPLIT[...])

    def all_planes(ref, lo):
        def body(q, _):
            split_planes(ref, lo, q)
            return 0

        lax.fori_loop(0, X // PER, body, 0)

    loads[3].wait()
    loads[4].wait()
    all_planes(EB, 2)
    gather_edge(1)
    all_planes(E, 3)
    gather_edge(0)

    pl.semaphore_wait(barrier, NB)

    def shares(ref, field, width):
        lo = width
        send, recv = hs_sem.at[field], hr_sem.at[field]
        return [
            (gx < n_gx - 1, gx > 0, pltpu.make_async_remote_copy(
                ref.at[pl.ds(X + lo - width, width), pl.ds(8, Y)], ref.at[pl.ds(lo - width, width), pl.ds(8, Y)],
                send.at[0], recv.at[0], device_id=(jnp.minimum(gx + 1, n_gx - 1), gy, blk), device_id_type=MESH)),
            (gx > 0, gx < n_gx - 1, pltpu.make_async_remote_copy(
                ref.at[pl.ds(lo, width), pl.ds(8, Y)], ref.at[pl.ds(X + lo, width), pl.ds(8, Y)],
                send.at[1], recv.at[1], device_id=(jnp.maximum(gx - 1, 0), gy, blk), device_id_type=MESH)),
            (gy < ny - 1, gy > 0, pltpu.make_async_remote_copy(
                ref.at[pl.ds(lo, X), pl.ds(Y + 8 - width, width)], ref.at[pl.ds(lo, X), pl.ds(8 - width, width)],
                send.at[2], recv.at[2], device_id=(gx, jnp.minimum(gy + 1, ny - 1), blk), device_id_type=MESH)),
            (gy > 0, gy < ny - 1, pltpu.make_async_remote_copy(
                ref.at[pl.ds(lo, X), pl.ds(8, width)], ref.at[pl.ds(lo, X), pl.ds(8 + Y, width)],
                send.at[3], recv.at[3], device_id=(gx, jnp.maximum(gy - 1, 0), blk), device_id_type=MESH)),
            (None, None, pltpu.make_async_remote_copy(
                ZS.at[field], ZR.at[field],
                send.at[4], recv.at[4], device_id=(gx, gy, 1 - blk), device_id_type=MESH)),
        ]

    def start(copies):
        for sends, _, copy in copies:
            if sends is None:
                copy.start()
            else:
                pl.when(sends)(lambda copy=copy: copy.start())

    def finish(copies):
        for sends, gets, copy in copies:
            if sends is None:
                copy.wait_send()
                copy.wait_recv()
            else:
                pl.when(sends)(lambda copy=copy: copy.wait_send())
                pl.when(gets)(lambda copy=copy: copy.wait_recv())

    def drained(ref, sem):
        pltpu.make_async_copy(ref, ref, sem).wait()

    for dz in range(1, nz):
        pltpu.make_async_remote_copy(
            CS.at[pl.ds(zs[dz], 1)], CR.at[pl.ds(dz, 1)], cs_sem, cr_sem,
            device_id=(zs[dz] * nx + xi, gy, blk), device_id_type=MESH,
        ).start()
    own_col = pltpu.make_async_copy(CS.at[pl.ds(zi, 1)], CR.at[pl.ds(0, 1)], self_sem.at[0])
    own_col.start()

    halo_p = shares(E, 0, 3)
    halo_b = shares(EB, 1, 2)
    start(halo_p)
    start(halo_b)

    for k, (dz, dx, dy) in enumerate(slots[:-1]):
        dest_gx = zs[dz] * nx + xs[dx]
        pltpu.make_async_remote_copy(
            SB.at[dest_gx * ny + ys[dy]], RV.at[k], as_sem, ar_sem.at[group_of(k)],
            device_id=(dest_gx, ys[dy], blk), device_id_type=MESH,
        ).start()
    own = pltpu.make_async_copy(SB.at[me], RV.at[NB - 1], self_sem.at[1])
    own.start()

    drained(CR.at[pl.ds(0, nz - 1)], cr_sem)
    own_col.wait()
    for dx, dy in plane[1:]:
        pltpu.make_async_remote_copy(
            CR, CA.at[dx * ny + dy], fs_sem, fr_sem,
            device_id=(zi * nx + xs[dx], ys[dy], blk), device_id_type=MESH,
        ).start()
    own_tile = pltpu.make_async_copy(CR, CA.at[0], self_sem.at[2])
    own_tile.start()

    rel_z = (placing // GS + (nz - zi)) % nz
    rel_x = (placing // (CAP * ny) % nx + (nx - xi)) % nx
    rel_y = (placing // CAP % ny + (ny - gy)) % ny
    relative = ((rel_z * nx + rel_x) * ny + rel_y) * CAP + placing % CAP
    weights_row = lax.broadcasted_iota(jnp.int32, (16, LANES), 0)
    place_row = lax.broadcasted_iota(jnp.int32, (16, HR), 0)
    place_code = jnp.where(
        place_row == 0, jnp.broadcast_to(relative // 32, (16, HR)),
        jnp.where(place_row == 1, jnp.broadcast_to(relative % 32, (16, HR)), 0),
    ).astype(F32).astype(BF16)
    place_w = jnp.where(weights_row == 0, 32.0, jnp.where(weights_row == 1, 1.0, 0.0)).astype(BF16)
    placing_col = dot_tn(place_code, place_w)
    span = min(LANES, NB * CAP)
    for m in range(NB * CAP // span):
        spot_lane = lax.broadcasted_iota(jnp.int32, (8, span), 1)
        label = spot_lane % CAP
        for j in range(span // CAP):
            dz, dx, dy = slots[m * (span // CAP) + j]
            base = ((dz * nx + dx) * ny + dy) * CAP
            label = jnp.where(spot_lane // CAP == j, label + base, label)
        label = jnp.broadcast_to(label[0:1], (HR, span)).astype(F32)
        PM[:, m * span : (m + 1) * span] = onehot(placing_col[:, :span] == label)

    w_row = lax.broadcasted_iota(jnp.int32, (2 * LANES, LANES), 0) % LANES
    w_col = lax.broadcasted_iota(jnp.int32, (2 * LANES, LANES), 1)

    def band(shift):
        at = w_row - w_col - shift
        val = jnp.where(at == 0, 27.0, jnp.where(at == -1, -27.0, 0.0))
        return (val + jnp.where(at == 1, -1.0, jnp.where(at == -2, 1.0, 0.0))).astype(BF16)

    ZW[0] = band(1)
    ZW[1] = band(0)
    f_row = lax.broadcasted_iota(jnp.int32, (16, LANES), 0) % 8
    f_lane = lax.broadcasted_iota(jnp.int32, (16, LANES), 1)
    fix_lane = jnp.where(f_row < 3, f_row, (LANES + 2) - f_row)
    fix_w = onehot((f_lane == fix_lane) & (f_row < 6))
    left_on = blk.astype(F32)
    right_on = 1.0 - left_on

    def along_z(q):
        at = pl.ds(q * PER * Y, PER * Y)
        slope = dot(SPLIT[at], ZW[0])
        flux = slope * jnp.concatenate([BZ[q * PER + i] for i in range(PER)], axis=0)
        val = dot(parts(flux), ZW[1]).reshape(PER, Y, LANES)
        for i in range(PER):
            TOT[q * PER + i] = val[i]

    def fix_z(field):
        def halo(r):
            return ZR[field, r : r + 1]

        def own(r):
            return ZS[field, r : r + 1]

        a3, a2, a1 = (halo(r) * left_on for r in range(3))
        n0, n1, n2 = (halo(r) * right_on for r in range(3))
        v0, v1, v_prev, v_last = own(3), own(4), own(5), own(6)
        at0 = ZB[0:1] * a1
        before1 = ZB[1:2] * (27.0 * (v0 - a1) - (v1 - a2))
        before2 = ZB[2:3] * (27.0 * (a1 - a2) - (v0 - a3))
        end1 = ZB[4:5] * (27.0 * (n0 - v_last) - (n1 - v_prev))
        end2 = ZB[3:4] * n0
        after = ZB[5:6] * (27.0 * (n1 - n0) - (n2 - v_last))
        rows = [
            27.0 * (at0 - before1) + before2,
            before1 - 27.0 * at0,
            at0,
            27.0 * (end1 + end2) - after,
            -27.0 * end2 - end1,
            end2,
            jnp.zeros_like(at0),
            jnp.zeros_like(at0),
        ]
        hi, lo = split2(jnp.concatenate(rows, axis=0))
        return jnp.concatenate([hi.astype(F32), lo.astype(F32)], axis=0).astype(BF16)

    def add_fix(fixes, q):
        val = dot_tn(fixes[:, q * PER * Y : (q + 1) * PER * Y], fix_w).reshape(PER, Y, LANES)
        for i in range(PER):
            TOT[q * PER + i] = TOT[q * PER + i] + val[i]

    finish(halo_b)

    inner_lane = lax.broadcasted_iota(jnp.int32, (Y, LANES), 1) < LANES - 1
    b_left = [ZR[1, r : r + 1] * left_on for r in (1, 2)]
    b_right = [ZR[1, r : r + 1] * right_on for r in (0, 1)]
    own_edge = [ZS[1, r : r + 1] for r in range(3, 7)]
    ZB[...] = FACE * jnp.concatenate(
        [
            own_edge[0] + own_edge[1],
            b_left[1] + own_edge[0],
            b_left[0] + b_left[1],
            own_edge[2] + own_edge[3],
            own_edge[3] + b_right[0],
            b_right[0] + b_right[1],
            jnp.zeros((2, cells), F32),
        ],
        axis=0,
    )

    def faces(q, _):
        for i in range(PER):
            c = q * PER + i
            BX[c] = (EB[c, 8 : 8 + Y] + EB[c + 1, 8 : 8 + Y]) * FACE
            BY[c] = (EB[c + 2, 6 : 14 + Y] + EB[c + 2, 7 : 15 + Y]) * FACE
            own_b = EB[c + 2, 8 : 8 + Y]
            BZ[c] = jnp.where(inner_lane, own_b + pltpu.roll(own_b, LANES - 1, 1), 0.0) * FACE
        return 0

    lax.fori_loop(0, X // PER, faces, 0)
    for c in range(X, X + 3):
        BX[c] = (EB[c, 8 : 8 + Y] + EB[c + 1, 8 : 8 + Y]) * FACE

    def flux_x(src, c):
        FX[c] = wide(src[c, 8 : 8 + Y], src[c + 1, 8 : 8 + Y], src[c + 2, 8 : 8 + Y], src[c + 3, 8 : 8 + Y]) * BX[c]

    def inner_x(src):
        for c in range(3, X):
            flux_x(src, c)

    def outer_x(src):
        for c in (0, 1, 2, X, X + 1, X + 2):
            flux_x(src, c)

    def across_y(src, c, i):
        FY[i] = wide(src[c + 3, 5 : 13 + Y], src[c + 3, 6 : 14 + Y], src[c + 3, 7 : 15 + Y], src[c + 3, 8 : 16 + Y]) * BY[c]
        return wide(FY[i, 0:Y], FY[i, 1 : 1 + Y], FY[i, 2 : 2 + Y], FY[i, 3 : 3 + Y])

    def laplace(c):
        return TOT[c] + wide(FX[c], FX[c + 1], FX[c + 2], FX[c + 3])

    loads[5].wait()
    loads[6].wait()
    finish(halo_p)
    inner_x(E)
    outer_x(E)
    fixes = fix_z(0)
    for q in range(X // PER):
        along_z(q)
        add_fix(fixes, q)

    def first(q, _):
        for i in range(PER):
            c = q * PER + i
            E2[c + 3, 8 : 8 + Y] = 2.0 * E[c + 3, 8 : 8 + Y] - PREV[c] + KAP[c] * (laplace(c) + across_y(E, c, i))
        return 0

    lax.fori_loop(0, X // PER, first, 0)

    drained(CA.at[pl.ds(0, G - 1)], fr_sem)
    own_tile.wait()
    keep = lax.broadcasted_iota(jnp.int32, (8, LANES), 1) == lax.broadcasted_iota(jnp.int32, (8, LANES), 0) + spot * CAP
    for k, (dz, dx, dy) in enumerate(slots):
        line = jnp.where(keep, jnp.broadcast_to(CA[dx * ny + dy, dz : dz + 1, :], (8, LANES)), 0.0)
        high = jnp.floor(line * (1.0 / 32.0))
        MC[k * 8 : k * 8 + 8, 0:LANES] = high
        MC[k * 8 : k * 8 + 8, LANES:] = line - 32.0 * high
    w_lane = jnp.where(lax.broadcasted_iota(jnp.int32, (8, 2 * LANES), 1) < LANES, 32.0, 1.0).astype(BF16)
    w_full = jnp.where(lax.broadcasted_iota(jnp.int32, (2 * LANES, LANES), 0) < LANES, 32.0, 1.0).astype(BF16)
    col_lane = dot_nt(w_lane, MC[...].astype(BF16))[0:1].astype(jnp.int32) - 1
    chunk = min(LANES, cells)

    def build_qt(m, _):
        ids = lax.broadcasted_iota(jnp.int32, (chunk, NB * CAP), 0) + m * chunk
        QT[pl.ds(m * chunk, chunk)] = onehot(ids == jnp.broadcast_to(col_lane, (chunk, NB * CAP)))
        return 0

    lax.fori_loop(0, cells // chunk, build_qt, 0)

    def build_q(dz, _):
        col_sub = dot(MC[pl.ds(dz * GS, GS)].astype(BF16), w_full) - 1.0
        for m in range(cells // chunk):
            ids = (lax.broadcasted_iota(jnp.int32, (GS, chunk), 1) + m * chunk).astype(F32)
            Q[pl.ds(dz * GS, GS), m * chunk : (m + 1) * chunk] = onehot(col_sub[:, :chunk] == ids)
        return 0

    lax.fori_loop(0, nz, build_q, 0)

    for n in range(parts_n):
        last = n == parts_n - 1
        drained(RV.at[pl.ds(0, share - 1 if last else share)], ar_sem.at[n])
        if last:
            own.wait()
        ROWS[n * share * CAP : (n + 1) * share * CAP] = parts(
            RV[n * share : (n + 1) * share].reshape(share * CAP, LANES)
        )
    halo_m = shares(E2, 2, 3)

    def middle(q):
        pushed = joined(dot(QT[q * PER * Y : (q + 1) * PER * Y], ROWS[...])).reshape(PER, Y, LANES)
        for i in range(PER):
            c = q * PER + i
            force = (GAIN * KAP[c]) * pushed[i]
            mid = E2[c + 3, 8 : 8 + Y] + force
            E2[c + 3, 8 : 8 + Y] = mid
            SPLIT[c * Y : (c + 1) * Y] = parts(mid)
            PREV[c] = force - E[c + 3, 8 : 8 + Y]

    quads = X // PER
    ends = sorted({0, quads - 1})
    inside = [q for q in range(quads) if q not in ends]
    for q in ends:
        middle(q)
    start(halo_m[0:2])
    for q in inside:
        middle(q)
    start(halo_m[2:4])
    gather_edge(2)
    start(halo_m[4:5])
    inner_x(E2)
    for q in range(quads):
        along_z(q)
    finish(halo_m[4:5])
    fixes = fix_z(2)
    for q in range(quads):
        add_fix(fixes, q)
    finish(halo_m[2:4])

    def second(q, with_y):
        for i in range(PER):
            c = q * PER + i
            total = laplace(c)
            if with_y:
                total = total + across_y(E2, c, i)
            val = 2.0 * E2[c + 3, 8 : 8 + Y] + PREV[c] + KAP[c] * total
            out_ref[c] = val
            hi, lo = split2(val)
            NEXT[c * Y : (c + 1) * Y, 0:LANES] = hi
            NEXT[c * Y : (c + 1) * Y, LANES : 2 * LANES] = lo

    for q in inside:
        second(q, True)
    for q in ends:
        for i in range(PER):
            c = q * PER + i
            TOT[c] = TOT[c] + across_y(E2, c, i)

    pieces = max(parts_n, NB * CAP // LANES)
    count = NB // pieces

    def pick(n, quad):
        at = slice(quad * PER * Y, (quad + 1) * PER * Y)
        return joined(dot(Q[n * count * CAP : (n + 1) * count * CAP, at], NEXT[at])).reshape(count, 8, LANES)

    for n in range(pieces):
        total = None
        for q in inside:
            total = pick(n, q) if total is None else total + pick(n, q)
        if total is not None:
            PK[n * count : (n + 1) * count] = total
    finish(halo_m[0:2])
    outer_x(E2)
    for q in ends:
        second(q, False)

    for n in range(pieces):
        total = None
        for q in ends:
            total = pick(n, q) if total is None else total + pick(n, q)
        if inside:
            total = total + PK[n * count : (n + 1) * count]
        PK[n * count : (n + 1) * count] = total
        for k in range(n * count, (n + 1) * count):
            dz, dx, dy = slots[k]
            if k < NB - 1:
                pltpu.make_async_remote_copy(
                    PK.at[k], RET.at[k], bs_sem, br_sem.at[group_of(k)],
                    device_id=(zb[dz] * nx + xb[dx], yb[dy], blk), device_id_type=MESH,
                ).start()
    back = pltpu.make_async_copy(PK.at[NB - 1], RET.at[NB - 1], self_sem.at[3])
    back.start()

    drained(CR.at[pl.ds(0, nz - 1)], cs_sem)
    drained(CA.at[pl.ds(0, G - 1)], fs_sem)
    drained(SB.at[pl.ds(0, NB - 1)], as_sem)
    for n in range(parts_n):
        last = n == parts_n - 1
        drained(RET.at[pl.ds(0, share - 1 if last else share)], br_sem.at[n])
        if last:
            back.wait()
        at = slice(n * share * CAP, (n + 1) * share * CAP)
        got = joined(dot(PM[:, at], parts(RET[n * share : (n + 1) * share].reshape(share * CAP, LANES))))
        hp_ref[...] = got if n == 0 else hp_ref[...] + got
    drained(PK.at[pl.ds(0, NB - 1)], bs_sem)


def keep_out(field, rows, field_out, rows_out, sem):
    copies = [
        pltpu.make_async_copy(field, field_out, sem.at[0]),
        pltpu.make_async_copy(rows, rows_out, sem.at[1]),
    ]
    for copy in copies:
        copy.start()
    for copy in copies:
        copy.wait()


def solution(mesh):
    n_gx, n_gy = mesh.shape["gx"], mesh.shape["gy"]
    dims = torus(n_gx, n_gy)
    NB = n_gx * n_gy

    def local(pressure, pressure_prev, buoyancy, kappa, hull_accel, row_block, row_column):
        X, Y, Z = pressure.shape
        HR = hull_accel.shape[0]
        any_spec = pl.BlockSpec(memory_space=pltpu.HBM)
        vmem_spec = pl.BlockSpec(memory_space=pltpu.VMEM)
        dma = pltpu.SemaphoreType.DMA
        V = pltpu.VMEM
        results = pl.pallas_call(
            functools.partial(kernel, dims),
            out_shape=(
                jax.ShapeDtypeStruct((X, Y, Z), F32),
                jax.ShapeDtypeStruct((HR, Z), F32),
            ),
            in_specs=[any_spec] * 7,
            out_specs=[vmem_spec] * 2,
            scratch_shapes=[
                V((X + 6, Y + 16, Z), F32),
                V((X + 4, Y + 16, Z), F32),
                V((X + 6, Y + 16, Z), F32),
                V((3, 8, X * Y), F32),
                V((3, 8, X * Y), F32),
                V((X * Y, 2 * Z), BF16),
                V((2, 2 * Z, Z), BF16),
                V((8, X * Y), F32),
                V((X, Y, Z), F32),
                V((X, Y, Z), F32),
                V((HR, Z), F32),
                V((X + 3, Y, Z), F32),
                V((256 // Y, Y + 8, Z), F32),
                V((X, Y, Z), F32),
                V((X + 3, Y, Z), F32),
                V((X, Y + 8, Z), F32),
                V((X, Y, Z), F32),
                V((X * Y, 2 * Z), BF16),
                V((8, Z), F32),
                V((dims[0], Z), F32),
                V((dims[1] * dims[2], dims[0], Z), F32),
                V((NB * CAP, 2 * Z), F32),
                V((NB, CAP, Z), F32),
                V((NB, CAP, Z), F32),
                V((NB * CAP, 2 * Z), BF16),
                V((NB, CAP, Z), F32),
                V((NB, CAP, Z), F32),
                V((NB * CAP, X * Y), BF16),
                V((X * Y, NB * CAP), BF16),
                V((HR, NB * CAP), BF16),
                V((1, HR), jnp.int32),
                V((1, HR), jnp.int32),
                dma((7,)), dma((3, 5)), dma((3, 5)),
                dma, dma, dma, dma, dma, dma((4,)), dma, dma((4,)), dma((4,)),
            ],
            compiler_params=pltpu.CompilerParams(collective_id=0, has_side_effects=True, vmem_limit_bytes=36 * 1024 * 1024),
            name="hull_leapfrog",
        )(
            *(pltpu.with_memory_space_constraint(v, pltpu.HBM) for v in (
                pressure, pressure_prev, buoyancy, kappa, hull_accel,
                row_block.reshape(1, HR), row_column.reshape(1, HR),
            ))
        )
        return pl.pallas_call(
            keep_out,
            out_shape=(
                jax.ShapeDtypeStruct((X, Y, Z), F32),
                jax.ShapeDtypeStruct((HR, Z), F32),
            ),
            in_specs=[vmem_spec] * 2,
            out_specs=[any_spec] * 2,
            scratch_shapes=[dma((2,))],
            compiler_params=pltpu.CompilerParams(vmem_limit_bytes=2 * 1024 * 1024),
            name="write_out",
        )(*results)

    return jax.shard_map(
        local,
        mesh=mesh,
        in_specs=(
            P("gx", "gy", "blk"),
            P("gx", "gy", "blk"),
            P("gx", "gy", "blk"),
            P("gx", "gy", "blk"),
            P(("gx", "gy", "blk"), None),
            P(("gx", "gy", "blk"), None),
            P(("gx", "gy", "blk"), None),
        ),
        out_specs=(P("gx", "gy", "blk"), P(("gx", "gy", "blk"), None)),
        check_vma=False,
    )
```

```python
import functools

import jax
import jax.numpy as jnp
from jax import lax
from jax.experimental import pallas as pl
from jax.experimental.pallas import tpu as pltpu
from jax.sharding import PartitionSpec as P

MESH = pl.DeviceIdType.MESH
F32 = jnp.float32
BF16 = jnp.bfloat16
LANES = 128
CAP = 8
COURANT = 0.05
GAIN = 0.5
FACE = COURANT * 0.5 / 576.0


def torus(n_gx, n_gy):
    nx = 4 if n_gx % 4 == 0 and n_gx > 4 else 2
    return n_gx // nx, nx, n_gy


def split2(v):
    hi = v.astype(BF16)
    lo = (v - hi.astype(F32)).astype(BF16)
    return hi, lo


def parts(v):
    hi, lo = split2(v)
    return jnp.concatenate([hi, lo], axis=1)


def joined(v):
    return v[:, :LANES] + v[:, LANES:]


def wide(a, b, c, d):
    return 27.0 * (c - b) - (d - a)


def dot(a, b):
    return jnp.dot(a, b, preferred_element_type=F32)


def dot_nt(a, b):
    return lax.dot_general(a, b, (((1,), (1,)), ((), ())), preferred_element_type=F32)


def dot_tn(a, b):
    return lax.dot_general(a, b, (((0,), (0,)), ((), ())), preferred_element_type=F32)


def onehot(mask):
    return jnp.where(mask, 1.0, 0.0).astype(BF16)


def kernel(
    dims,
    p_hbm, prev_hbm, b_hbm, kap_hbm, hull_hbm, rb_hbm, rc_hbm,
    out_ref, hp_ref,
    E, EB, E2, ZS, ZR, SPLIT, ZW, ZB, PREV, KAP, HULL, FX, FY, TOT, BX, BY, BZ, NEXT,
    CS, CR, CA, MC, SB, RV, ROWS, PK, RET, Q, QT, PM, RB, RC, RLP, RLB,
    in_sem, hs_sem, hr_sem, ls_sem, lr_sem, lf_sem, cs_sem, cr_sem, fs_sem, fr_sem, as_sem, ar_sem, bs_sem, br_sem, self_sem,
):
    nz, nx, ny = dims
    NB = nz * nx * ny
    G = nx * ny
    GS = G * CAP
    X, Y = PREV.shape[0], PREV.shape[1]
    T = Y // 8
    PER = LANES // (4 * T)
    HR = HULL.shape[0]
    cells = X * Y
    n_gx = nz * nx
    gx = lax.axis_index("gx")
    gy = lax.axis_index("gy")
    blk = lax.axis_index("blk")
    zi = gx // nx
    xi = gx % nx
    me = gx * ny + gy
    spot = xi * ny + gy

    zs = [(zi + dz) % nz for dz in range(nz)]
    xs = [(xi + dx) % nx for dx in range(nx)]
    ys = [(gy + dy) % ny for dy in range(ny)]
    zb = [(zi + nz - dz) % nz for dz in range(nz)]
    xb = [(xi + nx - dx) % nx for dx in range(nx)]
    yb = [(gy + ny - dy) % ny for dy in range(ny)]
    plane = [(dx, dy) for dx in range(nx) for dy in range(ny)]

    def hops(offset):
        return sum(min(d, n - d) for d, n in zip(offset, dims))

    slots = sorted(
        [(dz, dx, dy) for dz in range(nz) for dx, dy in plane],
        key=lambda o: (-hops(o), o[0] % 2),
    )
    parts_n = 4
    share = NB // parts_n

    def group_of(k):
        return k // share

    loads = [
        pltpu.make_async_copy(rb_hbm, RB, in_sem.at[5]),
        pltpu.make_async_copy(rc_hbm, RC, in_sem.at[6]),
        pltpu.make_async_copy(hull_hbm, HULL, in_sem.at[0]),
        pltpu.make_async_copy(p_hbm, E.at[pl.ds(3, X), pl.ds(8, Y)], in_sem.at[1]),
        pltpu.make_async_copy(b_hbm, EB.at[pl.ds(2, X), pl.ds(8, Y)], in_sem.at[2]),
        pltpu.make_async_copy(prev_hbm, PREV, in_sem.at[3]),
        pltpu.make_async_copy(kap_hbm, KAP, in_sem.at[4]),
    ]
    for load in loads:
        load.start()

    barrier = pltpu.get_barrier_semaphore()
    for dz, dx, dy in slots[:-1]:
        pl.semaphore_signal(
            barrier, inc=1, device_id=(zs[dz] * nx + xs[dx], ys[dy], blk), device_id_type=MESH
        )
    pl.semaphore_signal(barrier, inc=1, device_id=(gx, gy, 1 - blk), device_id_type=MESH)

    for ref, w in ((E, 3), (EB, 2), (E2, 3)):
        @pl.when(gx == 0)
        def _(ref=ref, w=w):
            ref[0:w] = jnp.zeros((w,) + ref.shape[1:], F32)

        @pl.when(gx == n_gx - 1)
        def _(ref=ref, w=w):
            ref[w + X :] = jnp.zeros((w,) + ref.shape[1:], F32)

        @pl.when(gy == 0)
        def _(ref=ref, w=w):
            ref[w : w + X, 0:8] = jnp.zeros((X, 8, LANES), F32)

        @pl.when(gy == ny - 1)
        def _(ref=ref, w=w):
            ref[w : w + X, 8 + Y :] = jnp.zeros((X, 8, LANES), F32)

    loads[0].wait()
    loads[1].wait()
    rb = RB[...]
    owner = onehot(jnp.broadcast_to(rb, (NB, HR)) == lax.broadcasted_iota(jnp.int32, (NB, HR), 0))
    before = onehot(
        lax.broadcasted_iota(jnp.int32, (HR, HR), 0) < lax.broadcasted_iota(jnp.int32, (HR, HR), 1)
    )
    earlier = dot(owner, before)
    slot = jnp.sum(owner.astype(F32) * earlier, axis=0, keepdims=True).astype(jnp.int32)
    placing = rb * CAP + slot
    code = RC[...] + 1
    row_z = lax.broadcasted_iota(jnp.int32, (16, HR), 0)
    which_z = jnp.broadcast_to(placing // GS, (16, HR))
    coded = jnp.where(row_z == which_z, jnp.broadcast_to(code // 32, (16, HR)), 0) + jnp.where(
        row_z == which_z + 8, jnp.broadcast_to(code % 32, (16, HR)), 0
    )
    lane_of = onehot(lax.broadcasted_iota(jnp.int32, (LANES, HR), 0) == jnp.broadcast_to(placing % GS, (LANES, HR)))
    sums = dot_nt(coded.astype(F32).astype(BF16), lane_of)
    CS[...] = sums[0:8] * 32.0 + sums[8:16]

    loads[2].wait()
    hull_parts = parts(HULL[...])

    def pack(m, _):
        rows = lax.broadcasted_iota(jnp.int32, (GS, HR), 0) + m * GS
        pt = onehot(rows == jnp.broadcast_to(placing, (GS, HR)))
        SB[pl.ds(m * G, G)] = joined(dot(pt, hull_parts)).reshape(G, 8, LANES)
        return 0

    lax.fori_loop(0, nz, pack, 0)

    e_row = lax.broadcasted_iota(jnp.int32, (8, 2 * LANES), 0)
    e_lane = lax.broadcasted_iota(jnp.int32, (8, 2 * LANES), 1) % LANES
    first_sent = jnp.broadcast_to((1 - blk) * (LANES - 3), (8, 2 * LANES))
    wanted = jnp.where(e_row < 3, first_sent + e_row, jnp.where(e_row < 5, e_row - 3, e_row + (LANES - 7)))
    edge_w = onehot((e_lane == wanted) & (e_row < 7))

    def split_planes(ref, lo, q):
        at = pl.ds(q * PER * Y, PER * Y)
        planes = [ref[q * PER + i + lo, 8 : 8 + Y] for i in range(PER)]
        SPLIT[at] = parts(jnp.concatenate(planes, axis=0))

    def gather_edge(field):
        ZS[field] = dot_nt(edge_w, SPLIT[...])

    def all_planes(ref, lo):
        def body(q, _):
            split_planes(ref, lo, q)
            return 0

        lax.fori_loop(0, X // PER, body, 0)

    loads[3].wait()
    loads[4].wait()
    all_planes(EB, 2)
    gather_edge(1)
    all_planes(E, 3)
    gather_edge(0)

    pl.semaphore_wait(barrier, NB)

    QY = Y // nx
    up_seam = (xi == nx - 1) & (zi < nz - 1)
    down_seam = (xi == 0) & (zi > 0)
    relay_up = (xi > 0) & (zi > 0)
    relay_down = (xi < nx - 1) & (zi < nz - 1)
    z_above, z_below = jnp.minimum(zi + 1, nz - 1), jnp.maximum(zi - 1, 0)

    def seams(ref, field, width, relay):
        lo = width
        copies = []
        for c in range(nx):
            band_y = pl.ds(8 + c * QY, QY)
            ends_here = c == 0
            copies.append((up_seam, pltpu.make_async_remote_copy(
                ref.at[pl.ds(X + lo - width, width), band_y],
                ref.at[pl.ds(lo - width, width), band_y] if ends_here else relay.at[0],
                ls_sem.at[field, 0, c], hr_sem.at[field, 0] if ends_here else lr_sem.at[field, 0],
                device_id=(z_above * nx + c, gy, blk), device_id_type=MESH)))
            ends_here = c == nx - 1
            copies.append((down_seam, pltpu.make_async_remote_copy(
                ref.at[pl.ds(lo, width), band_y],
                ref.at[pl.ds(X + lo, width), band_y] if ends_here else relay.at[1],
                ls_sem.at[field, 1, c], hr_sem.at[field, 1] if ends_here else lr_sem.at[field, 1],
                device_id=(z_below * nx + c, gy, blk), device_id_type=MESH)))
        band_x = pl.ds(8 + xi * QY, QY)
        onward = [
            (relay_up, 0, pltpu.make_async_remote_copy(
                relay.at[0], ref.at[pl.ds(lo - width, width), band_x],
                lf_sem.at[field, 0], hr_sem.at[field, 0],
                device_id=(zi * nx, gy, blk), device_id_type=MESH)),
            (relay_down, 1, pltpu.make_async_remote_copy(
                relay.at[1], ref.at[pl.ds(X + lo, width), band_x],
                lf_sem.at[field, 1], hr_sem.at[field, 1],
                device_id=(zi * nx + nx - 1, gy, blk), device_id_type=MESH)),
        ]

        def begin():
            for on, copy in copies:
                pl.when(on)(lambda copy=copy: copy.start())

        def forward():
            for on, way, copy in onward:
                @pl.when(on)
                def _(way=way, copy=copy):
                    drained(relay.at[way], lr_sem.at[field, way])
                    copy.start()

        def end():
            for on, copy in copies:
                pl.when(on)(lambda copy=copy: copy.wait_send())
            for on, _, copy in onward:
                pl.when(on)(lambda copy=copy: copy.wait_send())

        return begin, forward, end

    def shares(ref, field, width):
        lo = width
        send, recv = hs_sem.at[field], hr_sem.at[field]
        whole = field == 2
        return [
            (gx < n_gx - 1 if whole else xi < nx - 1, gx > 0, pltpu.make_async_remote_copy(
                ref.at[pl.ds(X + lo - width, width), pl.ds(8, Y)], ref.at[pl.ds(lo - width, width), pl.ds(8, Y)],
                send.at[0], recv.at[0], device_id=(jnp.minimum(gx + 1, n_gx - 1), gy, blk), device_id_type=MESH)),
            (gx > 0 if whole else xi > 0, gx < n_gx - 1, pltpu.make_async_remote_copy(
                ref.at[pl.ds(lo, width), pl.ds(8, Y)], ref.at[pl.ds(X + lo, width), pl.ds(8, Y)],
                send.at[1], recv.at[1], device_id=(jnp.maximum(gx - 1, 0), gy, blk), device_id_type=MESH)),
            (gy < ny - 1, gy > 0, pltpu.make_async_remote_copy(
                ref.at[pl.ds(lo, X), pl.ds(Y + 8 - width, width)], ref.at[pl.ds(lo, X), pl.ds(8 - width, width)],
                send.at[2], recv.at[2], device_id=(gx, jnp.minimum(gy + 1, ny - 1), blk), device_id_type=MESH)),
            (gy > 0, gy < ny - 1, pltpu.make_async_remote_copy(
                ref.at[pl.ds(lo, X), pl.ds(8, width)], ref.at[pl.ds(lo, X), pl.ds(8 + Y, width)],
                send.at[3], recv.at[3], device_id=(gx, jnp.maximum(gy - 1, 0), blk), device_id_type=MESH)),
            (None, None, pltpu.make_async_remote_copy(
                ZS.at[field], ZR.at[field],
                send.at[4], recv.at[4], device_id=(gx, gy, 1 - blk), device_id_type=MESH)),
        ]

    def start(copies):
        for sends, _, copy in copies:
            if sends is None:
                copy.start()
            else:
                pl.when(sends)(lambda copy=copy: copy.start())

    def finish(copies):
        for sends, gets, copy in copies:
            if sends is None:
                copy.wait_send()
                copy.wait_recv()
            else:
                pl.when(sends)(lambda copy=copy: copy.wait_send())
                pl.when(gets)(lambda copy=copy: copy.wait_recv())

    def drained(ref, sem):
        pltpu.make_async_copy(ref, ref, sem).wait()

    for dz in range(1, nz):
        pltpu.make_async_remote_copy(
            CS.at[pl.ds(zs[dz], 1)], CR.at[pl.ds(dz, 1)], cs_sem, cr_sem,
            device_id=(zs[dz] * nx + xi, gy, blk), device_id_type=MESH,
        ).start()
    own_col = pltpu.make_async_copy(CS.at[pl.ds(zi, 1)], CR.at[pl.ds(0, 1)], self_sem.at[0])
    own_col.start()

    halo_p = shares(E, 0, 3)
    halo_b = shares(EB, 1, 2)
    seam_p = seams(E, 0, 3, RLP)
    seam_b = seams(EB, 1, 2, RLB)
    seam_p[0]()
    seam_b[0]()
    start(halo_p)
    start(halo_b)

    for k, (dz, dx, dy) in enumerate(slots[:-1]):
        dest_gx = zs[dz] * nx + xs[dx]
        pltpu.make_async_remote_copy(
            SB.at[dest_gx * ny + ys[dy]], RV.at[k], as_sem, ar_sem.at[group_of(k)],
            device_id=(dest_gx, ys[dy], blk), device_id_type=MESH,
        ).start()
    own = pltpu.make_async_copy(SB.at[me], RV.at[NB - 1], self_sem.at[1])
    own.start()

    drained(CR.at[pl.ds(0, nz - 1)], cr_sem)
    own_col.wait()
    for dx, dy in plane[1:]:
        pltpu.make_async_remote_copy(
            CR, CA.at[dx * ny + dy], fs_sem, fr_sem,
            device_id=(zi * nx + xs[dx], ys[dy], blk), device_id_type=MESH,
        ).start()
    own_tile = pltpu.make_async_copy(CR, CA.at[0], self_sem.at[2])
    own_tile.start()
    seam_p[1]()
    seam_b[1]()

    rel_z = (placing // GS + (nz - zi)) % nz
    rel_x = (placing // (CAP * ny) % nx + (nx - xi)) % nx
    rel_y = (placing // CAP % ny + (ny - gy)) % ny
    relative = ((rel_z * nx + rel_x) * ny + rel_y) * CAP + placing % CAP
    weights_row = lax.broadcasted_iota(jnp.int32, (16, LANES), 0)
    place_row = lax.broadcasted_iota(jnp.int32, (16, HR), 0)
    place_code = jnp.where(
        place_row == 0, jnp.broadcast_to(relative // 32, (16, HR)),
        jnp.where(place_row == 1, jnp.broadcast_to(relative % 32, (16, HR)), 0),
    ).astype(F32).astype(BF16)
    place_w = jnp.where(weights_row == 0, 32.0, jnp.where(weights_row == 1, 1.0, 0.0)).astype(BF16)
    placing_col = dot_tn(place_code, place_w)
    span = min(LANES, NB * CAP)
    for m in range(NB * CAP // span):
        spot_lane = lax.broadcasted_iota(jnp.int32, (8, span), 1)
        label = spot_lane % CAP
        for j in range(span // CAP):
            dz, dx, dy = slots[m * (span // CAP) + j]
            base = ((dz * nx + dx) * ny + dy) * CAP
            label = jnp.where(spot_lane // CAP == j, label + base, label)
        label = jnp.broadcast_to(label[0:1], (HR, span)).astype(F32)
        PM[:, m * span : (m + 1) * span] = onehot(placing_col[:, :span] == label)

    w_row = lax.broadcasted_iota(jnp.int32, (2 * LANES, LANES), 0) % LANES
    w_col = lax.broadcasted_iota(jnp.int32, (2 * LANES, LANES), 1)

    def band(shift):
        at = w_row - w_col - shift
        val = jnp.where(at == 0, 27.0, jnp.where(at == -1, -27.0, 0.0))
        return (val + jnp.where(at == 1, -1.0, jnp.where(at == -2, 1.0, 0.0))).astype(BF16)

    ZW[0] = band(1)
    ZW[1] = band(0)
    f_row = lax.broadcasted_iota(jnp.int32, (16, LANES), 0) % 8
    f_lane = lax.broadcasted_iota(jnp.int32, (16, LANES), 1)
    fix_lane = jnp.where(f_row < 3, f_row, (LANES + 2) - f_row)
    fix_w = onehot((f_lane == fix_lane) & (f_row < 6))
    left_on = blk.astype(F32)
    right_on = 1.0 - left_on

    def along_z(q):
        at = pl.ds(q * PER * Y, PER * Y)
        slope = dot(SPLIT[at], ZW[0])
        flux = slope * jnp.concatenate([BZ[q * PER + i] for i in range(PER)], axis=0)
        val = dot(parts(flux), ZW[1]).reshape(PER, Y, LANES)
        for i in range(PER):
            TOT[q * PER + i] = val[i]

    def fix_z(field):
        def halo(r):
            return ZR[field, r : r + 1]

        def own(r):
            return ZS[field, r : r + 1]

        a3, a2, a1 = (halo(r) * left_on for r in range(3))
        n0, n1, n2 = (halo(r) * right_on for r in range(3))
        v0, v1, v_prev, v_last = own(3), own(4), own(5), own(6)
        at0 = ZB[0:1] * a1
        before1 = ZB[1:2] * (27.0 * (v0 - a1) - (v1 - a2))
        before2 = ZB[2:3] * (27.0 * (a1 - a2) - (v0 - a3))
        end1 = ZB[4:5] * (27.0 * (n0 - v_last) - (n1 - v_prev))
        end2 = ZB[3:4] * n0
        after = ZB[5:6] * (27.0 * (n1 - n0) - (n2 - v_last))
        rows = [
            27.0 * (at0 - before1) + before2,
            before1 - 27.0 * at0,
            at0,
            27.0 * (end1 + end2) - after,
            -27.0 * end2 - end1,
            end2,
            jnp.zeros_like(at0),
            jnp.zeros_like(at0),
        ]
        hi, lo = split2(jnp.concatenate(rows, axis=0))
        return jnp.concatenate([hi.astype(F32), lo.astype(F32)], axis=0).astype(BF16)

    def add_fix(fixes, q):
        val = dot_tn(fixes[:, q * PER * Y : (q + 1) * PER * Y], fix_w).reshape(PER, Y, LANES)
        for i in range(PER):
            TOT[q * PER + i] = TOT[q * PER + i] + val[i]

    finish(halo_b)

    inner_lane = lax.broadcasted_iota(jnp.int32, (Y, LANES), 1) < LANES - 1
    b_left = [ZR[1, r : r + 1] * left_on for r in (1, 2)]
    b_right = [ZR[1, r : r + 1] * right_on for r in (0, 1)]
    own_edge = [ZS[1, r : r + 1] for r in range(3, 7)]
    ZB[...] = FACE * jnp.concatenate(
        [
            own_edge[0] + own_edge[1],
            b_left[1] + own_edge[0],
            b_left[0] + b_left[1],
            own_edge[2] + own_edge[3],
            own_edge[3] + b_right[0],
            b_right[0] + b_right[1],
            jnp.zeros((2, cells), F32),
        ],
        axis=0,
    )

    def faces(q, _):
        for i in range(PER):
            c = q * PER + i
            BX[c] = (EB[c, 8 : 8 + Y] + EB[c + 1, 8 : 8 + Y]) * FACE
            BY[c] = (EB[c + 2, 6 : 14 + Y] + EB[c + 2, 7 : 15 + Y]) * FACE
            own_b = EB[c + 2, 8 : 8 + Y]
            BZ[c] = jnp.where(inner_lane, own_b + pltpu.roll(own_b, LANES - 1, 1), 0.0) * FACE
        return 0

    lax.fori_loop(0, X // PER, faces, 0)
    for c in range(X, X + 3):
        BX[c] = (EB[c, 8 : 8 + Y] + EB[c + 1, 8 : 8 + Y]) * FACE

    def flux_x(src, c):
        FX[c] = wide(src[c, 8 : 8 + Y], src[c + 1, 8 : 8 + Y], src[c + 2, 8 : 8 + Y], src[c + 3, 8 : 8 + Y]) * BX[c]

    def inner_x(src):
        for c in range(3, X):
            flux_x(src, c)

    def outer_x(src):
        for c in (0, 1, 2, X, X + 1, X + 2):
            flux_x(src, c)

    def across_y(src, c, i):
        FY[i] = wide(src[c + 3, 5 : 13 + Y], src[c + 3, 6 : 14 + Y], src[c + 3, 7 : 15 + Y], src[c + 3, 8 : 16 + Y]) * BY[c]
        return wide(FY[i, 0:Y], FY[i, 1 : 1 + Y], FY[i, 2 : 2 + Y], FY[i, 3 : 3 + Y])

    def laplace(c):
        return TOT[c] + wide(FX[c], FX[c + 1], FX[c + 2], FX[c + 3])

    loads[5].wait()
    loads[6].wait()
    finish(halo_p)
    inner_x(E)
    outer_x(E)
    fixes = fix_z(0)
    for q in range(X // PER):
        along_z(q)
        add_fix(fixes, q)

    def first(q, _):
        for i in range(PER):
            c = q * PER + i
            E2[c + 3, 8 : 8 + Y] = 2.0 * E[c + 3, 8 : 8 + Y] - PREV[c] + KAP[c] * (laplace(c) + across_y(E, c, i))
        return 0

    lax.fori_loop(0, X // PER, first, 0)

    seam_p[2]()
    seam_b[2]()

    drained(CA.at[pl.ds(0, G - 1)], fr_sem)
    own_tile.wait()
    keep = lax.broadcasted_iota(jnp.int32, (8, LANES), 1) == lax.broadcasted_iota(jnp.int32, (8, LANES), 0) + spot * CAP
    for k, (dz, dx, dy) in enumerate(slots):
        line = jnp.where(keep, jnp.broadcast_to(CA[dx * ny + dy, dz : dz + 1, :], (8, LANES)), 0.0)
        high = jnp.floor(line * (1.0 / 32.0))
        MC[k * 8 : k * 8 + 8, 0:LANES] = high
        MC[k * 8 : k * 8 + 8, LANES:] = line - 32.0 * high
    w_lane = jnp.where(lax.broadcasted_iota(jnp.int32, (8, 2 * LANES), 1) < LANES, 32.0, 1.0).astype(BF16)
    w_full = jnp.where(lax.broadcasted_iota(jnp.int32, (2 * LANES, LANES), 0) < LANES, 32.0, 1.0).astype(BF16)
    col_lane = dot_nt(w_lane, MC[...].astype(BF16))[0:1].astype(jnp.int32) - 1
    chunk = min(LANES, cells)

    def build_qt(m, _):
        ids = lax.broadcasted_iota(jnp.int32, (chunk, NB * CAP), 0) + m * chunk
        QT[pl.ds(m * chunk, chunk)] = onehot(ids == jnp.broadcast_to(col_lane, (chunk, NB * CAP)))
        return 0

    lax.fori_loop(0, cells // chunk, build_qt, 0)

    def build_q(dz, _):
        col_sub = dot(MC[pl.ds(dz * GS, GS)].astype(BF16), w_full) - 1.0
        for m in range(cells // chunk):
            ids = (lax.broadcasted_iota(jnp.int32, (GS, chunk), 1) + m * chunk).astype(F32)
            Q[pl.ds(dz * GS, GS), m * chunk : (m + 1) * chunk] = onehot(col_sub[:, :chunk] == ids)
        return 0

    lax.fori_loop(0, nz, build_q, 0)

    for n in range(parts_n):
        last = n == parts_n - 1
        drained(RV.at[pl.ds(0, share - 1 if last else share)], ar_sem.at[n])
        if last:
            own.wait()
        ROWS[n * share * CAP : (n + 1) * share * CAP] = parts(
            RV[n * share : (n + 1) * share].reshape(share * CAP, LANES)
        )
    halo_m = shares(E2, 2, 3)

    def middle(q):
        pushed = joined(dot(QT[q * PER * Y : (q + 1) * PER * Y], ROWS[...])).reshape(PER, Y, LANES)
        for i in range(PER):
            c = q * PER + i
            force = (GAIN * KAP[c]) * pushed[i]
            mid = E2[c + 3, 8 : 8 + Y] + force
            E2[c + 3, 8 : 8 + Y] = mid
            SPLIT[c * Y : (c + 1) * Y] = parts(mid)
            PREV[c] = force - E[c + 3, 8 : 8 + Y]

    quads = X // PER
    ends = sorted({0, quads - 1})
    inside = [q for q in range(quads) if q not in ends]
    for q in ends:
        middle(q)
    start(halo_m[0:2])
    for q in inside:
        middle(q)
    start(halo_m[2:4])
    gather_edge(2)
    start(halo_m[4:5])
    inner_x(E2)
    for q in range(quads):
        along_z(q)
    finish(halo_m[4:5])
    fixes = fix_z(2)
    for q in range(quads):
        add_fix(fixes, q)
    finish(halo_m[2:4])

    def second(q, with_y):
        for i in range(PER):
            c = q * PER + i
            total = laplace(c)
            if with_y:
                total = total + across_y(E2, c, i)
            val = 2.0 * E2[c + 3, 8 : 8 + Y] + PREV[c] + KAP[c] * total
            out_ref[c] = val
            hi, lo = split2(val)
            NEXT[c * Y : (c + 1) * Y, 0:LANES] = hi
            NEXT[c * Y : (c + 1) * Y, LANES : 2 * LANES] = lo

    for q in inside:
        second(q, True)
    for q in ends:
        for i in range(PER):
            c = q * PER + i
            TOT[c] = TOT[c] + across_y(E2, c, i)

    pieces = max(parts_n, NB * CAP // LANES)
    count = NB // pieces

    def pick(n, quad):
        at = slice(quad * PER * Y, (quad + 1) * PER * Y)
        return joined(dot(Q[n * count * CAP : (n + 1) * count * CAP, at], NEXT[at])).reshape(count, 8, LANES)

    for n in range(pieces):
        total = None
        for q in inside:
            total = pick(n, q) if total is None else total + pick(n, q)
        if total is not None:
            PK[n * count : (n + 1) * count] = total
    finish(halo_m[0:2])
    outer_x(E2)
    for q in ends:
        second(q, False)

    for n in range(pieces):
        total = None
        for q in ends:
            total = pick(n, q) if total is None else total + pick(n, q)
        if inside:
            total = total + PK[n * count : (n + 1) * count]
        PK[n * count : (n + 1) * count] = total
        for k in range(n * count, (n + 1) * count):
            dz, dx, dy = slots[k]
            if k < NB - 1:
                pltpu.make_async_remote_copy(
                    PK.at[k], RET.at[k], bs_sem, br_sem.at[group_of(k)],
                    device_id=(zb[dz] * nx + xb[dx], yb[dy], blk), device_id_type=MESH,
                ).start()
    back = pltpu.make_async_copy(PK.at[NB - 1], RET.at[NB - 1], self_sem.at[3])
    back.start()

    drained(CR.at[pl.ds(0, nz - 1)], cs_sem)
    drained(CA.at[pl.ds(0, G - 1)], fs_sem)
    drained(SB.at[pl.ds(0, NB - 1)], as_sem)
    for n in range(parts_n):
        last = n == parts_n - 1
        drained(RET.at[pl.ds(0, share - 1 if last else share)], br_sem.at[n])
        if last:
            back.wait()
        at = slice(n * share * CAP, (n + 1) * share * CAP)
        got = joined(dot(PM[:, at], parts(RET[n * share : (n + 1) * share].reshape(share * CAP, LANES))))
        hp_ref[...] = got if n == 0 else hp_ref[...] + got
    drained(PK.at[pl.ds(0, NB - 1)], bs_sem)


def keep_out(field, rows, field_out, rows_out, sem):
    copies = [
        pltpu.make_async_copy(field, field_out, sem.at[0]),
        pltpu.make_async_copy(rows, rows_out, sem.at[1]),
    ]
    for copy in copies:
        copy.start()
    for copy in copies:
        copy.wait()


def solution(mesh):
    n_gx, n_gy = mesh.shape["gx"], mesh.shape["gy"]
    dims = torus(n_gx, n_gy)
    NB = n_gx * n_gy

    def local(pressure, pressure_prev, buoyancy, kappa, hull_accel, row_block, row_column):
        X, Y, Z = pressure.shape
        HR = hull_accel.shape[0]
        any_spec = pl.BlockSpec(memory_space=pltpu.HBM)
        vmem_spec = pl.BlockSpec(memory_space=pltpu.VMEM)
        dma = pltpu.SemaphoreType.DMA
        V = pltpu.VMEM
        results = pl.pallas_call(
            functools.partial(kernel, dims),
            out_shape=(
                jax.ShapeDtypeStruct((X, Y, Z), F32),
                jax.ShapeDtypeStruct((HR, Z), F32),
            ),
            in_specs=[any_spec] * 7,
            out_specs=[vmem_spec] * 2,
            scratch_shapes=[
                V((X + 6, Y + 16, Z), F32),
                V((X + 4, Y + 16, Z), F32),
                V((X + 6, Y + 16, Z), F32),
                V((3, 8, X * Y), F32),
                V((3, 8, X * Y), F32),
                V((X * Y, 2 * Z), BF16),
                V((2, 2 * Z, Z), BF16),
                V((8, X * Y), F32),
                V((X, Y, Z), F32),
                V((X, Y, Z), F32),
                V((HR, Z), F32),
                V((X + 3, Y, Z), F32),
                V((256 // Y, Y + 8, Z), F32),
                V((X, Y, Z), F32),
                V((X + 3, Y, Z), F32),
                V((X, Y + 8, Z), F32),
                V((X, Y, Z), F32),
                V((X * Y, 2 * Z), BF16),
                V((8, Z), F32),
                V((dims[0], Z), F32),
                V((dims[1] * dims[2], dims[0], Z), F32),
                V((NB * CAP, 2 * Z), F32),
                V((NB, CAP, Z), F32),
                V((NB, CAP, Z), F32),
                V((NB * CAP, 2 * Z), BF16),
                V((NB, CAP, Z), F32),
                V((NB, CAP, Z), F32),
                V((NB * CAP, X * Y), BF16),
                V((X * Y, NB * CAP), BF16),
                V((HR, NB * CAP), BF16),
                V((1, HR), jnp.int32),
                V((1, HR), jnp.int32),
                V((2, 3, Y // dims[1], Z), F32),
                V((2, 2, Y // dims[1], Z), F32),
                dma((7,)), dma((3, 5)), dma((3, 5)), dma((2, 2, dims[1])), dma((2, 2)), dma((2, 2)),
                dma, dma, dma, dma, dma, dma((4,)), dma, dma((4,)), dma((4,)),
            ],
            compiler_params=pltpu.CompilerParams(collective_id=0, has_side_effects=True, vmem_limit_bytes=36 * 1024 * 1024),
            name="hull_leapfrog",
        )(
            *(pltpu.with_memory_space_constraint(v, pltpu.HBM) for v in (
                pressure, pressure_prev, buoyancy, kappa, hull_accel,
                row_block.reshape(1, HR), row_column.reshape(1, HR),
            ))
        )
        return pl.pallas_call(
            keep_out,
            out_shape=(
                jax.ShapeDtypeStruct((X, Y, Z), F32),
                jax.ShapeDtypeStruct((HR, Z), F32),
            ),
            in_specs=[vmem_spec] * 2,
            out_specs=[any_spec] * 2,
            scratch_shapes=[dma((2,))],
            compiler_params=pltpu.CompilerParams(vmem_limit_bytes=2 * 1024 * 1024),
            name="write_out",
        )(*results)

    return jax.shard_map(
        local,
        mesh=mesh,
        in_specs=(
            P("gx", "gy", "blk"),
            P("gx", "gy", "blk"),
            P("gx", "gy", "blk"),
            P("gx", "gy", "blk"),
            P(("gx", "gy", "blk"), None),
            P(("gx", "gy", "blk"), None),
            P(("gx", "gy", "blk"), None),
        ),
        out_specs=(P("gx", "gy", "blk"), P(("gx", "gy", "blk"), None)),
        check_vma=False,
    )
```

```python
import functools

import jax
import jax.numpy as jnp
from jax import lax
from jax.experimental import pallas as pl
from jax.experimental.pallas import tpu as pltpu
from jax.sharding import PartitionSpec as P

MESH = pl.DeviceIdType.MESH
F32 = jnp.float32
BF16 = jnp.bfloat16
LANES = 128
CAP = 8
COURANT = 0.05
GAIN = 0.5
FACE = COURANT * 0.5 / 576.0


def torus(n_gx, n_gy):
    nx = 4 if n_gx % 4 == 0 and n_gx > 4 else 2
    return n_gx // nx, nx, n_gy


def split2(v):
    hi = v.astype(BF16)
    lo = (v - hi.astype(F32)).astype(BF16)
    return hi, lo


def parts(v):
    hi, lo = split2(v)
    return jnp.concatenate([hi, lo], axis=1)


def joined(v):
    return v[:, :LANES] + v[:, LANES:]


def wide(a, b, c, d):
    return 27.0 * (c - b) - (d - a)


def dot(a, b):
    return jnp.dot(a, b, preferred_element_type=F32)


def dot_nt(a, b):
    return lax.dot_general(a, b, (((1,), (1,)), ((), ())), preferred_element_type=F32)


def dot_tn(a, b):
    return lax.dot_general(a, b, (((0,), (0,)), ((), ())), preferred_element_type=F32)


def onehot(mask):
    return jnp.where(mask, 1.0, 0.0).astype(BF16)


def kernel(
    dims,
    p_hbm, prev_hbm, b_hbm, kap_hbm, hull_hbm, rb_hbm, rc_hbm,
    out_ref, hp_ref,
    E, EB, E2, ZS, ZR, SPLIT, ZW, ZB, PREV, KAP, HULL, FX, FY, TOT, BX, BY, BZ, NEXT,
    CS, CR, CA, MC, SB, RV, ROWS, PK, RET, Q, QT, PM, RB, RC, RLP, RLB,
    in_sem, hs_sem, hr_sem, ls_sem, lr_sem, lf_sem, cs_sem, cr_sem, fs_sem, fr_sem, as_sem, ar_sem, bs_sem, br_sem, self_sem,
):
    nz, nx, ny = dims
    NB = nz * nx * ny
    G = nx * ny
    GS = G * CAP
    X, Y = PREV.shape[0], PREV.shape[1]
    T = Y // 8
    PER = LANES // (4 * T)
    HR = HULL.shape[0]
    cells = X * Y
    n_gx = nz * nx
    gx = lax.axis_index("gx")
    gy = lax.axis_index("gy")
    blk = lax.axis_index("blk")
    zi = gx // nx
    xi = gx % nx
    me = gx * ny + gy
    spot = xi * ny + gy

    zs = [(zi + dz) % nz for dz in range(nz)]
    xs = [(xi + dx) % nx for dx in range(nx)]
    ys = [(gy + dy) % ny for dy in range(ny)]
    zb = [(zi + nz - dz) % nz for dz in range(nz)]
    xb = [(xi + nx - dx) % nx for dx in range(nx)]
    yb = [(gy + ny - dy) % ny for dy in range(ny)]
    plane = [(dx, dy) for dx in range(nx) for dy in range(ny)]

    def hops(offset):
        return sum(min(d, n - d) for d, n in zip(offset, dims))

    slots = sorted(
        [(dz, dx, dy) for dz in range(nz) for dx, dy in plane],
        key=lambda o: (-hops(o), o[0] % 2),
    )
    parts_n = 4
    share = NB // parts_n

    def group_of(k):
        return k // share

    loads = [
        pltpu.make_async_copy(rb_hbm, RB, in_sem.at[5]),
        pltpu.make_async_copy(rc_hbm, RC, in_sem.at[6]),
        pltpu.make_async_copy(hull_hbm, HULL, in_sem.at[0]),
        pltpu.make_async_copy(p_hbm, E.at[pl.ds(3, X), pl.ds(8, Y)], in_sem.at[1]),
        pltpu.make_async_copy(b_hbm, EB.at[pl.ds(2, X), pl.ds(8, Y)], in_sem.at[2]),
        pltpu.make_async_copy(prev_hbm, PREV, in_sem.at[3]),
        pltpu.make_async_copy(kap_hbm, KAP, in_sem.at[4]),
    ]
    for load in loads:
        load.start()

    barrier = pltpu.get_barrier_semaphore()
    for dz, dx, dy in slots[:-1]:
        pl.semaphore_signal(
            barrier, inc=1, device_id=(zs[dz] * nx + xs[dx], ys[dy], blk), device_id_type=MESH
        )
    pl.semaphore_signal(barrier, inc=1, device_id=(gx, gy, 1 - blk), device_id_type=MESH)

    for ref, w in ((E, 3), (EB, 2), (E2, 3)):
        @pl.when(gx == 0)
        def _(ref=ref, w=w):
            ref[0:w] = jnp.zeros((w,) + ref.shape[1:], F32)

        @pl.when(gx == n_gx - 1)
        def _(ref=ref, w=w):
            ref[w + X :] = jnp.zeros((w,) + ref.shape[1:], F32)

        @pl.when(gy == 0)
        def _(ref=ref, w=w):
            ref[w : w + X, 0:8] = jnp.zeros((X, 8, LANES), F32)

        @pl.when(gy == ny - 1)
        def _(ref=ref, w=w):
            ref[w : w + X, 8 + Y :] = jnp.zeros((X, 8, LANES), F32)

    loads[0].wait()
    loads[1].wait()
    rb = RB[...]
    owner = onehot(jnp.broadcast_to(rb, (NB, HR)) == lax.broadcasted_iota(jnp.int32, (NB, HR), 0))
    before = onehot(
        lax.broadcasted_iota(jnp.int32, (HR, HR), 0) < lax.broadcasted_iota(jnp.int32, (HR, HR), 1)
    )
    earlier = dot(owner, before)
    slot = jnp.sum(owner.astype(F32) * earlier, axis=0, keepdims=True).astype(jnp.int32)
    placing = rb * CAP + slot
    code = RC[...] + 1
    row_z = lax.broadcasted_iota(jnp.int32, (16, HR), 0)
    which_z = jnp.broadcast_to(placing // GS, (16, HR))
    coded = jnp.where(row_z == which_z, jnp.broadcast_to(code // 32, (16, HR)), 0) + jnp.where(
        row_z == which_z + 8, jnp.broadcast_to(code % 32, (16, HR)), 0
    )
    lane_of = onehot(lax.broadcasted_iota(jnp.int32, (LANES, HR), 0) == jnp.broadcast_to(placing % GS, (LANES, HR)))
    sums = dot_nt(coded.astype(F32).astype(BF16), lane_of)
    CS[...] = sums[0:8] * 32.0 + sums[8:16]

    loads[2].wait()
    hull_parts = parts(HULL[...])

    def pack(m, _):
        rows = lax.broadcasted_iota(jnp.int32, (GS, HR), 0) + m * GS
        pt = onehot(rows == jnp.broadcast_to(placing, (GS, HR)))
        SB[pl.ds(m * G, G)] = joined(dot(pt, hull_parts)).reshape(G, 8, LANES)
        return 0

    lax.fori_loop(0, nz, pack, 0)

    e_row = lax.broadcasted_iota(jnp.int32, (8, 2 * LANES), 0)
    e_lane = lax.broadcasted_iota(jnp.int32, (8, 2 * LANES), 1) % LANES
    first_sent = jnp.broadcast_to((1 - blk) * (LANES - 3), (8, 2 * LANES))
    wanted = jnp.where(e_row < 3, first_sent + e_row, jnp.where(e_row < 5, e_row - 3, e_row + (LANES - 7)))
    edge_w = onehot((e_lane == wanted) & (e_row < 7))

    def split_planes(ref, lo, q):
        at = pl.ds(q * PER * Y, PER * Y)
        planes = [ref[q * PER + i + lo, 8 : 8 + Y] for i in range(PER)]
        SPLIT[at] = parts(jnp.concatenate(planes, axis=0))

    def gather_edge(field):
        ZS[field] = dot_nt(edge_w, SPLIT[...])

    def all_planes(ref, lo):
        def body(q, _):
            split_planes(ref, lo, q)
            return 0

        lax.fori_loop(0, X // PER, body, 0)

    loads[3].wait()
    loads[4].wait()
    all_planes(EB, 2)
    gather_edge(1)
    all_planes(E, 3)
    gather_edge(0)

    rel_z = (placing // GS + (nz - zi)) % nz
    rel_x = (placing // (CAP * ny) % nx + (nx - xi)) % nx
    rel_y = (placing // CAP % ny + (ny - gy)) % ny
    relative = ((rel_z * nx + rel_x) * ny + rel_y) * CAP + placing % CAP
    weights_row = lax.broadcasted_iota(jnp.int32, (16, LANES), 0)
    place_row = lax.broadcasted_iota(jnp.int32, (16, HR), 0)
    place_code = jnp.where(
        place_row == 0, jnp.broadcast_to(relative // 32, (16, HR)),
        jnp.where(place_row == 1, jnp.broadcast_to(relative % 32, (16, HR)), 0),
    ).astype(F32).astype(BF16)
    place_w = jnp.where(weights_row == 0, 32.0, jnp.where(weights_row == 1, 1.0, 0.0)).astype(BF16)
    placing_col = dot_tn(place_code, place_w)
    span = min(LANES, NB * CAP)
    for m in range(NB * CAP // span):
        spot_lane = lax.broadcasted_iota(jnp.int32, (8, span), 1)
        label = spot_lane % CAP
        for j in range(span // CAP):
            dz, dx, dy = slots[m * (span // CAP) + j]
            base = ((dz * nx + dx) * ny + dy) * CAP
            label = jnp.where(spot_lane // CAP == j, label + base, label)
        label = jnp.broadcast_to(label[0:1], (HR, span)).astype(F32)
        PM[:, m * span : (m + 1) * span] = onehot(placing_col[:, :span] == label)

    pl.semaphore_wait(barrier, NB)

    QY = Y // nx
    up_seam = (xi == nx - 1) & (zi < nz - 1)
    down_seam = (xi == 0) & (zi > 0)
    relay_up = (xi > 0) & (zi > 0)
    relay_down = (xi < nx - 1) & (zi < nz - 1)
    z_above, z_below = jnp.minimum(zi + 1, nz - 1), jnp.maximum(zi - 1, 0)

    def seams(ref, field, width, relay):
        lo = width
        copies = []
        for c in range(nx):
            band_y = pl.ds(8 + c * QY, QY)
            ends_here = c == 0
            copies.append((up_seam, pltpu.make_async_remote_copy(
                ref.at[pl.ds(X + lo - width, width), band_y],
                ref.at[pl.ds(lo - width, width), band_y] if ends_here else relay.at[0],
                ls_sem.at[field, 0, c], hr_sem.at[field, 0] if ends_here else lr_sem.at[field, 0],
                device_id=(z_above * nx + c, gy, blk), device_id_type=MESH)))
            ends_here = c == nx - 1
            copies.append((down_seam, pltpu.make_async_remote_copy(
                ref.at[pl.ds(lo, width), band_y],
                ref.at[pl.ds(X + lo, width), band_y] if ends_here else relay.at[1],
                ls_sem.at[field, 1, c], hr_sem.at[field, 1] if ends_here else lr_sem.at[field, 1],
                device_id=(z_below * nx + c, gy, blk), device_id_type=MESH)))
        band_x = pl.ds(8 + xi * QY, QY)
        onward = [
            (relay_up, 0, pltpu.make_async_remote_copy(
                relay.at[0], ref.at[pl.ds(lo - width, width), band_x],
                lf_sem.at[field, 0], hr_sem.at[field, 0],
                device_id=(zi * nx, gy, blk), device_id_type=MESH)),
            (relay_down, 1, pltpu.make_async_remote_copy(
                relay.at[1], ref.at[pl.ds(X + lo, width), band_x],
                lf_sem.at[field, 1], hr_sem.at[field, 1],
                device_id=(zi * nx + nx - 1, gy, blk), device_id_type=MESH)),
        ]

        def begin():
            for on, copy in copies:
                pl.when(on)(lambda copy=copy: copy.start())

        def forward():
            for on, way, copy in onward:
                @pl.when(on)
                def _(way=way, copy=copy):
                    drained(relay.at[way], lr_sem.at[field, way])
                    copy.start()

        def end():
            for on, copy in copies:
                pl.when(on)(lambda copy=copy: copy.wait_send())
            for on, _, copy in onward:
                pl.when(on)(lambda copy=copy: copy.wait_send())

        return begin, forward, end

    def shares(ref, field, width):
        lo = width
        send, recv = hs_sem.at[field], hr_sem.at[field]
        whole = field == 2
        return [
            (gx < n_gx - 1 if whole else xi < nx - 1, gx > 0, pltpu.make_async_remote_copy(
                ref.at[pl.ds(X + lo - width, width), pl.ds(8, Y)], ref.at[pl.ds(lo - width, width), pl.ds(8, Y)],
                send.at[0], recv.at[0], device_id=(jnp.minimum(gx + 1, n_gx - 1), gy, blk), device_id_type=MESH)),
            (gx > 0 if whole else xi > 0, gx < n_gx - 1, pltpu.make_async_remote_copy(
                ref.at[pl.ds(lo, width), pl.ds(8, Y)], ref.at[pl.ds(X + lo, width), pl.ds(8, Y)],
                send.at[1], recv.at[1], device_id=(jnp.maximum(gx - 1, 0), gy, blk), device_id_type=MESH)),
            (gy < ny - 1, gy > 0, pltpu.make_async_remote_copy(
                ref.at[pl.ds(lo, X), pl.ds(Y + 8 - width, width)], ref.at[pl.ds(lo, X), pl.ds(8 - width, width)],
                send.at[2], recv.at[2], device_id=(gx, jnp.minimum(gy + 1, ny - 1), blk), device_id_type=MESH)),
            (gy > 0, gy < ny - 1, pltpu.make_async_remote_copy(
                ref.at[pl.ds(lo, X), pl.ds(8, width)], ref.at[pl.ds(lo, X), pl.ds(8 + Y, width)],
                send.at[3], recv.at[3], device_id=(gx, jnp.maximum(gy - 1, 0), blk), device_id_type=MESH)),
            (None, None, pltpu.make_async_remote_copy(
                ZS.at[field], ZR.at[field],
                send.at[4], recv.at[4], device_id=(gx, gy, 1 - blk), device_id_type=MESH)),
        ]

    def start(copies):
        for sends, _, copy in copies:
            if sends is None:
                copy.start()
            else:
                pl.when(sends)(lambda copy=copy: copy.start())

    def finish(copies):
        for sends, gets, copy in copies:
            if sends is None:
                copy.wait_send()
                copy.wait_recv()
            else:
                pl.when(sends)(lambda copy=copy: copy.wait_send())
                pl.when(gets)(lambda copy=copy: copy.wait_recv())

    def drained(ref, sem):
        pltpu.make_async_copy(ref, ref, sem).wait()

    for dz in range(1, nz):
        pltpu.make_async_remote_copy(
            CS.at[pl.ds(zs[dz], 1)], CR.at[pl.ds(dz, 1)], cs_sem, cr_sem,
            device_id=(zs[dz] * nx + xi, gy, blk), device_id_type=MESH,
        ).start()
    own_col = pltpu.make_async_copy(CS.at[pl.ds(zi, 1)], CR.at[pl.ds(0, 1)], self_sem.at[0])
    own_col.start()

    halo_p = shares(E, 0, 3)
    halo_b = shares(EB, 1, 2)
    seam_p = seams(E, 0, 3, RLP)
    seam_b = seams(EB, 1, 2, RLB)
    seam_p[0]()
    seam_b[0]()
    start(halo_p)
    start(halo_b)

    for k, (dz, dx, dy) in enumerate(slots[:-1]):
        dest_gx = zs[dz] * nx + xs[dx]
        pltpu.make_async_remote_copy(
            SB.at[dest_gx * ny + ys[dy]], RV.at[k], as_sem, ar_sem.at[group_of(k)],
            device_id=(dest_gx, ys[dy], blk), device_id_type=MESH,
        ).start()
    own = pltpu.make_async_copy(SB.at[me], RV.at[NB - 1], self_sem.at[1])
    own.start()

    w_row = lax.broadcasted_iota(jnp.int32, (2 * LANES, LANES), 0) % LANES
    w_col = lax.broadcasted_iota(jnp.int32, (2 * LANES, LANES), 1)

    def band(shift):
        at = w_row - w_col - shift
        val = jnp.where(at == 0, 27.0, jnp.where(at == -1, -27.0, 0.0))
        return (val + jnp.where(at == 1, -1.0, jnp.where(at == -2, 1.0, 0.0))).astype(BF16)

    ZW[0] = band(1)
    ZW[1] = band(0)
    f_row = lax.broadcasted_iota(jnp.int32, (16, LANES), 0) % 8
    f_lane = lax.broadcasted_iota(jnp.int32, (16, LANES), 1)
    fix_lane = jnp.where(f_row < 3, f_row, (LANES + 2) - f_row)
    fix_w = onehot((f_lane == fix_lane) & (f_row < 6))
    left_on = blk.astype(F32)
    right_on = 1.0 - left_on

    def along_z(q):
        at = pl.ds(q * PER * Y, PER * Y)
        slope = dot(SPLIT[at], ZW[0])
        flux = slope * jnp.concatenate([BZ[q * PER + i] for i in range(PER)], axis=0)
        val = dot(parts(flux), ZW[1]).reshape(PER, Y, LANES)
        for i in range(PER):
            TOT[q * PER + i] = val[i]

    def fix_z(field):
        def halo(r):
            return ZR[field, r : r + 1]

        def own(r):
            return ZS[field, r : r + 1]

        a3, a2, a1 = (halo(r) * left_on for r in range(3))
        n0, n1, n2 = (halo(r) * right_on for r in range(3))
        v0, v1, v_prev, v_last = own(3), own(4), own(5), own(6)
        at0 = ZB[0:1] * a1
        before1 = ZB[1:2] * (27.0 * (v0 - a1) - (v1 - a2))
        before2 = ZB[2:3] * (27.0 * (a1 - a2) - (v0 - a3))
        end1 = ZB[4:5] * (27.0 * (n0 - v_last) - (n1 - v_prev))
        end2 = ZB[3:4] * n0
        after = ZB[5:6] * (27.0 * (n1 - n0) - (n2 - v_last))
        rows = [
            27.0 * (at0 - before1) + before2,
            before1 - 27.0 * at0,
            at0,
            27.0 * (end1 + end2) - after,
            -27.0 * end2 - end1,
            end2,
            jnp.zeros_like(at0),
            jnp.zeros_like(at0),
        ]
        hi, lo = split2(jnp.concatenate(rows, axis=0))
        return jnp.concatenate([hi.astype(F32), lo.astype(F32)], axis=0).astype(BF16)

    def add_fix(fixes, q):
        val = dot_tn(fixes[:, q * PER * Y : (q + 1) * PER * Y], fix_w).reshape(PER, Y, LANES)
        for i in range(PER):
            TOT[q * PER + i] = TOT[q * PER + i] + val[i]

    inner_lane = lax.broadcasted_iota(jnp.int32, (Y, LANES), 1) < LANES - 1

    def face_x(c):
        BX[c] = (EB[c, 8 : 8 + Y] + EB[c + 1, 8 : 8 + Y]) * FACE

    def own_faces(q, _):
        for i in range(PER):
            c = q * PER + i
            own_b = EB[c + 2, 8 : 8 + Y]
            BZ[c] = jnp.where(inner_lane, own_b + pltpu.roll(own_b, LANES - 1, 1), 0.0) * FACE
        return 0

    def flux_x(src, c):
        FX[c] = wide(src[c, 8 : 8 + Y], src[c + 1, 8 : 8 + Y], src[c + 2, 8 : 8 + Y], src[c + 3, 8 : 8 + Y]) * BX[c]

    def inner_x(src):
        for c in range(3, X):
            flux_x(src, c)

    def outer_x(src):
        for c in (0, 1, 2, X, X + 1, X + 2):
            flux_x(src, c)

    def across_y(src, c, i):
        FY[i] = wide(src[c + 3, 5 : 13 + Y], src[c + 3, 6 : 14 + Y], src[c + 3, 7 : 15 + Y], src[c + 3, 8 : 16 + Y]) * BY[c]
        return wide(FY[i, 0:Y], FY[i, 1 : 1 + Y], FY[i, 2 : 2 + Y], FY[i, 3 : 3 + Y])

    lax.fori_loop(0, X // PER, own_faces, 0)
    for c in range(3, X):
        face_x(c)
    inner_x(E)
    for q in range(X // PER):
        along_z(q)

    drained(CR.at[pl.ds(0, nz - 1)], cr_sem)
    own_col.wait()
    for dx, dy in plane[1:]:
        pltpu.make_async_remote_copy(
            CR, CA.at[dx * ny + dy], fs_sem, fr_sem,
            device_id=(zi * nx + xs[dx], ys[dy], blk), device_id_type=MESH,
        ).start()
    own_tile = pltpu.make_async_copy(CR, CA.at[0], self_sem.at[2])
    own_tile.start()
    seam_p[1]()
    seam_b[1]()

    finish(halo_b)
    b_left = [ZR[1, r : r + 1] * left_on for r in (1, 2)]
    b_right = [ZR[1, r : r + 1] * right_on for r in (0, 1)]
    own_edge = [ZS[1, r : r + 1] for r in range(3, 7)]
    ZB[...] = FACE * jnp.concatenate(
        [
            own_edge[0] + own_edge[1],
            b_left[1] + own_edge[0],
            b_left[0] + b_left[1],
            own_edge[2] + own_edge[3],
            own_edge[3] + b_right[0],
            b_right[0] + b_right[1],
            jnp.zeros((2, cells), F32),
        ],
        axis=0,
    )
    for c in (0, 1, 2, X, X + 1, X + 2):
        face_x(c)

    def faces_y(q, _):
        for i in range(PER):
            c = q * PER + i
            BY[c] = (EB[c + 2, 6 : 14 + Y] + EB[c + 2, 7 : 15 + Y]) * FACE
        return 0

    lax.fori_loop(0, X // PER, faces_y, 0)

    def laplace(c):
        return TOT[c] + wide(FX[c], FX[c + 1], FX[c + 2], FX[c + 3])

    loads[5].wait()
    loads[6].wait()
    finish(halo_p)
    outer_x(E)
    fixes = fix_z(0)
    for q in range(X // PER):
        add_fix(fixes, q)

    def first(q, _):
        for i in range(PER):
            c = q * PER + i
            E2[c + 3, 8 : 8 + Y] = 2.0 * E[c + 3, 8 : 8 + Y] - PREV[c] + KAP[c] * (laplace(c) + across_y(E, c, i))
        return 0

    lax.fori_loop(0, X // PER, first, 0)

    seam_p[2]()
    seam_b[2]()

    drained(CA.at[pl.ds(0, G - 1)], fr_sem)
    own_tile.wait()
    keep = lax.broadcasted_iota(jnp.int32, (8, LANES), 1) == lax.broadcasted_iota(jnp.int32, (8, LANES), 0) + spot * CAP
    for k, (dz, dx, dy) in enumerate(slots):
        line = jnp.where(keep, jnp.broadcast_to(CA[dx * ny + dy, dz : dz + 1, :], (8, LANES)), 0.0)
        high = jnp.floor(line * (1.0 / 32.0))
        MC[k * 8 : k * 8 + 8, 0:LANES] = high
        MC[k * 8 : k * 8 + 8, LANES:] = line - 32.0 * high
    w_lane = jnp.where(lax.broadcasted_iota(jnp.int32, (8, 2 * LANES), 1) < LANES, 32.0, 1.0).astype(BF16)
    w_full = jnp.where(lax.broadcasted_iota(jnp.int32, (2 * LANES, LANES), 0) < LANES, 32.0, 1.0).astype(BF16)
    col_lane = dot_nt(w_lane, MC[...].astype(BF16))[0:1].astype(jnp.int32) - 1
    chunk = min(LANES, cells)

    def build_qt(m, _):
        ids = lax.broadcasted_iota(jnp.int32, (chunk, NB * CAP), 0) + m * chunk
        QT[pl.ds(m * chunk, chunk)] = onehot(ids == jnp.broadcast_to(col_lane, (chunk, NB * CAP)))
        return 0

    lax.fori_loop(0, cells // chunk, build_qt, 0)

    def build_q(dz, _):
        col_sub = dot(MC[pl.ds(dz * GS, GS)].astype(BF16), w_full) - 1.0
        for m in range(cells // chunk):
            ids = (lax.broadcasted_iota(jnp.int32, (GS, chunk), 1) + m * chunk).astype(F32)
            Q[pl.ds(dz * GS, GS), m * chunk : (m + 1) * chunk] = onehot(col_sub[:, :chunk] == ids)
        return 0

    lax.fori_loop(0, nz, build_q, 0)

    for n in range(parts_n):
        last = n == parts_n - 1
        drained(RV.at[pl.ds(0, share - 1 if last else share)], ar_sem.at[n])
        if last:
            own.wait()
        ROWS[n * share * CAP : (n + 1) * share * CAP] = parts(
            RV[n * share : (n + 1) * share].reshape(share * CAP, LANES)
        )
    halo_m = shares(E2, 2, 3)

    def middle(q):
        pushed = joined(dot(QT[q * PER * Y : (q + 1) * PER * Y], ROWS[...])).reshape(PER, Y, LANES)
        for i in range(PER):
            c = q * PER + i
            force = (GAIN * KAP[c]) * pushed[i]
            mid = E2[c + 3, 8 : 8 + Y] + force
            E2[c + 3, 8 : 8 + Y] = mid
            SPLIT[c * Y : (c + 1) * Y] = parts(mid)
            PREV[c] = force - E[c + 3, 8 : 8 + Y]

    quads = X // PER
    ends = sorted({0, quads - 1})
    inside = [q for q in range(quads) if q not in ends]
    for q in ends:
        middle(q)
    start(halo_m[0:2])
    for q in inside:
        middle(q)
    start(halo_m[2:4])
    gather_edge(2)
    start(halo_m[4:5])
    inner_x(E2)
    for q in range(quads):
        along_z(q)
    finish(halo_m[4:5])
    fixes = fix_z(2)
    for q in range(quads):
        add_fix(fixes, q)
    finish(halo_m[2:4])

    def second(q, with_y):
        for i in range(PER):
            c = q * PER + i
            total = laplace(c)
            if with_y:
                total = total + across_y(E2, c, i)
            val = 2.0 * E2[c + 3, 8 : 8 + Y] + PREV[c] + KAP[c] * total
            out_ref[c] = val
            hi, lo = split2(val)
            NEXT[c * Y : (c + 1) * Y, 0:LANES] = hi
            NEXT[c * Y : (c + 1) * Y, LANES : 2 * LANES] = lo

    for q in inside:
        second(q, True)
    for q in ends:
        for i in range(PER):
            c = q * PER + i
            TOT[c] = TOT[c] + across_y(E2, c, i)

    pieces = max(parts_n, NB * CAP // LANES)
    count = NB // pieces

    def pick(n, quad):
        at = slice(quad * PER * Y, (quad + 1) * PER * Y)
        return joined(dot(Q[n * count * CAP : (n + 1) * count * CAP, at], NEXT[at])).reshape(count, 8, LANES)

    for n in range(pieces):
        total = None
        for q in inside:
            total = pick(n, q) if total is None else total + pick(n, q)
        if total is not None:
            PK[n * count : (n + 1) * count] = total
    finish(halo_m[0:2])
    outer_x(E2)
    for q in ends:
        second(q, False)

    for n in range(pieces):
        total = None
        for q in ends:
            total = pick(n, q) if total is None else total + pick(n, q)
        if inside:
            total = total + PK[n * count : (n + 1) * count]
        PK[n * count : (n + 1) * count] = total
        for k in range(n * count, (n + 1) * count):
            dz, dx, dy = slots[k]
            if k < NB - 1:
                pltpu.make_async_remote_copy(
                    PK.at[k], RET.at[k], bs_sem, br_sem.at[group_of(k)],
                    device_id=(zb[dz] * nx + xb[dx], yb[dy], blk), device_id_type=MESH,
                ).start()
    back = pltpu.make_async_copy(PK.at[NB - 1], RET.at[NB - 1], self_sem.at[3])
    back.start()

    drained(CR.at[pl.ds(0, nz - 1)], cs_sem)
    drained(CA.at[pl.ds(0, G - 1)], fs_sem)
    drained(SB.at[pl.ds(0, NB - 1)], as_sem)
    for n in range(parts_n):
        last = n == parts_n - 1
        drained(RET.at[pl.ds(0, share - 1 if last else share)], br_sem.at[n])
        if last:
            back.wait()
        at = slice(n * share * CAP, (n + 1) * share * CAP)
        got = joined(dot(PM[:, at], parts(RET[n * share : (n + 1) * share].reshape(share * CAP, LANES))))
        hp_ref[...] = got if n == 0 else hp_ref[...] + got
    drained(PK.at[pl.ds(0, NB - 1)], bs_sem)


def keep_out(field, rows, field_out, rows_out, sem):
    copies = [
        pltpu.make_async_copy(field, field_out, sem.at[0]),
        pltpu.make_async_copy(rows, rows_out, sem.at[1]),
    ]
    for copy in copies:
        copy.start()
    for copy in copies:
        copy.wait()


def solution(mesh):
    n_gx, n_gy = mesh.shape["gx"], mesh.shape["gy"]
    dims = torus(n_gx, n_gy)
    NB = n_gx * n_gy

    def local(pressure, pressure_prev, buoyancy, kappa, hull_accel, row_block, row_column):
        X, Y, Z = pressure.shape
        HR = hull_accel.shape[0]
        any_spec = pl.BlockSpec(memory_space=pltpu.HBM)
        vmem_spec = pl.BlockSpec(memory_space=pltpu.VMEM)
        dma = pltpu.SemaphoreType.DMA
        V = pltpu.VMEM
        results = pl.pallas_call(
            functools.partial(kernel, dims),
            out_shape=(
                jax.ShapeDtypeStruct((X, Y, Z), F32),
                jax.ShapeDtypeStruct((HR, Z), F32),
            ),
            in_specs=[any_spec] * 7,
            out_specs=[vmem_spec] * 2,
            scratch_shapes=[
                V((X + 6, Y + 16, Z), F32),
                V((X + 4, Y + 16, Z), F32),
                V((X + 6, Y + 16, Z), F32),
                V((3, 8, X * Y), F32),
                V((3, 8, X * Y), F32),
                V((X * Y, 2 * Z), BF16),
                V((2, 2 * Z, Z), BF16),
                V((8, X * Y), F32),
                V((X, Y, Z), F32),
                V((X, Y, Z), F32),
                V((HR, Z), F32),
                V((X + 3, Y, Z), F32),
                V((256 // Y, Y + 8, Z), F32),
                V((X, Y, Z), F32),
                V((X + 3, Y, Z), F32),
                V((X, Y + 8, Z), F32),
                V((X, Y, Z), F32),
                V((X * Y, 2 * Z), BF16),
                V((8, Z), F32),
                V((dims[0], Z), F32),
                V((dims[1] * dims[2], dims[0], Z), F32),
                V((NB * CAP, 2 * Z), F32),
                V((NB, CAP, Z), F32),
                V((NB, CAP, Z), F32),
                V((NB * CAP, 2 * Z), BF16),
                V((NB, CAP, Z), F32),
                V((NB, CAP, Z), F32),
                V((NB * CAP, X * Y), BF16),
                V((X * Y, NB * CAP), BF16),
                V((HR, NB * CAP), BF16),
                V((1, HR), jnp.int32),
                V((1, HR), jnp.int32),
                V((2, 3, Y // dims[1], Z), F32),
                V((2, 2, Y // dims[1], Z), F32),
                dma((7,)), dma((3, 5)), dma((3, 5)), dma((2, 2, dims[1])), dma((2, 2)), dma((2, 2)),
                dma, dma, dma, dma, dma, dma((4,)), dma, dma((4,)), dma((4,)),
            ],
            compiler_params=pltpu.CompilerParams(collective_id=0, has_side_effects=True, vmem_limit_bytes=36 * 1024 * 1024),
            name="hull_leapfrog",
        )(
            *(pltpu.with_memory_space_constraint(v, pltpu.HBM) for v in (
                pressure, pressure_prev, buoyancy, kappa, hull_accel,
                row_block.reshape(1, HR), row_column.reshape(1, HR),
            ))
        )
        return pl.pallas_call(
            keep_out,
            out_shape=(
                jax.ShapeDtypeStruct((X, Y, Z), F32),
                jax.ShapeDtypeStruct((HR, Z), F32),
            ),
            in_specs=[vmem_spec] * 2,
            out_specs=[any_spec] * 2,
            scratch_shapes=[dma((2,))],
            compiler_params=pltpu.CompilerParams(vmem_limit_bytes=2 * 1024 * 1024),
            name="write_out",
        )(*results)

    return jax.shard_map(
        local,
        mesh=mesh,
        in_specs=(
            P("gx", "gy", "blk"),
            P("gx", "gy", "blk"),
            P("gx", "gy", "blk"),
            P("gx", "gy", "blk"),
            P(("gx", "gy", "blk"), None),
            P(("gx", "gy", "blk"), None),
            P(("gx", "gy", "blk"), None),
        ),
        out_specs=(P("gx", "gy", "blk"), P(("gx", "gy", "blk"), None)),
        check_vma=False,
    )
```

```python
import functools

import jax
import jax.numpy as jnp
from jax import lax
from jax.experimental import pallas as pl
from jax.experimental.pallas import tpu as pltpu
from jax.sharding import PartitionSpec as P

MESH = pl.DeviceIdType.MESH
F32 = jnp.float32
BF16 = jnp.bfloat16
LANES = 128
CAP = 8
COURANT = 0.05
GAIN = 0.5
FACE = COURANT * 0.5 / 576.0


def torus(n_gx, n_gy):
    nx = 4 if n_gx % 4 == 0 and n_gx > 4 else 2
    return n_gx // nx, nx, n_gy


def split2(v):
    hi = v.astype(BF16)
    lo = (v - hi.astype(F32)).astype(BF16)
    return hi, lo


def parts(v):
    hi, lo = split2(v)
    return jnp.concatenate([hi, lo], axis=1)


def joined(v):
    return v[:, :LANES] + v[:, LANES:]


def wide(a, b, c, d):
    return 27.0 * (c - b) - (d - a)


def dot(a, b):
    return jnp.dot(a, b, preferred_element_type=F32)


def dot_nt(a, b):
    return lax.dot_general(a, b, (((1,), (1,)), ((), ())), preferred_element_type=F32)


def dot_tn(a, b):
    return lax.dot_general(a, b, (((0,), (0,)), ((), ())), preferred_element_type=F32)


def onehot(mask):
    return jnp.where(mask, 1.0, 0.0).astype(BF16)


def kernel(
    dims,
    p_hbm, prev_hbm, b_hbm, kap_hbm, hull_hbm, rb_hbm, rc_hbm,
    out_ref, hp_ref,
    E, EB, E2, ZS, ZR, SPLIT, ZW, ZB, PREV, KAP, HULL, FX, FY, TOT, BX, BY, BZ, NEXT,
    CS, CR, CA, MC, SB, RV, ROWS, PK, RET, Q, QT, PM, RB, RC, RLP, RLB,
    in_sem, hs_sem, hr_sem, ls_sem, lr_sem, lf_sem, cs_sem, cr_sem, fs_sem, fr_sem, as_sem, ar_sem, bs_sem, br_sem, self_sem,
):
    nz, nx, ny = dims
    NB = nz * nx * ny
    G = nx * ny
    GS = G * CAP
    X, Y = PREV.shape[0], PREV.shape[1]
    T = Y // 8
    PER = LANES // (4 * T)
    HR = HULL.shape[0]
    cells = X * Y
    n_gx = nz * nx
    gx = lax.axis_index("gx")
    gy = lax.axis_index("gy")
    blk = lax.axis_index("blk")
    zi = gx // nx
    xi = gx % nx
    me = gx * ny + gy
    spot = xi * ny + gy

    zs = [(zi + dz) % nz for dz in range(nz)]
    xs = [(xi + dx) % nx for dx in range(nx)]
    ys = [(gy + dy) % ny for dy in range(ny)]
    zb = [(zi + nz - dz) % nz for dz in range(nz)]
    xb = [(xi + nx - dx) % nx for dx in range(nx)]
    yb = [(gy + ny - dy) % ny for dy in range(ny)]
    plane = [(dx, dy) for dx in range(nx) for dy in range(ny)]

    def hops(offset):
        return sum(min(d, n - d) for d, n in zip(offset, dims))

    slots = sorted(
        [(dz, dx, dy) for dz in range(nz) for dx, dy in plane],
        key=lambda o: (-hops(o), o[0] % 2),
    )
    parts_n = 4
    share = NB // parts_n

    def group_of(k):
        return k // share

    loads = [
        pltpu.make_async_copy(rb_hbm, RB, in_sem.at[5]),
        pltpu.make_async_copy(rc_hbm, RC, in_sem.at[6]),
        pltpu.make_async_copy(hull_hbm, HULL, in_sem.at[0]),
        pltpu.make_async_copy(p_hbm, E.at[pl.ds(3, X), pl.ds(8, Y)], in_sem.at[1]),
        pltpu.make_async_copy(b_hbm, EB.at[pl.ds(2, X), pl.ds(8, Y)], in_sem.at[2]),
        pltpu.make_async_copy(prev_hbm, PREV, in_sem.at[3]),
        pltpu.make_async_copy(kap_hbm, KAP, in_sem.at[4]),
    ]
    for load in loads:
        load.start()

    barrier = pltpu.get_barrier_semaphore()
    for dz, dx, dy in slots[:-1]:
        pl.semaphore_signal(
            barrier, inc=1, device_id=(zs[dz] * nx + xs[dx], ys[dy], blk), device_id_type=MESH
        )
    pl.semaphore_signal(barrier, inc=1, device_id=(gx, gy, 1 - blk), device_id_type=MESH)

    for ref, w in ((E, 3), (EB, 2), (E2, 3)):
        @pl.when(gx == 0)
        def _(ref=ref, w=w):
            ref[0:w] = jnp.zeros((w,) + ref.shape[1:], F32)

        @pl.when(gx == n_gx - 1)
        def _(ref=ref, w=w):
            ref[w + X :] = jnp.zeros((w,) + ref.shape[1:], F32)

        @pl.when(gy == 0)
        def _(ref=ref, w=w):
            ref[w : w + X, 0:8] = jnp.zeros((X, 8, LANES), F32)

        @pl.when(gy == ny - 1)
        def _(ref=ref, w=w):
            ref[w : w + X, 8 + Y :] = jnp.zeros((X, 8, LANES), F32)

    loads[0].wait()
    loads[1].wait()
    rb = RB[...]
    owner = onehot(jnp.broadcast_to(rb, (NB, HR)) == lax.broadcasted_iota(jnp.int32, (NB, HR), 0))
    before = onehot(
        lax.broadcasted_iota(jnp.int32, (HR, HR), 0) < lax.broadcasted_iota(jnp.int32, (HR, HR), 1)
    )
    earlier = dot(owner, before)
    slot = jnp.sum(owner.astype(F32) * earlier, axis=0, keepdims=True).astype(jnp.int32)
    placing = rb * CAP + slot
    code = RC[...] + 1
    row_z = lax.broadcasted_iota(jnp.int32, (16, HR), 0)
    which_z = jnp.broadcast_to(placing // GS, (16, HR))
    coded = jnp.where(row_z == which_z, jnp.broadcast_to(code // 32, (16, HR)), 0) + jnp.where(
        row_z == which_z + 8, jnp.broadcast_to(code % 32, (16, HR)), 0
    )
    lane_of = onehot(lax.broadcasted_iota(jnp.int32, (LANES, HR), 0) == jnp.broadcast_to(placing % GS, (LANES, HR)))
    sums = dot_nt(coded.astype(F32).astype(BF16), lane_of)
    CS[...] = sums[0:8] * 32.0 + sums[8:16]

    loads[2].wait()
    hull_parts = parts(HULL[...])

    def pack(m, _):
        rows = lax.broadcasted_iota(jnp.int32, (GS, HR), 0) + m * GS
        pt = onehot(rows == jnp.broadcast_to(placing, (GS, HR)))
        SB[pl.ds(m * G, G)] = joined(dot(pt, hull_parts)).reshape(G, 8, LANES)
        return 0

    lax.fori_loop(0, nz, pack, 0)

    e_row = lax.broadcasted_iota(jnp.int32, (8, 2 * LANES), 0)
    e_lane = lax.broadcasted_iota(jnp.int32, (8, 2 * LANES), 1) % LANES
    first_sent = jnp.broadcast_to((1 - blk) * (LANES - 3), (8, 2 * LANES))
    wanted = jnp.where(e_row < 3, first_sent + e_row, jnp.where(e_row < 5, e_row - 3, e_row + (LANES - 7)))
    edge_w = onehot((e_lane == wanted) & (e_row < 7))

    def split_planes(ref, lo, q):
        at = pl.ds(q * PER * Y, PER * Y)
        planes = [ref[q * PER + i + lo, 8 : 8 + Y] for i in range(PER)]
        SPLIT[at] = parts(jnp.concatenate(planes, axis=0))

    def gather_edge(field):
        ZS[field] = dot_nt(edge_w, SPLIT[...])

    def all_planes(ref, lo):
        def body(q, _):
            split_planes(ref, lo, q)
            return 0

        lax.fori_loop(0, X // PER, body, 0)

    loads[3].wait()
    loads[4].wait()
    all_planes(EB, 2)
    gather_edge(1)
    all_planes(E, 3)
    gather_edge(0)

    rel_z = (placing // GS + (nz - zi)) % nz
    rel_x = (placing // (CAP * ny) % nx + (nx - xi)) % nx
    rel_y = (placing // CAP % ny + (ny - gy)) % ny
    relative = ((rel_z * nx + rel_x) * ny + rel_y) * CAP + placing % CAP
    weights_row = lax.broadcasted_iota(jnp.int32, (16, LANES), 0)
    place_row = lax.broadcasted_iota(jnp.int32, (16, HR), 0)
    place_code = jnp.where(
        place_row == 0, jnp.broadcast_to(relative // 32, (16, HR)),
        jnp.where(place_row == 1, jnp.broadcast_to(relative % 32, (16, HR)), 0),
    ).astype(F32).astype(BF16)
    place_w = jnp.where(weights_row == 0, 32.0, jnp.where(weights_row == 1, 1.0, 0.0)).astype(BF16)
    placing_col = dot_tn(place_code, place_w)
    span = min(LANES, NB * CAP)
    for m in range(NB * CAP // span):
        spot_lane = lax.broadcasted_iota(jnp.int32, (8, span), 1)
        label = spot_lane % CAP
        for j in range(span // CAP):
            dz, dx, dy = slots[m * (span // CAP) + j]
            base = ((dz * nx + dx) * ny + dy) * CAP
            label = jnp.where(spot_lane // CAP == j, label + base, label)
        label = jnp.broadcast_to(label[0:1], (HR, span)).astype(F32)
        PM[:, m * span : (m + 1) * span] = onehot(placing_col[:, :span] == label)

    pl.semaphore_wait(barrier, NB)

    QY = Y // nx
    up_seam = (xi == nx - 1) & (zi < nz - 1)
    down_seam = (xi == 0) & (zi > 0)
    relay_up = (xi > 0) & (zi > 0)
    relay_down = (xi < nx - 1) & (zi < nz - 1)
    z_above, z_below = jnp.minimum(zi + 1, nz - 1), jnp.maximum(zi - 1, 0)

    def seams(ref, field, width, relay):
        lo = width
        copies = []
        for c in range(nx):
            band_y = pl.ds(8 + c * QY, QY)
            ends_here = c == 0
            copies.append((up_seam, pltpu.make_async_remote_copy(
                ref.at[pl.ds(X + lo - width, width), band_y],
                ref.at[pl.ds(lo - width, width), band_y] if ends_here else relay.at[0],
                ls_sem.at[field, 0, c], hr_sem.at[field, 0] if ends_here else lr_sem.at[field, 0],
                device_id=(z_above * nx + c, gy, blk), device_id_type=MESH)))
            ends_here = c == nx - 1
            copies.append((down_seam, pltpu.make_async_remote_copy(
                ref.at[pl.ds(lo, width), band_y],
                ref.at[pl.ds(X + lo, width), band_y] if ends_here else relay.at[1],
                ls_sem.at[field, 1, c], hr_sem.at[field, 1] if ends_here else lr_sem.at[field, 1],
                device_id=(z_below * nx + c, gy, blk), device_id_type=MESH)))
        band_x = pl.ds(8 + xi * QY, QY)
        onward = [
            (relay_up, 0, pltpu.make_async_remote_copy(
                relay.at[0], ref.at[pl.ds(lo - width, width), band_x],
                lf_sem.at[field, 0], hr_sem.at[field, 0],
                device_id=(zi * nx, gy, blk), device_id_type=MESH)),
            (relay_down, 1, pltpu.make_async_remote_copy(
                relay.at[1], ref.at[pl.ds(X + lo, width), band_x],
                lf_sem.at[field, 1], hr_sem.at[field, 1],
                device_id=(zi * nx + nx - 1, gy, blk), device_id_type=MESH)),
        ]

        def begin():
            for on, copy in copies:
                pl.when(on)(lambda copy=copy: copy.start())

        def forward():
            for on, way, copy in onward:
                @pl.when(on)
                def _(way=way, copy=copy):
                    drained(relay.at[way], lr_sem.at[field, way])
                    copy.start()

        def end():
            for on, copy in copies:
                pl.when(on)(lambda copy=copy: copy.wait_send())
            for on, _, copy in onward:
                pl.when(on)(lambda copy=copy: copy.wait_send())

        return begin, forward, end

    def shares(ref, field, width):
        lo = width
        send, recv = hs_sem.at[field], hr_sem.at[field]
        whole = field == 2
        return [
            (gx < n_gx - 1 if whole else xi < nx - 1, gx > 0, pltpu.make_async_remote_copy(
                ref.at[pl.ds(X + lo - width, width), pl.ds(8, Y)], ref.at[pl.ds(lo - width, width), pl.ds(8, Y)],
                send.at[0], recv.at[0], device_id=(jnp.minimum(gx + 1, n_gx - 1), gy, blk), device_id_type=MESH)),
            (gx > 0 if whole else xi > 0, gx < n_gx - 1, pltpu.make_async_remote_copy(
                ref.at[pl.ds(lo, width), pl.ds(8, Y)], ref.at[pl.ds(X + lo, width), pl.ds(8, Y)],
                send.at[1], recv.at[1], device_id=(jnp.maximum(gx - 1, 0), gy, blk), device_id_type=MESH)),
            (gy < ny - 1, gy > 0, pltpu.make_async_remote_copy(
                ref.at[pl.ds(lo, X), pl.ds(Y + 8 - width, width)], ref.at[pl.ds(lo, X), pl.ds(8 - width, width)],
                send.at[2], recv.at[2], device_id=(gx, jnp.minimum(gy + 1, ny - 1), blk), device_id_type=MESH)),
            (gy > 0, gy < ny - 1, pltpu.make_async_remote_copy(
                ref.at[pl.ds(lo, X), pl.ds(8, width)], ref.at[pl.ds(lo, X), pl.ds(8 + Y, width)],
                send.at[3], recv.at[3], device_id=(gx, jnp.maximum(gy - 1, 0), blk), device_id_type=MESH)),
            (None, None, pltpu.make_async_remote_copy(
                ZS.at[field], ZR.at[field],
                send.at[4], recv.at[4], device_id=(gx, gy, 1 - blk), device_id_type=MESH)),
        ]

    def start(copies):
        for sends, _, copy in copies:
            if sends is None:
                copy.start()
            else:
                pl.when(sends)(lambda copy=copy: copy.start())

    def finish(copies):
        for sends, gets, copy in copies:
            if sends is None:
                copy.wait_send()
                copy.wait_recv()
            else:
                pl.when(sends)(lambda copy=copy: copy.wait_send())
                pl.when(gets)(lambda copy=copy: copy.wait_recv())

    def drained(ref, sem):
        pltpu.make_async_copy(ref, ref, sem).wait()

    for dz in range(1, nz):
        pltpu.make_async_remote_copy(
            CS.at[pl.ds(zs[dz], 1)], CR.at[pl.ds(dz, 1)], cs_sem, cr_sem,
            device_id=(zs[dz] * nx + xi, gy, blk), device_id_type=MESH,
        ).start()
    own_col = pltpu.make_async_copy(CS.at[pl.ds(zi, 1)], CR.at[pl.ds(0, 1)], self_sem.at[0])
    own_col.start()

    halo_p = shares(E, 0, 3)
    halo_b = shares(EB, 1, 2)
    seam_p = seams(E, 0, 3, RLP)
    seam_b = seams(EB, 1, 2, RLB)
    start(halo_p[2:])
    start(halo_b[2:])

    def send_rows(some):
        for k in some:
            dz, dx, dy = slots[k]
            dest_gx = zs[dz] * nx + xs[dx]
            pltpu.make_async_remote_copy(
                SB.at[dest_gx * ny + ys[dy]], RV.at[k], as_sem, ar_sem.at[group_of(k)],
                device_id=(dest_gx, ys[dy], blk), device_id_type=MESH,
            ).start()

    send_rows(range(NB // 2))
    seam_p[0]()
    seam_b[0]()
    start(halo_p[0:2])
    start(halo_b[0:2])

    w_row = lax.broadcasted_iota(jnp.int32, (2 * LANES, LANES), 0) % LANES
    w_col = lax.broadcasted_iota(jnp.int32, (2 * LANES, LANES), 1)

    def band(shift):
        at = w_row - w_col - shift
        val = jnp.where(at == 0, 27.0, jnp.where(at == -1, -27.0, 0.0))
        return (val + jnp.where(at == 1, -1.0, jnp.where(at == -2, 1.0, 0.0))).astype(BF16)

    ZW[0] = band(1)
    ZW[1] = band(0)
    f_row = lax.broadcasted_iota(jnp.int32, (16, LANES), 0) % 8
    f_lane = lax.broadcasted_iota(jnp.int32, (16, LANES), 1)
    fix_lane = jnp.where(f_row < 3, f_row, (LANES + 2) - f_row)
    fix_w = onehot((f_lane == fix_lane) & (f_row < 6))
    left_on = blk.astype(F32)
    right_on = 1.0 - left_on

    def along_z(q):
        at = pl.ds(q * PER * Y, PER * Y)
        slope = dot(SPLIT[at], ZW[0])
        flux = slope * jnp.concatenate([BZ[q * PER + i] for i in range(PER)], axis=0)
        val = dot(parts(flux), ZW[1]).reshape(PER, Y, LANES)
        for i in range(PER):
            TOT[q * PER + i] = val[i]

    def fix_z(field):
        def halo(r):
            return ZR[field, r : r + 1]

        def own(r):
            return ZS[field, r : r + 1]

        a3, a2, a1 = (halo(r) * left_on for r in range(3))
        n0, n1, n2 = (halo(r) * right_on for r in range(3))
        v0, v1, v_prev, v_last = own(3), own(4), own(5), own(6)
        at0 = ZB[0:1] * a1
        before1 = ZB[1:2] * (27.0 * (v0 - a1) - (v1 - a2))
        before2 = ZB[2:3] * (27.0 * (a1 - a2) - (v0 - a3))
        end1 = ZB[4:5] * (27.0 * (n0 - v_last) - (n1 - v_prev))
        end2 = ZB[3:4] * n0
        after = ZB[5:6] * (27.0 * (n1 - n0) - (n2 - v_last))
        rows = [
            27.0 * (at0 - before1) + before2,
            before1 - 27.0 * at0,
            at0,
            27.0 * (end1 + end2) - after,
            -27.0 * end2 - end1,
            end2,
            jnp.zeros_like(at0),
            jnp.zeros_like(at0),
        ]
        hi, lo = split2(jnp.concatenate(rows, axis=0))
        return jnp.concatenate([hi.astype(F32), lo.astype(F32)], axis=0).astype(BF16)

    def add_fix(fixes, q):
        val = dot_tn(fixes[:, q * PER * Y : (q + 1) * PER * Y], fix_w).reshape(PER, Y, LANES)
        for i in range(PER):
            TOT[q * PER + i] = TOT[q * PER + i] + val[i]

    inner_lane = lax.broadcasted_iota(jnp.int32, (Y, LANES), 1) < LANES - 1

    def face_x(c):
        BX[c] = (EB[c, 8 : 8 + Y] + EB[c + 1, 8 : 8 + Y]) * FACE

    def own_faces(q, _):
        for i in range(PER):
            c = q * PER + i
            own_b = EB[c + 2, 8 : 8 + Y]
            BZ[c] = jnp.where(inner_lane, own_b + pltpu.roll(own_b, LANES - 1, 1), 0.0) * FACE
        return 0

    def flux_x(src, c):
        FX[c] = wide(src[c, 8 : 8 + Y], src[c + 1, 8 : 8 + Y], src[c + 2, 8 : 8 + Y], src[c + 3, 8 : 8 + Y]) * BX[c]

    def inner_x(src):
        for c in range(3, X):
            flux_x(src, c)

    def outer_x(src):
        for c in (0, 1, 2, X, X + 1, X + 2):
            flux_x(src, c)

    def across_y(src, c, i):
        FY[i] = wide(src[c + 3, 5 : 13 + Y], src[c + 3, 6 : 14 + Y], src[c + 3, 7 : 15 + Y], src[c + 3, 8 : 16 + Y]) * BY[c]
        return wide(FY[i, 0:Y], FY[i, 1 : 1 + Y], FY[i, 2 : 2 + Y], FY[i, 3 : 3 + Y])

    lax.fori_loop(0, X // PER, own_faces, 0)
    for c in range(3, X):
        face_x(c)
    inner_x(E)
    for q in range(X // PER):
        along_z(q)

    drained(CR.at[pl.ds(0, nz - 1)], cr_sem)
    own_col.wait()
    for dx, dy in plane[1:]:
        pltpu.make_async_remote_copy(
            CR, CA.at[dx * ny + dy], fs_sem, fr_sem,
            device_id=(zi * nx + xs[dx], ys[dy], blk), device_id_type=MESH,
        ).start()
    own_tile = pltpu.make_async_copy(CR, CA.at[0], self_sem.at[2])
    own_tile.start()
    send_rows(range(NB // 2, NB - 1))
    own = pltpu.make_async_copy(SB.at[me], RV.at[NB - 1], self_sem.at[1])
    own.start()

    finish(halo_b[2:])
    b_left = [ZR[1, r : r + 1] * left_on for r in (1, 2)]
    b_right = [ZR[1, r : r + 1] * right_on for r in (0, 1)]
    own_edge = [ZS[1, r : r + 1] for r in range(3, 7)]
    ZB[...] = FACE * jnp.concatenate(
        [
            own_edge[0] + own_edge[1],
            b_left[1] + own_edge[0],
            b_left[0] + b_left[1],
            own_edge[2] + own_edge[3],
            own_edge[3] + b_right[0],
            b_right[0] + b_right[1],
            jnp.zeros((2, cells), F32),
        ],
        axis=0,
    )
    def faces_y(q, _):
        for i in range(PER):
            c = q * PER + i
            BY[c] = (EB[c + 2, 6 : 14 + Y] + EB[c + 2, 7 : 15 + Y]) * FACE
        return 0

    lax.fori_loop(0, X // PER, faces_y, 0)

    def laplace(c):
        return TOT[c] + wide(FX[c], FX[c + 1], FX[c + 2], FX[c + 3])

    finish(halo_p[2:])
    fixes = fix_z(0)
    for q in range(X // PER):
        add_fix(fixes, q)
    seam_p[1]()
    seam_b[1]()

    drained(CA.at[pl.ds(0, G - 1)], fr_sem)
    own_tile.wait()
    keep = lax.broadcasted_iota(jnp.int32, (8, LANES), 1) == lax.broadcasted_iota(jnp.int32, (8, LANES), 0) + spot * CAP
    for k, (dz, dx, dy) in enumerate(slots):
        line = jnp.where(keep, jnp.broadcast_to(CA[dx * ny + dy, dz : dz + 1, :], (8, LANES)), 0.0)
        high = jnp.floor(line * (1.0 / 32.0))
        MC[k * 8 : k * 8 + 8, 0:LANES] = high
        MC[k * 8 : k * 8 + 8, LANES:] = line - 32.0 * high
    w_lane = jnp.where(lax.broadcasted_iota(jnp.int32, (8, 2 * LANES), 1) < LANES, 32.0, 1.0).astype(BF16)
    w_full = jnp.where(lax.broadcasted_iota(jnp.int32, (2 * LANES, LANES), 0) < LANES, 32.0, 1.0).astype(BF16)
    col_lane = dot_nt(w_lane, MC[...].astype(BF16))[0:1].astype(jnp.int32) - 1
    chunk = min(LANES, cells)

    def build_qt(m, _):
        ids = lax.broadcasted_iota(jnp.int32, (chunk, NB * CAP), 0) + m * chunk
        QT[pl.ds(m * chunk, chunk)] = onehot(ids == jnp.broadcast_to(col_lane, (chunk, NB * CAP)))
        return 0

    lax.fori_loop(0, cells // chunk, build_qt, 0)

    def build_q(dz, _):
        col_sub = dot(MC[pl.ds(dz * GS, GS)].astype(BF16), w_full) - 1.0
        for m in range(cells // chunk):
            ids = (lax.broadcasted_iota(jnp.int32, (GS, chunk), 1) + m * chunk).astype(F32)
            Q[pl.ds(dz * GS, GS), m * chunk : (m + 1) * chunk] = onehot(col_sub[:, :chunk] == ids)
        return 0

    lax.fori_loop(0, nz, build_q, 0)

    quads = X // PER
    ends = sorted({0, quads - 1})
    inside = [q for q in range(quads) if q not in ends]

    def first(q):
        for i in range(PER):
            c = q * PER + i
            E2[c + 3, 8 : 8 + Y] = 2.0 * E[c + 3, 8 : 8 + Y] - PREV[c] + KAP[c] * (laplace(c) + across_y(E, c, i))

    loads[5].wait()
    loads[6].wait()
    for q in inside:
        first(q)
    finish(halo_b[0:2])
    for c in (0, 1, 2, X, X + 1, X + 2):
        face_x(c)
    finish(halo_p[0:2])
    outer_x(E)
    for q in ends:
        first(q)
    seam_p[2]()
    seam_b[2]()

    for n in range(parts_n):
        last = n == parts_n - 1
        drained(RV.at[pl.ds(0, share - 1 if last else share)], ar_sem.at[n])
        if last:
            own.wait()
        ROWS[n * share * CAP : (n + 1) * share * CAP] = parts(
            RV[n * share : (n + 1) * share].reshape(share * CAP, LANES)
        )
    halo_m = shares(E2, 2, 3)

    def middle(q):
        pushed = joined(dot(QT[q * PER * Y : (q + 1) * PER * Y], ROWS[...])).reshape(PER, Y, LANES)
        for i in range(PER):
            c = q * PER + i
            force = (GAIN * KAP[c]) * pushed[i]
            mid = E2[c + 3, 8 : 8 + Y] + force
            E2[c + 3, 8 : 8 + Y] = mid
            SPLIT[c * Y : (c + 1) * Y] = parts(mid)
            PREV[c] = force - E[c + 3, 8 : 8 + Y]

    for q in ends:
        middle(q)
    start(halo_m[0:2])
    for q in inside:
        middle(q)
    start(halo_m[2:4])
    gather_edge(2)
    start(halo_m[4:5])
    inner_x(E2)
    for q in range(quads):
        along_z(q)
    finish(halo_m[4:5])
    fixes = fix_z(2)
    for q in range(quads):
        add_fix(fixes, q)
    finish(halo_m[2:4])

    def second(q, with_y):
        for i in range(PER):
            c = q * PER + i
            total = laplace(c)
            if with_y:
                total = total + across_y(E2, c, i)
            val = 2.0 * E2[c + 3, 8 : 8 + Y] + PREV[c] + KAP[c] * total
            out_ref[c] = val
            hi, lo = split2(val)
            NEXT[c * Y : (c + 1) * Y, 0:LANES] = hi
            NEXT[c * Y : (c + 1) * Y, LANES : 2 * LANES] = lo

    for q in inside:
        second(q, True)
    for q in ends:
        for i in range(PER):
            c = q * PER + i
            TOT[c] = TOT[c] + across_y(E2, c, i)

    pieces = max(parts_n, NB * CAP // LANES)
    count = NB // pieces

    def pick(n, quad):
        at = slice(quad * PER * Y, (quad + 1) * PER * Y)
        return joined(dot(Q[n * count * CAP : (n + 1) * count * CAP, at], NEXT[at])).reshape(count, 8, LANES)

    for n in range(pieces):
        total = None
        for q in inside:
            total = pick(n, q) if total is None else total + pick(n, q)
        if total is not None:
            PK[n * count : (n + 1) * count] = total
    finish(halo_m[0:2])
    outer_x(E2)
    for q in ends:
        second(q, False)

    for n in range(pieces):
        total = None
        for q in ends:
            total = pick(n, q) if total is None else total + pick(n, q)
        if inside:
            total = total + PK[n * count : (n + 1) * count]
        PK[n * count : (n + 1) * count] = total
        for k in range(n * count, (n + 1) * count):
            dz, dx, dy = slots[k]
            if k < NB - 1:
                pltpu.make_async_remote_copy(
                    PK.at[k], RET.at[k], bs_sem, br_sem.at[group_of(k)],
                    device_id=(zb[dz] * nx + xb[dx], yb[dy], blk), device_id_type=MESH,
                ).start()
    back = pltpu.make_async_copy(PK.at[NB - 1], RET.at[NB - 1], self_sem.at[3])
    back.start()

    drained(CR.at[pl.ds(0, nz - 1)], cs_sem)
    drained(CA.at[pl.ds(0, G - 1)], fs_sem)
    drained(SB.at[pl.ds(0, NB - 1)], as_sem)
    for n in range(parts_n):
        last = n == parts_n - 1
        drained(RET.at[pl.ds(0, share - 1 if last else share)], br_sem.at[n])
        if last:
            back.wait()
        at = slice(n * share * CAP, (n + 1) * share * CAP)
        got = joined(dot(PM[:, at], parts(RET[n * share : (n + 1) * share].reshape(share * CAP, LANES))))
        hp_ref[...] = got if n == 0 else hp_ref[...] + got
    drained(PK.at[pl.ds(0, NB - 1)], bs_sem)


def keep_out(field, rows, field_out, rows_out, sem):
    copies = [
        pltpu.make_async_copy(field, field_out, sem.at[0]),
        pltpu.make_async_copy(rows, rows_out, sem.at[1]),
    ]
    for copy in copies:
        copy.start()
    for copy in copies:
        copy.wait()


def solution(mesh):
    n_gx, n_gy = mesh.shape["gx"], mesh.shape["gy"]
    dims = torus(n_gx, n_gy)
    NB = n_gx * n_gy

    def local(pressure, pressure_prev, buoyancy, kappa, hull_accel, row_block, row_column):
        X, Y, Z = pressure.shape
        HR = hull_accel.shape[0]
        any_spec = pl.BlockSpec(memory_space=pltpu.HBM)
        vmem_spec = pl.BlockSpec(memory_space=pltpu.VMEM)
        dma = pltpu.SemaphoreType.DMA
        V = pltpu.VMEM
        results = pl.pallas_call(
            functools.partial(kernel, dims),
            out_shape=(
                jax.ShapeDtypeStruct((X, Y, Z), F32),
                jax.ShapeDtypeStruct((HR, Z), F32),
            ),
            in_specs=[any_spec] * 7,
            out_specs=[vmem_spec] * 2,
            scratch_shapes=[
                V((X + 6, Y + 16, Z), F32),
                V((X + 4, Y + 16, Z), F32),
                V((X + 6, Y + 16, Z), F32),
                V((3, 8, X * Y), F32),
                V((3, 8, X * Y), F32),
                V((X * Y, 2 * Z), BF16),
                V((2, 2 * Z, Z), BF16),
                V((8, X * Y), F32),
                V((X, Y, Z), F32),
                V((X, Y, Z), F32),
                V((HR, Z), F32),
                V((X + 3, Y, Z), F32),
                V((256 // Y, Y + 8, Z), F32),
                V((X, Y, Z), F32),
                V((X + 3, Y, Z), F32),
                V((X, Y + 8, Z), F32),
                V((X, Y, Z), F32),
                V((X * Y, 2 * Z), BF16),
                V((8, Z), F32),
                V((dims[0], Z), F32),
                V((dims[1] * dims[2], dims[0], Z), F32),
                V((NB * CAP, 2 * Z), F32),
                V((NB, CAP, Z), F32),
                V((NB, CAP, Z), F32),
                V((NB * CAP, 2 * Z), BF16),
                V((NB, CAP, Z), F32),
                V((NB, CAP, Z), F32),
                V((NB * CAP, X * Y), BF16),
                V((X * Y, NB * CAP), BF16),
                V((HR, NB * CAP), BF16),
                V((1, HR), jnp.int32),
                V((1, HR), jnp.int32),
                V((2, 3, Y // dims[1], Z), F32),
                V((2, 2, Y // dims[1], Z), F32),
                dma((7,)), dma((3, 5)), dma((3, 5)), dma((2, 2, dims[1])), dma((2, 2)), dma((2, 2)),
                dma, dma, dma, dma, dma, dma((4,)), dma, dma((4,)), dma((4,)),
            ],
            compiler_params=pltpu.CompilerParams(collective_id=0, has_side_effects=True, vmem_limit_bytes=36 * 1024 * 1024),
            name="hull_leapfrog",
        )(
            *(pltpu.with_memory_space_constraint(v, pltpu.HBM) for v in (
                pressure, pressure_prev, buoyancy, kappa, hull_accel,
                row_block.reshape(1, HR), row_column.reshape(1, HR),
            ))
        )
        return pl.pallas_call(
            keep_out,
            out_shape=(
                jax.ShapeDtypeStruct((X, Y, Z), F32),
                jax.ShapeDtypeStruct((HR, Z), F32),
            ),
            in_specs=[vmem_spec] * 2,
            out_specs=[any_spec] * 2,
            scratch_shapes=[dma((2,))],
            compiler_params=pltpu.CompilerParams(vmem_limit_bytes=2 * 1024 * 1024),
            name="write_out",
        )(*results)

    return jax.shard_map(
        local,
        mesh=mesh,
        in_specs=(
            P("gx", "gy", "blk"),
            P("gx", "gy", "blk"),
            P("gx", "gy", "blk"),
            P("gx", "gy", "blk"),
            P(("gx", "gy", "blk"), None),
            P(("gx", "gy", "blk"), None),
            P(("gx", "gy", "blk"), None),
        ),
        out_specs=(P("gx", "gy", "blk"), P(("gx", "gy", "blk"), None)),
        check_vma=False,
    )
```

```python
import functools

import jax
import jax.numpy as jnp
from jax import lax
from jax.experimental import pallas as pl
from jax.experimental.pallas import tpu as pltpu
from jax.sharding import PartitionSpec as P

MESH = pl.DeviceIdType.MESH
F32 = jnp.float32
BF16 = jnp.bfloat16
LANES = 128
CAP = 8
COURANT = 0.05
GAIN = 0.5
FACE = COURANT * 0.5 / 576.0


def torus(n_gx, n_gy):
    nx = 4 if n_gx % 4 == 0 and n_gx > 4 else 2
    return n_gx // nx, nx, n_gy


def split2(v):
    hi = v.astype(BF16)
    lo = (v - hi.astype(F32)).astype(BF16)
    return hi, lo


def parts(v):
    hi, lo = split2(v)
    return jnp.concatenate([hi, lo], axis=1)


def joined(v):
    return v[:, :LANES] + v[:, LANES:]


def wide(a, b, c, d):
    return 27.0 * (c - b) - (d - a)


def dot(a, b):
    return jnp.dot(a, b, preferred_element_type=F32)


def dot_nt(a, b):
    return lax.dot_general(a, b, (((1,), (1,)), ((), ())), preferred_element_type=F32)


def dot_tn(a, b):
    return lax.dot_general(a, b, (((0,), (0,)), ((), ())), preferred_element_type=F32)


def onehot(mask):
    return jnp.where(mask, 1.0, 0.0).astype(BF16)


def kernel(
    dims,
    p_hbm, prev_hbm, b_hbm, kap_hbm, hull_hbm, rb_hbm, rc_hbm,
    out_ref, hp_ref,
    E, EB, E2, ZS, ZR, SPLIT, ZW, ZB, PREV, KAP, HULL, FX, FY, TOT, BX, BY, BZ, NEXT,
    CS, CR, CA, MC, SB, RV, ROWS, PK, RET, Q, QT, PM, RB, RC, RLP, RLB,
    in_sem, hs_sem, hr_sem, ls_sem, lr_sem, lf_sem, cs_sem, cr_sem, fs_sem, fr_sem, as_sem, ar_sem, bs_sem, br_sem, self_sem,
):
    nz, nx, ny = dims
    NB = nz * nx * ny
    G = nx * ny
    GS = G * CAP
    X, Y = PREV.shape[0], PREV.shape[1]
    T = Y // 8
    PER = LANES // (4 * T)
    HR = HULL.shape[0]
    cells = X * Y
    n_gx = nz * nx
    gx = lax.axis_index("gx")
    gy = lax.axis_index("gy")
    blk = lax.axis_index("blk")
    zi = gx // nx
    xi = gx % nx
    me = gx * ny + gy
    spot = xi * ny + gy

    zs = [(zi + dz) % nz for dz in range(nz)]
    xs = [(xi + dx) % nx for dx in range(nx)]
    ys = [(gy + dy) % ny for dy in range(ny)]
    zb = [(zi + nz - dz) % nz for dz in range(nz)]
    xb = [(xi + nx - dx) % nx for dx in range(nx)]
    yb = [(gy + ny - dy) % ny for dy in range(ny)]
    plane = [(dx, dy) for dx in range(nx) for dy in range(ny)]

    def hops(offset):
        return sum(min(d, n - d) for d, n in zip(offset, dims))

    slots = sorted(
        [(dz, dx, dy) for dz in range(nz) for dx, dy in plane],
        key=lambda o: (-hops(o), o[0] % 2),
    )
    parts_n = 4
    share = NB // parts_n

    def group_of(k):
        return k // share

    loads = [
        pltpu.make_async_copy(rb_hbm, RB, in_sem.at[5]),
        pltpu.make_async_copy(rc_hbm, RC, in_sem.at[6]),
        pltpu.make_async_copy(hull_hbm, HULL, in_sem.at[0]),
        pltpu.make_async_copy(p_hbm, E.at[pl.ds(3, X), pl.ds(8, Y)], in_sem.at[1]),
        pltpu.make_async_copy(b_hbm, EB.at[pl.ds(2, X), pl.ds(8, Y)], in_sem.at[2]),
        pltpu.make_async_copy(prev_hbm, PREV, in_sem.at[3]),
        pltpu.make_async_copy(kap_hbm, KAP, in_sem.at[4]),
    ]
    for load in loads:
        load.start()

    barrier = pltpu.get_barrier_semaphore()
    for dz, dx, dy in slots[:-1]:
        pl.semaphore_signal(
            barrier, inc=1, device_id=(zs[dz] * nx + xs[dx], ys[dy], blk), device_id_type=MESH
        )
    pl.semaphore_signal(barrier, inc=1, device_id=(gx, gy, 1 - blk), device_id_type=MESH)

    for ref, w in ((E, 3), (EB, 2), (E2, 3)):
        @pl.when(gx == 0)
        def _(ref=ref, w=w):
            ref[0:w] = jnp.zeros((w,) + ref.shape[1:], F32)

        @pl.when(gx == n_gx - 1)
        def _(ref=ref, w=w):
            ref[w + X :] = jnp.zeros((w,) + ref.shape[1:], F32)

        @pl.when(gy == 0)
        def _(ref=ref, w=w):
            ref[w : w + X, 0:8] = jnp.zeros((X, 8, LANES), F32)

        @pl.when(gy == ny - 1)
        def _(ref=ref, w=w):
            ref[w : w + X, 8 + Y :] = jnp.zeros((X, 8, LANES), F32)

    loads[0].wait()
    loads[1].wait()
    rb = RB[...]
    owner = onehot(jnp.broadcast_to(rb, (NB, HR)) == lax.broadcasted_iota(jnp.int32, (NB, HR), 0))
    before = onehot(
        lax.broadcasted_iota(jnp.int32, (HR, HR), 0) < lax.broadcasted_iota(jnp.int32, (HR, HR), 1)
    )
    earlier = dot(owner, before)
    slot = jnp.sum(owner.astype(F32) * earlier, axis=0, keepdims=True).astype(jnp.int32)
    placing = rb * CAP + slot
    code = RC[...] + 1
    row_z = lax.broadcasted_iota(jnp.int32, (16, HR), 0)
    which_z = jnp.broadcast_to(placing // GS, (16, HR))
    coded = jnp.where(row_z == which_z, jnp.broadcast_to(code // 32, (16, HR)), 0) + jnp.where(
        row_z == which_z + 8, jnp.broadcast_to(code % 32, (16, HR)), 0
    )
    lane_of = onehot(lax.broadcasted_iota(jnp.int32, (LANES, HR), 0) == jnp.broadcast_to(placing % GS, (LANES, HR)))
    sums = dot_nt(coded.astype(F32).astype(BF16), lane_of)
    CS[...] = sums[0:8] * 32.0 + sums[8:16]

    loads[2].wait()
    hull_parts = parts(HULL[...])

    def pack(m, _):
        rows = lax.broadcasted_iota(jnp.int32, (GS, HR), 0) + m * GS
        pt = onehot(rows == jnp.broadcast_to(placing, (GS, HR)))
        SB[pl.ds(m * G, G)] = joined(dot(pt, hull_parts)).reshape(G, 8, LANES)
        return 0

    lax.fori_loop(0, nz, pack, 0)

    e_row = lax.broadcasted_iota(jnp.int32, (8, 2 * LANES), 0)
    e_lane = lax.broadcasted_iota(jnp.int32, (8, 2 * LANES), 1) % LANES
    first_sent = jnp.broadcast_to((1 - blk) * (LANES - 3), (8, 2 * LANES))
    wanted = jnp.where(e_row < 3, first_sent + e_row, jnp.where(e_row < 5, e_row - 3, e_row + (LANES - 7)))
    edge_w = onehot((e_lane == wanted) & (e_row < 7))

    def split_planes(ref, lo, q):
        at = pl.ds(q * PER * Y, PER * Y)
        planes = [ref[q * PER + i + lo, 8 : 8 + Y] for i in range(PER)]
        SPLIT[at] = parts(jnp.concatenate(planes, axis=0))

    def gather_edge(field):
        ZS[field] = dot_nt(edge_w, SPLIT[...])

    def all_planes(ref, lo):
        def body(q, _):
            split_planes(ref, lo, q)
            return 0

        lax.fori_loop(0, X // PER, body, 0)

    loads[3].wait()
    loads[4].wait()
    all_planes(EB, 2)
    gather_edge(1)
    all_planes(E, 3)
    gather_edge(0)

    rel_z = (placing // GS + (nz - zi)) % nz
    rel_x = (placing // (CAP * ny) % nx + (nx - xi)) % nx
    rel_y = (placing // CAP % ny + (ny - gy)) % ny
    relative = ((rel_z * nx + rel_x) * ny + rel_y) * CAP + placing % CAP
    weights_row = lax.broadcasted_iota(jnp.int32, (16, LANES), 0)
    place_row = lax.broadcasted_iota(jnp.int32, (16, HR), 0)
    place_code = jnp.where(
        place_row == 0, jnp.broadcast_to(relative // 32, (16, HR)),
        jnp.where(place_row == 1, jnp.broadcast_to(relative % 32, (16, HR)), 0),
    ).astype(F32).astype(BF16)
    place_w = jnp.where(weights_row == 0, 32.0, jnp.where(weights_row == 1, 1.0, 0.0)).astype(BF16)
    placing_col = dot_tn(place_code, place_w)
    span = min(LANES, NB * CAP)
    for m in range(NB * CAP // span):
        spot_lane = lax.broadcasted_iota(jnp.int32, (8, span), 1)
        label = spot_lane % CAP
        for j in range(span // CAP):
            dz, dx, dy = slots[m * (span // CAP) + j]
            base = ((dz * nx + dx) * ny + dy) * CAP
            label = jnp.where(spot_lane // CAP == j, label + base, label)
        label = jnp.broadcast_to(label[0:1], (HR, span)).astype(F32)
        PM[:, m * span : (m + 1) * span] = onehot(placing_col[:, :span] == label)

    pl.semaphore_wait(barrier, NB)

    QY = Y // nx
    up_seam = (xi == nx - 1) & (zi < nz - 1)
    down_seam = (xi == 0) & (zi > 0)
    relay_up = (xi > 0) & (zi > 0)
    relay_down = (xi < nx - 1) & (zi < nz - 1)
    z_above, z_below = jnp.minimum(zi + 1, nz - 1), jnp.maximum(zi - 1, 0)

    def seams(ref, field, width, relay):
        lo = width
        copies = []
        for c in range(nx):
            band_y = pl.ds(8 + c * QY, QY)
            ends_here = c == 0
            copies.append((up_seam, pltpu.make_async_remote_copy(
                ref.at[pl.ds(X + lo - width, width), band_y],
                ref.at[pl.ds(lo - width, width), band_y] if ends_here else relay.at[0],
                ls_sem.at[field, 0, c], hr_sem.at[field, 0] if ends_here else lr_sem.at[field, 0],
                device_id=(z_above * nx + c, gy, blk), device_id_type=MESH)))
            ends_here = c == nx - 1
            copies.append((down_seam, pltpu.make_async_remote_copy(
                ref.at[pl.ds(lo, width), band_y],
                ref.at[pl.ds(X + lo, width), band_y] if ends_here else relay.at[1],
                ls_sem.at[field, 1, c], hr_sem.at[field, 1] if ends_here else lr_sem.at[field, 1],
                device_id=(z_below * nx + c, gy, blk), device_id_type=MESH)))
        band_x = pl.ds(8 + xi * QY, QY)
        onward = [
            (relay_up, 0, pltpu.make_async_remote_copy(
                relay.at[0], ref.at[pl.ds(lo - width, width), band_x],
                lf_sem.at[field, 0], hr_sem.at[field, 0],
                device_id=(zi * nx, gy, blk), device_id_type=MESH)),
            (relay_down, 1, pltpu.make_async_remote_copy(
                relay.at[1], ref.at[pl.ds(X + lo, width), band_x],
                lf_sem.at[field, 1], hr_sem.at[field, 1],
                device_id=(zi * nx + nx - 1, gy, blk), device_id_type=MESH)),
        ]

        def begin():
            for on, copy in copies:
                pl.when(on)(lambda copy=copy: copy.start())

        def forward():
            for on, way, copy in onward:
                @pl.when(on)
                def _(way=way, copy=copy):
                    drained(relay.at[way], lr_sem.at[field, way])
                    copy.start()

        def end():
            for on, copy in copies:
                pl.when(on)(lambda copy=copy: copy.wait_send())
            for on, _, copy in onward:
                pl.when(on)(lambda copy=copy: copy.wait_send())

        return begin, forward, end

    def shares(ref, field, width):
        lo = width
        send, recv = hs_sem.at[field], hr_sem.at[field]
        whole = field == 2
        return [
            (gx < n_gx - 1 if whole else xi < nx - 1, gx > 0, pltpu.make_async_remote_copy(
                ref.at[pl.ds(X + lo - width, width), pl.ds(8, Y)], ref.at[pl.ds(lo - width, width), pl.ds(8, Y)],
                send.at[0], recv.at[0], device_id=(jnp.minimum(gx + 1, n_gx - 1), gy, blk), device_id_type=MESH)),
            (gx > 0 if whole else xi > 0, gx < n_gx - 1, pltpu.make_async_remote_copy(
                ref.at[pl.ds(lo, width), pl.ds(8, Y)], ref.at[pl.ds(X + lo, width), pl.ds(8, Y)],
                send.at[1], recv.at[1], device_id=(jnp.maximum(gx - 1, 0), gy, blk), device_id_type=MESH)),
            (gy < ny - 1, gy > 0, pltpu.make_async_remote_copy(
                ref.at[pl.ds(lo, X), pl.ds(Y + 8 - width, width)], ref.at[pl.ds(lo, X), pl.ds(8 - width, width)],
                send.at[2], recv.at[2], device_id=(gx, jnp.minimum(gy + 1, ny - 1), blk), device_id_type=MESH)),
            (gy > 0, gy < ny - 1, pltpu.make_async_remote_copy(
                ref.at[pl.ds(lo, X), pl.ds(8, width)], ref.at[pl.ds(lo, X), pl.ds(8 + Y, width)],
                send.at[3], recv.at[3], device_id=(gx, jnp.maximum(gy - 1, 0), blk), device_id_type=MESH)),
            (None, None, pltpu.make_async_remote_copy(
                ZS.at[field], ZR.at[field],
                send.at[4], recv.at[4], device_id=(gx, gy, 1 - blk), device_id_type=MESH)),
        ]

    def start(copies):
        for sends, _, copy in copies:
            if sends is None:
                copy.start()
            else:
                pl.when(sends)(lambda copy=copy: copy.start())

    def finish(copies):
        for sends, gets, copy in copies:
            if sends is None:
                copy.wait_send()
                copy.wait_recv()
            else:
                pl.when(sends)(lambda copy=copy: copy.wait_send())
                pl.when(gets)(lambda copy=copy: copy.wait_recv())

    def drained(ref, sem):
        pltpu.make_async_copy(ref, ref, sem).wait()

    for dz in range(1, nz):
        pltpu.make_async_remote_copy(
            CS.at[pl.ds(zs[dz], 1)], CR.at[pl.ds(dz, 1)], cs_sem, cr_sem,
            device_id=(zs[dz] * nx + xi, gy, blk), device_id_type=MESH,
        ).start()
    own_col = pltpu.make_async_copy(CS.at[pl.ds(zi, 1)], CR.at[pl.ds(0, 1)], self_sem.at[0])
    own_col.start()

    halo_p = shares(E, 0, 3)
    halo_b = shares(EB, 1, 2)
    seam_p = seams(E, 0, 3, RLP)
    seam_b = seams(EB, 1, 2, RLB)
    start(halo_p[2:])
    start(halo_b[2:])

    def send_rows(some):
        for k in some:
            dz, dx, dy = slots[k]
            dest_gx = zs[dz] * nx + xs[dx]
            pltpu.make_async_remote_copy(
                SB.at[dest_gx * ny + ys[dy]], RV.at[k], as_sem, ar_sem.at[group_of(k)],
                device_id=(dest_gx, ys[dy], blk), device_id_type=MESH,
            ).start()

    seam_p[0]()
    seam_b[0]()
    start(halo_p[0:2])
    start(halo_b[0:2])
    send_rows(range(NB - 1))
    own = pltpu.make_async_copy(SB.at[me], RV.at[NB - 1], self_sem.at[1])
    own.start()

    w_row = lax.broadcasted_iota(jnp.int32, (2 * LANES, LANES), 0) % LANES
    w_col = lax.broadcasted_iota(jnp.int32, (2 * LANES, LANES), 1)

    def band(shift):
        at = w_row - w_col - shift
        val = jnp.where(at == 0, 27.0, jnp.where(at == -1, -27.0, 0.0))
        return (val + jnp.where(at == 1, -1.0, jnp.where(at == -2, 1.0, 0.0))).astype(BF16)

    ZW[0] = band(1)
    ZW[1] = band(0)
    f_row = lax.broadcasted_iota(jnp.int32, (16, LANES), 0) % 8
    f_lane = lax.broadcasted_iota(jnp.int32, (16, LANES), 1)
    fix_lane = jnp.where(f_row < 3, f_row, (LANES + 2) - f_row)
    fix_w = onehot((f_lane == fix_lane) & (f_row < 6))
    left_on = blk.astype(F32)
    right_on = 1.0 - left_on

    def along_z(q):
        at = pl.ds(q * PER * Y, PER * Y)
        slope = dot(SPLIT[at], ZW[0])
        flux = slope * jnp.concatenate([BZ[q * PER + i] for i in range(PER)], axis=0)
        val = dot(parts(flux), ZW[1]).reshape(PER, Y, LANES)
        for i in range(PER):
            TOT[q * PER + i] = val[i]

    def fix_z(field):
        def halo(r):
            return ZR[field, r : r + 1]

        def own(r):
            return ZS[field, r : r + 1]

        a3, a2, a1 = (halo(r) * left_on for r in range(3))
        n0, n1, n2 = (halo(r) * right_on for r in range(3))
        v0, v1, v_prev, v_last = own(3), own(4), own(5), own(6)
        at0 = ZB[0:1] * a1
        before1 = ZB[1:2] * (27.0 * (v0 - a1) - (v1 - a2))
        before2 = ZB[2:3] * (27.0 * (a1 - a2) - (v0 - a3))
        end1 = ZB[4:5] * (27.0 * (n0 - v_last) - (n1 - v_prev))
        end2 = ZB[3:4] * n0
        after = ZB[5:6] * (27.0 * (n1 - n0) - (n2 - v_last))
        rows = [
            27.0 * (at0 - before1) + before2,
            before1 - 27.0 * at0,
            at0,
            27.0 * (end1 + end2) - after,
            -27.0 * end2 - end1,
            end2,
            jnp.zeros_like(at0),
            jnp.zeros_like(at0),
        ]
        hi, lo = split2(jnp.concatenate(rows, axis=0))
        return jnp.concatenate([hi.astype(F32), lo.astype(F32)], axis=0).astype(BF16)

    def add_fix(fixes, q):
        val = dot_tn(fixes[:, q * PER * Y : (q + 1) * PER * Y], fix_w).reshape(PER, Y, LANES)
        for i in range(PER):
            TOT[q * PER + i] = TOT[q * PER + i] + val[i]

    inner_lane = lax.broadcasted_iota(jnp.int32, (Y, LANES), 1) < LANES - 1

    def face_x(c):
        BX[c] = (EB[c, 8 : 8 + Y] + EB[c + 1, 8 : 8 + Y]) * FACE

    def own_faces(q, _):
        for i in range(PER):
            c = q * PER + i
            own_b = EB[c + 2, 8 : 8 + Y]
            BZ[c] = jnp.where(inner_lane, own_b + pltpu.roll(own_b, LANES - 1, 1), 0.0) * FACE
        return 0

    def flux_x(src, c):
        FX[c] = wide(src[c, 8 : 8 + Y], src[c + 1, 8 : 8 + Y], src[c + 2, 8 : 8 + Y], src[c + 3, 8 : 8 + Y]) * BX[c]

    def inner_x(src):
        for c in range(3, X):
            flux_x(src, c)

    def outer_x(src):
        for c in (0, 1, 2, X, X + 1, X + 2):
            flux_x(src, c)

    def across_y(src, c, i):
        FY[i] = wide(src[c + 3, 5 : 13 + Y], src[c + 3, 6 : 14 + Y], src[c + 3, 7 : 15 + Y], src[c + 3, 8 : 16 + Y]) * BY[c]
        return wide(FY[i, 0:Y], FY[i, 1 : 1 + Y], FY[i, 2 : 2 + Y], FY[i, 3 : 3 + Y])

    lax.fori_loop(0, X // PER, own_faces, 0)
    for c in range(3, X):
        face_x(c)
    inner_x(E)
    for q in range(X // PER):
        along_z(q)

    drained(CR.at[pl.ds(0, nz - 1)], cr_sem)
    own_col.wait()
    for dx, dy in plane[1:]:
        pltpu.make_async_remote_copy(
            CR, CA.at[dx * ny + dy], fs_sem, fr_sem,
            device_id=(zi * nx + xs[dx], ys[dy], blk), device_id_type=MESH,
        ).start()
    own_tile = pltpu.make_async_copy(CR, CA.at[0], self_sem.at[2])
    own_tile.start()

    finish(halo_b[2:])
    b_left = [ZR[1, r : r + 1] * left_on for r in (1, 2)]
    b_right = [ZR[1, r : r + 1] * right_on for r in (0, 1)]
    own_edge = [ZS[1, r : r + 1] for r in range(3, 7)]
    ZB[...] = FACE * jnp.concatenate(
        [
            own_edge[0] + own_edge[1],
            b_left[1] + own_edge[0],
            b_left[0] + b_left[1],
            own_edge[2] + own_edge[3],
            own_edge[3] + b_right[0],
            b_right[0] + b_right[1],
            jnp.zeros((2, cells), F32),
        ],
        axis=0,
    )
    def faces_y(q, _):
        for i in range(PER):
            c = q * PER + i
            BY[c] = (EB[c + 2, 6 : 14 + Y] + EB[c + 2, 7 : 15 + Y]) * FACE
        return 0

    lax.fori_loop(0, X // PER, faces_y, 0)

    def laplace(c):
        return TOT[c] + wide(FX[c], FX[c + 1], FX[c + 2], FX[c + 3])

    finish(halo_p[2:])
    fixes = fix_z(0)
    for q in range(X // PER):
        add_fix(fixes, q)
    seam_p[1]()
    seam_b[1]()

    drained(CA.at[pl.ds(0, G - 1)], fr_sem)
    own_tile.wait()
    keep = lax.broadcasted_iota(jnp.int32, (8, LANES), 1) == lax.broadcasted_iota(jnp.int32, (8, LANES), 0) + spot * CAP
    for k, (dz, dx, dy) in enumerate(slots):
        line = jnp.where(keep, jnp.broadcast_to(CA[dx * ny + dy, dz : dz + 1, :], (8, LANES)), 0.0)
        high = jnp.floor(line * (1.0 / 32.0))
        MC[k * 8 : k * 8 + 8, 0:LANES] = high
        MC[k * 8 : k * 8 + 8, LANES:] = line - 32.0 * high
    w_lane = jnp.where(lax.broadcasted_iota(jnp.int32, (8, 2 * LANES), 1) < LANES, 32.0, 1.0).astype(BF16)
    w_full = jnp.where(lax.broadcasted_iota(jnp.int32, (2 * LANES, LANES), 0) < LANES, 32.0, 1.0).astype(BF16)
    col_lane = dot_nt(w_lane, MC[...].astype(BF16))[0:1].astype(jnp.int32) - 1
    chunk = min(LANES, cells)

    def build_qt(m, _):
        ids = lax.broadcasted_iota(jnp.int32, (chunk, NB * CAP), 0) + m * chunk
        QT[pl.ds(m * chunk, chunk)] = onehot(ids == jnp.broadcast_to(col_lane, (chunk, NB * CAP)))
        return 0

    lax.fori_loop(0, cells // chunk, build_qt, 0)

    def build_q(dz, _):
        col_sub = dot(MC[pl.ds(dz * GS, GS)].astype(BF16), w_full) - 1.0
        for m in range(cells // chunk):
            ids = (lax.broadcasted_iota(jnp.int32, (GS, chunk), 1) + m * chunk).astype(F32)
            Q[pl.ds(dz * GS, GS), m * chunk : (m + 1) * chunk] = onehot(col_sub[:, :chunk] == ids)
        return 0

    lax.fori_loop(0, nz, build_q, 0)

    quads = X // PER
    ends = sorted({0, quads - 1})
    inside = [q for q in range(quads) if q not in ends]

    def first(q):
        for i in range(PER):
            c = q * PER + i
            E2[c + 3, 8 : 8 + Y] = 2.0 * E[c + 3, 8 : 8 + Y] - PREV[c] + KAP[c] * (laplace(c) + across_y(E, c, i))

    loads[5].wait()
    loads[6].wait()
    for q in inside:
        first(q)
    finish(halo_b[0:2])
    for c in (0, 1, 2, X, X + 1, X + 2):
        face_x(c)
    finish(halo_p[0:2])
    outer_x(E)
    for q in ends:
        first(q)
    seam_p[2]()
    seam_b[2]()

    for n in range(parts_n):
        last = n == parts_n - 1
        drained(RV.at[pl.ds(0, share - 1 if last else share)], ar_sem.at[n])
        if last:
            own.wait()
        ROWS[n * share * CAP : (n + 1) * share * CAP] = parts(
            RV[n * share : (n + 1) * share].reshape(share * CAP, LANES)
        )
    halo_m = shares(E2, 2, 3)

    def middle(q):
        pushed = joined(dot(QT[q * PER * Y : (q + 1) * PER * Y], ROWS[...])).reshape(PER, Y, LANES)
        for i in range(PER):
            c = q * PER + i
            force = (GAIN * KAP[c]) * pushed[i]
            mid = E2[c + 3, 8 : 8 + Y] + force
            E2[c + 3, 8 : 8 + Y] = mid
            SPLIT[c * Y : (c + 1) * Y] = parts(mid)
            PREV[c] = force - E[c + 3, 8 : 8 + Y]

    for q in ends:
        middle(q)
    start(halo_m[0:2])
    for q in inside:
        middle(q)
    start(halo_m[2:4])
    gather_edge(2)
    start(halo_m[4:5])
    inner_x(E2)
    for q in range(quads):
        along_z(q)
    finish(halo_m[4:5])
    fixes = fix_z(2)
    for q in range(quads):
        add_fix(fixes, q)
    finish(halo_m[2:4])

    def second(q, with_y):
        for i in range(PER):
            c = q * PER + i
            total = laplace(c)
            if with_y:
                total = total + across_y(E2, c, i)
            val = 2.0 * E2[c + 3, 8 : 8 + Y] + PREV[c] + KAP[c] * total
            out_ref[c] = val
            hi, lo = split2(val)
            NEXT[c * Y : (c + 1) * Y, 0:LANES] = hi
            NEXT[c * Y : (c + 1) * Y, LANES : 2 * LANES] = lo

    for q in inside:
        second(q, True)
    for q in ends:
        for i in range(PER):
            c = q * PER + i
            TOT[c] = TOT[c] + across_y(E2, c, i)

    pieces = max(parts_n, NB * CAP // LANES)
    count = NB // pieces

    def pick(n, quad):
        at = slice(quad * PER * Y, (quad + 1) * PER * Y)
        return joined(dot(Q[n * count * CAP : (n + 1) * count * CAP, at], NEXT[at])).reshape(count, 8, LANES)

    for n in range(pieces):
        total = None
        for q in inside:
            total = pick(n, q) if total is None else total + pick(n, q)
        if total is not None:
            PK[n * count : (n + 1) * count] = total
    finish(halo_m[0:2])
    outer_x(E2)
    for q in ends:
        second(q, False)

    for n in range(pieces):
        total = None
        for q in ends:
            total = pick(n, q) if total is None else total + pick(n, q)
        if inside:
            total = total + PK[n * count : (n + 1) * count]
        PK[n * count : (n + 1) * count] = total
        for k in range(n * count, (n + 1) * count):
            dz, dx, dy = slots[k]
            if k < NB - 1:
                pltpu.make_async_remote_copy(
                    PK.at[k], RET.at[k], bs_sem, br_sem.at[group_of(k)],
                    device_id=(zb[dz] * nx + xb[dx], yb[dy], blk), device_id_type=MESH,
                ).start()
    back = pltpu.make_async_copy(PK.at[NB - 1], RET.at[NB - 1], self_sem.at[3])
    back.start()

    drained(CR.at[pl.ds(0, nz - 1)], cs_sem)
    drained(CA.at[pl.ds(0, G - 1)], fs_sem)
    drained(SB.at[pl.ds(0, NB - 1)], as_sem)
    for n in range(parts_n):
        last = n == parts_n - 1
        drained(RET.at[pl.ds(0, share - 1 if last else share)], br_sem.at[n])
        if last:
            back.wait()
        at = slice(n * share * CAP, (n + 1) * share * CAP)
        got = joined(dot(PM[:, at], parts(RET[n * share : (n + 1) * share].reshape(share * CAP, LANES))))
        hp_ref[...] = got if n == 0 else hp_ref[...] + got
    drained(PK.at[pl.ds(0, NB - 1)], bs_sem)


def keep_out(field, rows, field_out, rows_out, sem):
    copies = [
        pltpu.make_async_copy(field, field_out, sem.at[0]),
        pltpu.make_async_copy(rows, rows_out, sem.at[1]),
    ]
    for copy in copies:
        copy.start()
    for copy in copies:
        copy.wait()


def solution(mesh):
    n_gx, n_gy = mesh.shape["gx"], mesh.shape["gy"]
    dims = torus(n_gx, n_gy)
    NB = n_gx * n_gy

    def local(pressure, pressure_prev, buoyancy, kappa, hull_accel, row_block, row_column):
        X, Y, Z = pressure.shape
        HR = hull_accel.shape[0]
        any_spec = pl.BlockSpec(memory_space=pltpu.HBM)
        vmem_spec = pl.BlockSpec(memory_space=pltpu.VMEM)
        dma = pltpu.SemaphoreType.DMA
        V = pltpu.VMEM
        results = pl.pallas_call(
            functools.partial(kernel, dims),
            out_shape=(
                jax.ShapeDtypeStruct((X, Y, Z), F32),
                jax.ShapeDtypeStruct((HR, Z), F32),
            ),
            in_specs=[any_spec] * 7,
            out_specs=[vmem_spec] * 2,
            scratch_shapes=[
                V((X + 6, Y + 16, Z), F32),
                V((X + 4, Y + 16, Z), F32),
                V((X + 6, Y + 16, Z), F32),
                V((3, 8, X * Y), F32),
                V((3, 8, X * Y), F32),
                V((X * Y, 2 * Z), BF16),
                V((2, 2 * Z, Z), BF16),
                V((8, X * Y), F32),
                V((X, Y, Z), F32),
                V((X, Y, Z), F32),
                V((HR, Z), F32),
                V((X + 3, Y, Z), F32),
                V((256 // Y, Y + 8, Z), F32),
                V((X, Y, Z), F32),
                V((X + 3, Y, Z), F32),
                V((X, Y + 8, Z), F32),
                V((X, Y, Z), F32),
                V((X * Y, 2 * Z), BF16),
                V((8, Z), F32),
                V((dims[0], Z), F32),
                V((dims[1] * dims[2], dims[0], Z), F32),
                V((NB * CAP, 2 * Z), F32),
                V((NB, CAP, Z), F32),
                V((NB, CAP, Z), F32),
                V((NB * CAP, 2 * Z), BF16),
                V((NB, CAP, Z), F32),
                V((NB, CAP, Z), F32),
                V((NB * CAP, X * Y), BF16),
                V((X * Y, NB * CAP), BF16),
                V((HR, NB * CAP), BF16),
                V((1, HR), jnp.int32),
                V((1, HR), jnp.int32),
                V((2, 3, Y // dims[1], Z), F32),
                V((2, 2, Y // dims[1], Z), F32),
                dma((7,)), dma((3, 5)), dma((3, 5)), dma((2, 2, dims[1])), dma((2, 2)), dma((2, 2)),
                dma, dma, dma, dma, dma, dma((4,)), dma, dma((4,)), dma((4,)),
            ],
            compiler_params=pltpu.CompilerParams(collective_id=0, has_side_effects=True, vmem_limit_bytes=36 * 1024 * 1024),
            name="hull_leapfrog",
        )(
            *(pltpu.with_memory_space_constraint(v, pltpu.HBM) for v in (
                pressure, pressure_prev, buoyancy, kappa, hull_accel,
                row_block.reshape(1, HR), row_column.reshape(1, HR),
            ))
        )
        return pl.pallas_call(
            keep_out,
            out_shape=(
                jax.ShapeDtypeStruct((X, Y, Z), F32),
                jax.ShapeDtypeStruct((HR, Z), F32),
            ),
            in_specs=[vmem_spec] * 2,
            out_specs=[any_spec] * 2,
            scratch_shapes=[dma((2,))],
            compiler_params=pltpu.CompilerParams(vmem_limit_bytes=2 * 1024 * 1024),
            name="write_out",
        )(*results)

    return jax.shard_map(
        local,
        mesh=mesh,
        in_specs=(
            P("gx", "gy", "blk"),
            P("gx", "gy", "blk"),
            P("gx", "gy", "blk"),
            P("gx", "gy", "blk"),
            P(("gx", "gy", "blk"), None),
            P(("gx", "gy", "blk"), None),
            P(("gx", "gy", "blk"), None),
        ),
        out_specs=(P("gx", "gy", "blk"), P(("gx", "gy", "blk"), None)),
        check_vma=False,
    )
```

```python
import functools

import jax
import jax.numpy as jnp
from jax import lax
from jax.experimental import pallas as pl
from jax.experimental.pallas import tpu as pltpu
from jax.sharding import PartitionSpec as P

MESH = pl.DeviceIdType.MESH
F32 = jnp.float32
BF16 = jnp.bfloat16
LANES = 128
CAP = 8
COURANT = 0.05
GAIN = 0.5
FACE = COURANT * 0.5 / 576.0


def torus(n_gx, n_gy):
    nx = 4 if n_gx % 4 == 0 and n_gx > 4 else 2
    return n_gx // nx, nx, n_gy


def split2(v):
    hi = v.astype(BF16)
    lo = (v - hi.astype(F32)).astype(BF16)
    return hi, lo


def parts(v):
    hi, lo = split2(v)
    return jnp.concatenate([hi, lo], axis=1)


def joined(v):
    return v[:, :LANES] + v[:, LANES:]


def wide(a, b, c, d):
    return 27.0 * (c - b) - (d - a)


def dot(a, b):
    return jnp.dot(a, b, preferred_element_type=F32)


def dot_nt(a, b):
    return lax.dot_general(a, b, (((1,), (1,)), ((), ())), preferred_element_type=F32)


def dot_tn(a, b):
    return lax.dot_general(a, b, (((0,), (0,)), ((), ())), preferred_element_type=F32)


def onehot(mask):
    return jnp.where(mask, 1.0, 0.0).astype(BF16)


def kernel(
    dims,
    p_hbm, prev_hbm, b_hbm, kap_hbm, hull_hbm, rb_hbm, rc_hbm,
    out_ref, hp_ref,
    E, EB, E2, ZS, ZR, SPLIT, ZW, ZB, PREV, KAP, HULL, FX, FY, TOT, BX, BY, BZ, NEXT,
    CS, CR, CA, MC, SB, RV, ROWS, PK, RET, Q, QT, PM, RB, RC, RLP, RLB,
    in_sem, hs_sem, hr_sem, ls_sem, lr_sem, lf_sem, cs_sem, cr_sem, fs_sem, fr_sem, as_sem, ar_sem, bs_sem, br_sem, self_sem,
):
    nz, nx, ny = dims
    NB = nz * nx * ny
    G = nx * ny
    GS = G * CAP
    X, Y = PREV.shape[0], PREV.shape[1]
    T = Y // 8
    PER = LANES // (4 * T)
    HR = HULL.shape[0]
    cells = X * Y
    n_gx = nz * nx
    gx = lax.axis_index("gx")
    gy = lax.axis_index("gy")
    blk = lax.axis_index("blk")
    zi = gx // nx
    xi = gx % nx
    me = gx * ny + gy
    spot = xi * ny + gy

    zs = [(zi + dz) % nz for dz in range(nz)]
    xs = [(xi + dx) % nx for dx in range(nx)]
    ys = [(gy + dy) % ny for dy in range(ny)]
    zb = [(zi + nz - dz) % nz for dz in range(nz)]
    xb = [(xi + nx - dx) % nx for dx in range(nx)]
    yb = [(gy + ny - dy) % ny for dy in range(ny)]
    plane = [(dx, dy) for dx in range(nx) for dy in range(ny)]

    def hops(offset):
        return sum(min(d, n - d) for d, n in zip(offset, dims))

    slots = sorted(
        [(dz, dx, dy) for dz in range(nz) for dx, dy in plane],
        key=lambda o: (-hops(o), o[0] % 2),
    )
    parts_n = 4
    share = NB // parts_n

    def group_of(k):
        return k // share

    loads = [
        pltpu.make_async_copy(rb_hbm, RB, in_sem.at[5]),
        pltpu.make_async_copy(rc_hbm, RC, in_sem.at[6]),
        pltpu.make_async_copy(hull_hbm, HULL, in_sem.at[0]),
        pltpu.make_async_copy(p_hbm, E.at[pl.ds(3, X), pl.ds(8, Y)], in_sem.at[1]),
        pltpu.make_async_copy(b_hbm, EB.at[pl.ds(2, X), pl.ds(8, Y)], in_sem.at[2]),
        pltpu.make_async_copy(prev_hbm, PREV, in_sem.at[3]),
        pltpu.make_async_copy(kap_hbm, KAP, in_sem.at[4]),
    ]
    for load in loads:
        load.start()

    barrier = pltpu.get_barrier_semaphore()
    for dz, dx, dy in slots[:-1]:
        pl.semaphore_signal(
            barrier, inc=1, device_id=(zs[dz] * nx + xs[dx], ys[dy], blk), device_id_type=MESH
        )
    pl.semaphore_signal(barrier, inc=1, device_id=(gx, gy, 1 - blk), device_id_type=MESH)

    for ref, w in ((E, 3), (EB, 2), (E2, 3)):
        @pl.when(gx == 0)
        def _(ref=ref, w=w):
            ref[0:w] = jnp.zeros((w,) + ref.shape[1:], F32)

        @pl.when(gx == n_gx - 1)
        def _(ref=ref, w=w):
            ref[w + X :] = jnp.zeros((w,) + ref.shape[1:], F32)

        @pl.when(gy == 0)
        def _(ref=ref, w=w):
            ref[w : w + X, 0:8] = jnp.zeros((X, 8, LANES), F32)

        @pl.when(gy == ny - 1)
        def _(ref=ref, w=w):
            ref[w : w + X, 8 + Y :] = jnp.zeros((X, 8, LANES), F32)

    loads[0].wait()
    loads[1].wait()
    rb = RB[...]
    owner = onehot(jnp.broadcast_to(rb, (NB, HR)) == lax.broadcasted_iota(jnp.int32, (NB, HR), 0))
    before = onehot(
        lax.broadcasted_iota(jnp.int32, (HR, HR), 0) < lax.broadcasted_iota(jnp.int32, (HR, HR), 1)
    )
    earlier = dot(owner, before)
    slot = jnp.sum(owner.astype(F32) * earlier, axis=0, keepdims=True).astype(jnp.int32)
    placing = rb * CAP + slot
    code = RC[...] + 1
    row_z = lax.broadcasted_iota(jnp.int32, (16, HR), 0)
    which_z = jnp.broadcast_to(placing // GS, (16, HR))
    coded = jnp.where(row_z == which_z, jnp.broadcast_to(code // 32, (16, HR)), 0) + jnp.where(
        row_z == which_z + 8, jnp.broadcast_to(code % 32, (16, HR)), 0
    )
    lane_of = onehot(lax.broadcasted_iota(jnp.int32, (LANES, HR), 0) == jnp.broadcast_to(placing % GS, (LANES, HR)))
    sums = dot_nt(coded.astype(F32).astype(BF16), lane_of)
    CS[...] = sums[0:8] * 32.0 + sums[8:16]

    loads[2].wait()
    hull_parts = parts(HULL[...])

    def pack(m, _):
        rows = lax.broadcasted_iota(jnp.int32, (GS, HR), 0) + m * GS
        pt = onehot(rows == jnp.broadcast_to(placing, (GS, HR)))
        SB[pl.ds(m * G, G)] = joined(dot(pt, hull_parts)).reshape(G, 8, LANES)
        return 0

    lax.fori_loop(0, nz, pack, 0)

    e_row = lax.broadcasted_iota(jnp.int32, (8, 2 * LANES), 0)
    e_lane = lax.broadcasted_iota(jnp.int32, (8, 2 * LANES), 1) % LANES
    first_sent = jnp.broadcast_to((1 - blk) * (LANES - 3), (8, 2 * LANES))
    wanted = jnp.where(e_row < 3, first_sent + e_row, jnp.where(e_row < 5, e_row - 3, e_row + (LANES - 7)))
    edge_w = onehot((e_lane == wanted) & (e_row < 7))

    def split_planes(ref, lo, q):
        at = pl.ds(q * PER * Y, PER * Y)
        planes = [ref[q * PER + i + lo, 8 : 8 + Y] for i in range(PER)]
        SPLIT[at] = parts(jnp.concatenate(planes, axis=0))

    def gather_edge(field):
        ZS[field] = dot_nt(edge_w, SPLIT[...])

    def all_planes(ref, lo):
        def body(q, _):
            split_planes(ref, lo, q)
            return 0

        lax.fori_loop(0, X // PER, body, 0)

    loads[3].wait()
    loads[4].wait()
    all_planes(EB, 2)
    gather_edge(1)
    all_planes(E, 3)
    gather_edge(0)

    rel_z = (placing // GS + (nz - zi)) % nz
    rel_x = (placing // (CAP * ny) % nx + (nx - xi)) % nx
    rel_y = (placing // CAP % ny + (ny - gy)) % ny
    relative = ((rel_z * nx + rel_x) * ny + rel_y) * CAP + placing % CAP
    weights_row = lax.broadcasted_iota(jnp.int32, (16, LANES), 0)
    place_row = lax.broadcasted_iota(jnp.int32, (16, HR), 0)
    place_code = jnp.where(
        place_row == 0, jnp.broadcast_to(relative // 32, (16, HR)),
        jnp.where(place_row == 1, jnp.broadcast_to(relative % 32, (16, HR)), 0),
    ).astype(F32).astype(BF16)
    place_w = jnp.where(weights_row == 0, 32.0, jnp.where(weights_row == 1, 1.0, 0.0)).astype(BF16)
    placing_col = dot_tn(place_code, place_w)
    span = min(LANES, NB * CAP)
    for m in range(NB * CAP // span):
        spot_lane = lax.broadcasted_iota(jnp.int32, (8, span), 1)
        label = spot_lane % CAP
        for j in range(span // CAP):
            dz, dx, dy = slots[m * (span // CAP) + j]
            base = ((dz * nx + dx) * ny + dy) * CAP
            label = jnp.where(spot_lane // CAP == j, label + base, label)
        label = jnp.broadcast_to(label[0:1], (HR, span)).astype(F32)
        PM[:, m * span : (m + 1) * span] = onehot(placing_col[:, :span] == label)

    pl.semaphore_wait(barrier, NB)

    QY = Y // nx
    up_seam = (xi == nx - 1) & (zi < nz - 1)
    down_seam = (xi == 0) & (zi > 0)
    relay_up = (xi > 0) & (zi > 0)
    relay_down = (xi < nx - 1) & (zi < nz - 1)
    z_above, z_below = jnp.minimum(zi + 1, nz - 1), jnp.maximum(zi - 1, 0)

    def seams(ref, field, width, relay):
        lo = width
        copies = []
        for c in range(nx):
            band_y = pl.ds(8 + c * QY, QY)
            ends_here = c == 0
            copies.append((up_seam, pltpu.make_async_remote_copy(
                ref.at[pl.ds(X + lo - width, width), band_y],
                ref.at[pl.ds(lo - width, width), band_y] if ends_here else relay.at[0],
                ls_sem.at[field, 0, c], hr_sem.at[field, 0] if ends_here else lr_sem.at[field, 0],
                device_id=(z_above * nx + c, gy, blk), device_id_type=MESH)))
            ends_here = c == nx - 1
            copies.append((down_seam, pltpu.make_async_remote_copy(
                ref.at[pl.ds(lo, width), band_y],
                ref.at[pl.ds(X + lo, width), band_y] if ends_here else relay.at[1],
                ls_sem.at[field, 1, c], hr_sem.at[field, 1] if ends_here else lr_sem.at[field, 1],
                device_id=(z_below * nx + c, gy, blk), device_id_type=MESH)))
        band_x = pl.ds(8 + xi * QY, QY)
        onward = [
            (relay_up, 0, pltpu.make_async_remote_copy(
                relay.at[0], ref.at[pl.ds(lo - width, width), band_x],
                lf_sem.at[field, 0], hr_sem.at[field, 0],
                device_id=(zi * nx, gy, blk), device_id_type=MESH)),
            (relay_down, 1, pltpu.make_async_remote_copy(
                relay.at[1], ref.at[pl.ds(X + lo, width), band_x],
                lf_sem.at[field, 1], hr_sem.at[field, 1],
                device_id=(zi * nx + nx - 1, gy, blk), device_id_type=MESH)),
        ]

        def begin():
            for on, copy in copies:
                pl.when(on)(lambda copy=copy: copy.start())

        def forward():
            for on, way, copy in onward:
                @pl.when(on)
                def _(way=way, copy=copy):
                    drained(relay.at[way], lr_sem.at[field, way])
                    copy.start()

        def end():
            for on, copy in copies:
                pl.when(on)(lambda copy=copy: copy.wait_send())
            for on, _, copy in onward:
                pl.when(on)(lambda copy=copy: copy.wait_send())

        return begin, forward, end

    def shares(ref, field, width):
        lo = width
        send, recv = hs_sem.at[field], hr_sem.at[field]
        whole = field == 2
        return [
            (gx < n_gx - 1 if whole else xi < nx - 1, gx > 0, pltpu.make_async_remote_copy(
                ref.at[pl.ds(X + lo - width, width), pl.ds(8, Y)], ref.at[pl.ds(lo - width, width), pl.ds(8, Y)],
                send.at[0], recv.at[0], device_id=(jnp.minimum(gx + 1, n_gx - 1), gy, blk), device_id_type=MESH)),
            (gx > 0 if whole else xi > 0, gx < n_gx - 1, pltpu.make_async_remote_copy(
                ref.at[pl.ds(lo, width), pl.ds(8, Y)], ref.at[pl.ds(X + lo, width), pl.ds(8, Y)],
                send.at[1], recv.at[1], device_id=(jnp.maximum(gx - 1, 0), gy, blk), device_id_type=MESH)),
            (gy < ny - 1, gy > 0, pltpu.make_async_remote_copy(
                ref.at[pl.ds(lo, X), pl.ds(Y + 8 - width, width)], ref.at[pl.ds(lo, X), pl.ds(8 - width, width)],
                send.at[2], recv.at[2], device_id=(gx, jnp.minimum(gy + 1, ny - 1), blk), device_id_type=MESH)),
            (gy > 0, gy < ny - 1, pltpu.make_async_remote_copy(
                ref.at[pl.ds(lo, X), pl.ds(8, width)], ref.at[pl.ds(lo, X), pl.ds(8 + Y, width)],
                send.at[3], recv.at[3], device_id=(gx, jnp.maximum(gy - 1, 0), blk), device_id_type=MESH)),
            (None, None, pltpu.make_async_remote_copy(
                ZS.at[field], ZR.at[field],
                send.at[4], recv.at[4], device_id=(gx, gy, 1 - blk), device_id_type=MESH)),
        ]

    def start(copies):
        for sends, _, copy in copies:
            if sends is None:
                copy.start()
            else:
                pl.when(sends)(lambda copy=copy: copy.start())

    def finish(copies):
        for sends, gets, copy in copies:
            if sends is None:
                copy.wait_send()
                copy.wait_recv()
            else:
                pl.when(sends)(lambda copy=copy: copy.wait_send())
                pl.when(gets)(lambda copy=copy: copy.wait_recv())

    def drained(ref, sem):
        pltpu.make_async_copy(ref, ref, sem).wait()

    for dz in range(1, nz):
        pltpu.make_async_remote_copy(
            CS.at[pl.ds(zs[dz], 1)], CR.at[pl.ds(dz, 1)], cs_sem, cr_sem,
            device_id=(zs[dz] * nx + xi, gy, blk), device_id_type=MESH,
        ).start()
    own_col = pltpu.make_async_copy(CS.at[pl.ds(zi, 1)], CR.at[pl.ds(0, 1)], self_sem.at[0])
    own_col.start()

    halo_p = shares(E, 0, 3)
    halo_b = shares(EB, 1, 2)
    seam_p = seams(E, 0, 3, RLP)
    seam_b = seams(EB, 1, 2, RLB)
    start(halo_p[2:])
    start(halo_b[2:])

    def send_rows(some):
        for k in some:
            dz, dx, dy = slots[k]
            dest_gx = zs[dz] * nx + xs[dx]
            pltpu.make_async_remote_copy(
                SB.at[dest_gx * ny + ys[dy]], RV.at[k], as_sem, ar_sem.at[group_of(k)],
                device_id=(dest_gx, ys[dy], blk), device_id_type=MESH,
            ).start()

    send_rows(range(NB // 8))
    seam_p[0]()
    seam_b[0]()
    start(halo_p[0:2])
    start(halo_b[0:2])

    w_row = lax.broadcasted_iota(jnp.int32, (2 * LANES, LANES), 0) % LANES
    w_col = lax.broadcasted_iota(jnp.int32, (2 * LANES, LANES), 1)

    def band(shift):
        at = w_row - w_col - shift
        val = jnp.where(at == 0, 27.0, jnp.where(at == -1, -27.0, 0.0))
        return (val + jnp.where(at == 1, -1.0, jnp.where(at == -2, 1.0, 0.0))).astype(BF16)

    ZW[0] = band(1)
    ZW[1] = band(0)
    f_row = lax.broadcasted_iota(jnp.int32, (16, LANES), 0) % 8
    f_lane = lax.broadcasted_iota(jnp.int32, (16, LANES), 1)
    fix_lane = jnp.where(f_row < 3, f_row, (LANES + 2) - f_row)
    fix_w = onehot((f_lane == fix_lane) & (f_row < 6))
    left_on = blk.astype(F32)
    right_on = 1.0 - left_on

    def along_z(q):
        at = pl.ds(q * PER * Y, PER * Y)
        slope = dot(SPLIT[at], ZW[0])
        flux = slope * jnp.concatenate([BZ[q * PER + i] for i in range(PER)], axis=0)
        val = dot(parts(flux), ZW[1]).reshape(PER, Y, LANES)
        for i in range(PER):
            TOT[q * PER + i] = val[i]

    def fix_z(field):
        def halo(r):
            return ZR[field, r : r + 1]

        def own(r):
            return ZS[field, r : r + 1]

        a3, a2, a1 = (halo(r) * left_on for r in range(3))
        n0, n1, n2 = (halo(r) * right_on for r in range(3))
        v0, v1, v_prev, v_last = own(3), own(4), own(5), own(6)
        at0 = ZB[0:1] * a1
        before1 = ZB[1:2] * (27.0 * (v0 - a1) - (v1 - a2))
        before2 = ZB[2:3] * (27.0 * (a1 - a2) - (v0 - a3))
        end1 = ZB[4:5] * (27.0 * (n0 - v_last) - (n1 - v_prev))
        end2 = ZB[3:4] * n0
        after = ZB[5:6] * (27.0 * (n1 - n0) - (n2 - v_last))
        rows = [
            27.0 * (at0 - before1) + before2,
            before1 - 27.0 * at0,
            at0,
            27.0 * (end1 + end2) - after,
            -27.0 * end2 - end1,
            end2,
            jnp.zeros_like(at0),
            jnp.zeros_like(at0),
        ]
        hi, lo = split2(jnp.concatenate(rows, axis=0))
        return jnp.concatenate([hi.astype(F32), lo.astype(F32)], axis=0).astype(BF16)

    def add_fix(fixes, q):
        val = dot_tn(fixes[:, q * PER * Y : (q + 1) * PER * Y], fix_w).reshape(PER, Y, LANES)
        for i in range(PER):
            TOT[q * PER + i] = TOT[q * PER + i] + val[i]

    inner_lane = lax.broadcasted_iota(jnp.int32, (Y, LANES), 1) < LANES - 1

    def face_x(c):
        BX[c] = (EB[c, 8 : 8 + Y] + EB[c + 1, 8 : 8 + Y]) * FACE

    def own_faces(q, _):
        for i in range(PER):
            c = q * PER + i
            own_b = EB[c + 2, 8 : 8 + Y]
            BZ[c] = jnp.where(inner_lane, own_b + pltpu.roll(own_b, LANES - 1, 1), 0.0) * FACE
        return 0

    def flux_x(src, c):
        FX[c] = wide(src[c, 8 : 8 + Y], src[c + 1, 8 : 8 + Y], src[c + 2, 8 : 8 + Y], src[c + 3, 8 : 8 + Y]) * BX[c]

    def inner_x(src):
        for c in range(3, X):
            flux_x(src, c)

    def outer_x(src):
        for c in (0, 1, 2, X, X + 1, X + 2):
            flux_x(src, c)

    def across_y(src, c, i):
        FY[i] = wide(src[c + 3, 5 : 13 + Y], src[c + 3, 6 : 14 + Y], src[c + 3, 7 : 15 + Y], src[c + 3, 8 : 16 + Y]) * BY[c]
        return wide(FY[i, 0:Y], FY[i, 1 : 1 + Y], FY[i, 2 : 2 + Y], FY[i, 3 : 3 + Y])

    lax.fori_loop(0, X // PER, own_faces, 0)
    for c in range(3, X):
        face_x(c)
    inner_x(E)
    for q in range(X // PER):
        along_z(q)

    drained(CR.at[pl.ds(0, nz - 1)], cr_sem)
    own_col.wait()
    for dx, dy in plane[1:]:
        pltpu.make_async_remote_copy(
            CR, CA.at[dx * ny + dy], fs_sem, fr_sem,
            device_id=(zi * nx + xs[dx], ys[dy], blk), device_id_type=MESH,
        ).start()
    own_tile = pltpu.make_async_copy(CR, CA.at[0], self_sem.at[2])
    own_tile.start()
    send_rows(range(NB // 8, NB - 1))
    own = pltpu.make_async_copy(SB.at[me], RV.at[NB - 1], self_sem.at[1])
    own.start()

    finish(halo_b[2:])
    b_left = [ZR[1, r : r + 1] * left_on for r in (1, 2)]
    b_right = [ZR[1, r : r + 1] * right_on for r in (0, 1)]
    own_edge = [ZS[1, r : r + 1] for r in range(3, 7)]
    ZB[...] = FACE * jnp.concatenate(
        [
            own_edge[0] + own_edge[1],
            b_left[1] + own_edge[0],
            b_left[0] + b_left[1],
            own_edge[2] + own_edge[3],
            own_edge[3] + b_right[0],
            b_right[0] + b_right[1],
            jnp.zeros((2, cells), F32),
        ],
        axis=0,
    )
    def faces_y(q, _):
        for i in range(PER):
            c = q * PER + i
            BY[c] = (EB[c + 2, 6 : 14 + Y] + EB[c + 2, 7 : 15 + Y]) * FACE
        return 0

    lax.fori_loop(0, X // PER, faces_y, 0)

    def laplace(c):
        return TOT[c] + wide(FX[c], FX[c + 1], FX[c + 2], FX[c + 3])

    finish(halo_p[2:])
    fixes = fix_z(0)
    for q in range(X // PER):
        add_fix(fixes, q)
    seam_p[1]()
    seam_b[1]()

    drained(CA.at[pl.ds(0, G - 1)], fr_sem)
    own_tile.wait()
    keep = lax.broadcasted_iota(jnp.int32, (8, LANES), 1) == lax.broadcasted_iota(jnp.int32, (8, LANES), 0) + spot * CAP
    for k, (dz, dx, dy) in enumerate(slots):
        line = jnp.where(keep, jnp.broadcast_to(CA[dx * ny + dy, dz : dz + 1, :], (8, LANES)), 0.0)
        high = jnp.floor(line * (1.0 / 32.0))
        MC[k * 8 : k * 8 + 8, 0:LANES] = high
        MC[k * 8 : k * 8 + 8, LANES:] = line - 32.0 * high
    w_lane = jnp.where(lax.broadcasted_iota(jnp.int32, (8, 2 * LANES), 1) < LANES, 32.0, 1.0).astype(BF16)
    w_full = jnp.where(lax.broadcasted_iota(jnp.int32, (2 * LANES, LANES), 0) < LANES, 32.0, 1.0).astype(BF16)
    col_lane = dot_nt(w_lane, MC[...].astype(BF16))[0:1].astype(jnp.int32) - 1
    chunk = min(LANES, cells)

    def build_qt(m, _):
        ids = lax.broadcasted_iota(jnp.int32, (chunk, NB * CAP), 0) + m * chunk
        QT[pl.ds(m * chunk, chunk)] = onehot(ids == jnp.broadcast_to(col_lane, (chunk, NB * CAP)))
        return 0

    lax.fori_loop(0, cells // chunk, build_qt, 0)

    def build_q(dz, _):
        col_sub = dot(MC[pl.ds(dz * GS, GS)].astype(BF16), w_full) - 1.0
        for m in range(cells // chunk):
            ids = (lax.broadcasted_iota(jnp.int32, (GS, chunk), 1) + m * chunk).astype(F32)
            Q[pl.ds(dz * GS, GS), m * chunk : (m + 1) * chunk] = onehot(col_sub[:, :chunk] == ids)
        return 0

    lax.fori_loop(0, nz, build_q, 0)

    quads = X // PER
    ends = sorted({0, quads - 1})
    inside = [q for q in range(quads) if q not in ends]

    def first(q):
        for i in range(PER):
            c = q * PER + i
            E2[c + 3, 8 : 8 + Y] = 2.0 * E[c + 3, 8 : 8 + Y] - PREV[c] + KAP[c] * (laplace(c) + across_y(E, c, i))

    loads[5].wait()
    loads[6].wait()
    for q in inside:
        first(q)
    finish(halo_b[0:2])
    for c in (0, 1, 2, X, X + 1, X + 2):
        face_x(c)
    finish(halo_p[0:2])
    outer_x(E)
    for q in ends:
        first(q)
    seam_p[2]()
    seam_b[2]()

    for n in range(parts_n):
        last = n == parts_n - 1
        drained(RV.at[pl.ds(0, share - 1 if last else share)], ar_sem.at[n])
        if last:
            own.wait()
        ROWS[n * share * CAP : (n + 1) * share * CAP] = parts(
            RV[n * share : (n + 1) * share].reshape(share * CAP, LANES)
        )
    halo_m = shares(E2, 2, 3)

    def middle(q):
        pushed = joined(dot(QT[q * PER * Y : (q + 1) * PER * Y], ROWS[...])).reshape(PER, Y, LANES)
        for i in range(PER):
            c = q * PER + i
            force = (GAIN * KAP[c]) * pushed[i]
            mid = E2[c + 3, 8 : 8 + Y] + force
            E2[c + 3, 8 : 8 + Y] = mid
            SPLIT[c * Y : (c + 1) * Y] = parts(mid)
            PREV[c] = force - E[c + 3, 8 : 8 + Y]

    for q in ends:
        middle(q)
    start(halo_m[0:2])
    for q in inside:
        middle(q)
    start(halo_m[2:4])
    gather_edge(2)
    start(halo_m[4:5])
    inner_x(E2)
    for q in range(quads):
        along_z(q)
    finish(halo_m[4:5])
    fixes = fix_z(2)
    for q in range(quads):
        add_fix(fixes, q)
    finish(halo_m[2:4])

    def second(q, with_y):
        for i in range(PER):
            c = q * PER + i
            total = laplace(c)
            if with_y:
                total = total + across_y(E2, c, i)
            val = 2.0 * E2[c + 3, 8 : 8 + Y] + PREV[c] + KAP[c] * total
            out_ref[c] = val
            hi, lo = split2(val)
            NEXT[c * Y : (c + 1) * Y, 0:LANES] = hi
            NEXT[c * Y : (c + 1) * Y, LANES : 2 * LANES] = lo

    for q in inside:
        second(q, True)
    for q in ends:
        for i in range(PER):
            c = q * PER + i
            TOT[c] = TOT[c] + across_y(E2, c, i)

    pieces = max(parts_n, NB * CAP // LANES)
    count = NB // pieces

    def pick(n, quad):
        at = slice(quad * PER * Y, (quad + 1) * PER * Y)
        return joined(dot(Q[n * count * CAP : (n + 1) * count * CAP, at], NEXT[at])).reshape(count, 8, LANES)

    for n in range(pieces):
        total = None
        for q in inside:
            total = pick(n, q) if total is None else total + pick(n, q)
        if total is not None:
            PK[n * count : (n + 1) * count] = total
    finish(halo_m[0:2])
    outer_x(E2)
    for q in ends:
        second(q, False)

    for n in range(pieces):
        total = None
        for q in ends:
            total = pick(n, q) if total is None else total + pick(n, q)
        if inside:
            total = total + PK[n * count : (n + 1) * count]
        PK[n * count : (n + 1) * count] = total
        for k in range(n * count, (n + 1) * count):
            dz, dx, dy = slots[k]
            if k < NB - 1:
                pltpu.make_async_remote_copy(
                    PK.at[k], RET.at[k], bs_sem, br_sem.at[group_of(k)],
                    device_id=(zb[dz] * nx + xb[dx], yb[dy], blk), device_id_type=MESH,
                ).start()
    back = pltpu.make_async_copy(PK.at[NB - 1], RET.at[NB - 1], self_sem.at[3])
    back.start()

    drained(CR.at[pl.ds(0, nz - 1)], cs_sem)
    drained(CA.at[pl.ds(0, G - 1)], fs_sem)
    drained(SB.at[pl.ds(0, NB - 1)], as_sem)
    for n in range(parts_n):
        last = n == parts_n - 1
        drained(RET.at[pl.ds(0, share - 1 if last else share)], br_sem.at[n])
        if last:
            back.wait()
        at = slice(n * share * CAP, (n + 1) * share * CAP)
        got = joined(dot(PM[:, at], parts(RET[n * share : (n + 1) * share].reshape(share * CAP, LANES))))
        hp_ref[...] = got if n == 0 else hp_ref[...] + got
    drained(PK.at[pl.ds(0, NB - 1)], bs_sem)


def keep_out(field, rows, field_out, rows_out, sem):
    copies = [
        pltpu.make_async_copy(field, field_out, sem.at[0]),
        pltpu.make_async_copy(rows, rows_out, sem.at[1]),
    ]
    for copy in copies:
        copy.start()
    for copy in copies:
        copy.wait()


def solution(mesh):
    n_gx, n_gy = mesh.shape["gx"], mesh.shape["gy"]
    dims = torus(n_gx, n_gy)
    NB = n_gx * n_gy

    def local(pressure, pressure_prev, buoyancy, kappa, hull_accel, row_block, row_column):
        X, Y, Z = pressure.shape
        HR = hull_accel.shape[0]
        any_spec = pl.BlockSpec(memory_space=pltpu.HBM)
        vmem_spec = pl.BlockSpec(memory_space=pltpu.VMEM)
        dma = pltpu.SemaphoreType.DMA
        V = pltpu.VMEM
        results = pl.pallas_call(
            functools.partial(kernel, dims),
            out_shape=(
                jax.ShapeDtypeStruct((X, Y, Z), F32),
                jax.ShapeDtypeStruct((HR, Z), F32),
            ),
            in_specs=[any_spec] * 7,
            out_specs=[vmem_spec] * 2,
            scratch_shapes=[
                V((X + 6, Y + 16, Z), F32),
                V((X + 4, Y + 16, Z), F32),
                V((X + 6, Y + 16, Z), F32),
                V((3, 8, X * Y), F32),
                V((3, 8, X * Y), F32),
                V((X * Y, 2 * Z), BF16),
                V((2, 2 * Z, Z), BF16),
                V((8, X * Y), F32),
                V((X, Y, Z), F32),
                V((X, Y, Z), F32),
                V((HR, Z), F32),
                V((X + 3, Y, Z), F32),
                V((256 // Y, Y + 8, Z), F32),
                V((X, Y, Z), F32),
                V((X + 3, Y, Z), F32),
                V((X, Y + 8, Z), F32),
                V((X, Y, Z), F32),
                V((X * Y, 2 * Z), BF16),
                V((8, Z), F32),
                V((dims[0], Z), F32),
                V((dims[1] * dims[2], dims[0], Z), F32),
                V((NB * CAP, 2 * Z), F32),
                V((NB, CAP, Z), F32),
                V((NB, CAP, Z), F32),
                V((NB * CAP, 2 * Z), BF16),
                V((NB, CAP, Z), F32),
                V((NB, CAP, Z), F32),
                V((NB * CAP, X * Y), BF16),
                V((X * Y, NB * CAP), BF16),
                V((HR, NB * CAP), BF16),
                V((1, HR), jnp.int32),
                V((1, HR), jnp.int32),
                V((2, 3, Y // dims[1], Z), F32),
                V((2, 2, Y // dims[1], Z), F32),
                dma((7,)), dma((3, 5)), dma((3, 5)), dma((2, 2, dims[1])), dma((2, 2)), dma((2, 2)),
                dma, dma, dma, dma, dma, dma((4,)), dma, dma((4,)), dma((4,)),
            ],
            compiler_params=pltpu.CompilerParams(collective_id=0, has_side_effects=True, vmem_limit_bytes=36 * 1024 * 1024),
            name="hull_leapfrog",
        )(
            *(pltpu.with_memory_space_constraint(v, pltpu.HBM) for v in (
                pressure, pressure_prev, buoyancy, kappa, hull_accel,
                row_block.reshape(1, HR), row_column.reshape(1, HR),
            ))
        )
        return pl.pallas_call(
            keep_out,
            out_shape=(
                jax.ShapeDtypeStruct((X, Y, Z), F32),
                jax.ShapeDtypeStruct((HR, Z), F32),
            ),
            in_specs=[vmem_spec] * 2,
            out_specs=[any_spec] * 2,
            scratch_shapes=[dma((2,))],
            compiler_params=pltpu.CompilerParams(vmem_limit_bytes=2 * 1024 * 1024),
            name="write_out",
        )(*results)

    return jax.shard_map(
        local,
        mesh=mesh,
        in_specs=(
            P("gx", "gy", "blk"),
            P("gx", "gy", "blk"),
            P("gx", "gy", "blk"),
            P("gx", "gy", "blk"),
            P(("gx", "gy", "blk"), None),
            P(("gx", "gy", "blk"), None),
            P(("gx", "gy", "blk"), None),
        ),
        out_specs=(P("gx", "gy", "blk"), P(("gx", "gy", "blk"), None)),
        check_vma=False,
    )
```
